128 devices in a mesh: doc: 8 (over y, core), seq: 16 (over z, x).
Axes of the slice: x: 4, y: 4, z: 4, core: 2. Of those that a mesh axis runs over, the one named last changes fastest.
Arguments:
- hidden: bfloat16 [8, 8192, 768], P('doc', 'seq'), may hold values from -6 to 6
- token_ids: int32 [8, 8192], P('doc', 'seq'), may hold values from 0 to 50264, as said below
- w_query: bfloat16 [768, 768], replicated, may hold values from -0.625 to 0.625
- w_keyval: bfloat16 [768, 1536], replicated, may hold values from -0.21875 to 0.21875
- w_out: bfloat16 [768, 768], replicated, may hold values from -0.21875 to 0.21875
- x_query: bfloat16 [768, 768], replicated, may hold values from -0.21875 to 0.21875
- x_out: bfloat16 [768, 768], replicated, may hold values from -0.21875 to 0.21875
- shortlist: int32 [8, 320], P('doc'), may hold values from 0 to 36863, as said below
- code_row: int32 [36864], replicated, may hold values from 0 to 36863, as said below
- code_cache: bfloat16 [36864, 2, 8, 768], P(('doc', 'seq')), may hold values from -10 to 10
Outputs:
- refined: bfloat16 [8, 8192, 768], P('doc', 'seq')
- cand_score: float32 [8, 320], P('doc')
The draws below stay inside these ranges and needn't reach their ends.
Inputs may be any that keep to these rules, and one draw needn't show every extreme that they name: `token_ids`: each summary is a run of ids of 1 or more followed by padding ids 0 up to its end; every summary has 2048 or more nonzero ids and one summary has no padding. `shortlist`: the candidates of one summary are distinct codes; at most 4 of them have code_row in one block of 288 rows (row // 288 equal), and for every summary some block holds exactly 4 of them. `code_row`: each row of the cache holds exactly one code.
All inputs are finite; a program needn't handle non-finite values.
Results may differ from the reference program's by a relative error of at most 0.018.
Values may be sent and summed in bfloat16 or wider, within the bound.
No kernel may reach another device: no remote copies, remote signals or barrier semaphores. Data moves between devices by JAX's collectives and lax.ppermute only.
A program may use at most 192 MiB of HBM per device.

```python
import math
import jax
import jax.numpy as jnp
from jax import lax

D = 768
HEADS = 12
HALF_WIN = 256
TOK_DEV = 512
SEQ_LEN = 8192
DOCS = 8
C = 320
DESC = 8
CODE_DEV = 288
CODES = 36864
CAP = 4
VOCAB = 50265
DEVICES = 128


def code_layout(key):
    return jax.random.permutation(jax.random.fold_in(key, 701), CODES).astype(jnp.int32)


def draw_code_row(key, part):
    return code_layout(key)


def draw_shortlist(key, part):
    layout = code_layout(key)
    code_of_row = jnp.zeros((CODES,), jnp.int32).at[layout].set(jnp.arange(CODES, dtype=jnp.int32))
    grid_size = DEVICES * CAP
    owner_ids = jnp.arange(DEVICES, dtype=jnp.int32)
    popular = jax.random.randint(jax.random.fold_in(key, 711), (DEVICES,), 0, 4)
    noise = jax.random.randint(jax.random.fold_in(key, 712), (DOCS, DEVICES, CAP), 0, 65536)
    full_owner = jax.random.randint(jax.random.fold_in(key, 713), (DOCS,), 0, DEVICES)
    boost = popular[None, :] + 8 * (owner_ids[None, :] == full_owner[:, None]).astype(jnp.int32)
    position = jnp.arange(grid_size, dtype=jnp.int32).reshape(DEVICES, CAP)
    scores = (boost[:, :, None] * 65536 + noise) * grid_size + position[None]
    unused, picked = lax.top_k(scores.reshape(DOCS, grid_size), C)
    picked = picked.astype(jnp.int32)
    owner_dev = picked // CAP
    slot_rank = picked % CAP
    offsets = jax.random.randint(jax.random.fold_in(key, 714), (DOCS, DEVICES), 0, CODE_DEV)
    local_row = (jnp.take_along_axis(offsets, owner_dev, axis=1) + slot_rank) % CODE_DEV
    return code_of_row[owner_dev * CODE_DEV + local_row]


def draw_token_ids(key, part):
    lengths = jax.random.randint(jax.random.fold_in(key, 721), (DOCS,), SEQ_LEN // 4, SEQ_LEN + 1)
    full_doc = jax.random.randint(jax.random.fold_in(key, 722), (), 0, DOCS)
    doc_ids = jnp.arange(DOCS)
    lengths = jnp.where(doc_ids == full_doc, SEQ_LEN, lengths)
    words = jax.random.randint(jax.random.fold_in(key, 723), (DOCS, SEQ_LEN), 1, VOCAB)
    positions = jnp.arange(SEQ_LEN)[None, :]
    top_spot = (doc_ids[:, None] == full_doc) & (positions == 0)
    words = jnp.where(top_spot, VOCAB - 1, words)
    return jnp.where(positions < lengths[:, None], words, 0).astype(jnp.int32)


def steps_of(key, extent, pieces, least, high):
    def one(dim, blocks):
        heights = jax.random.uniform(jax.random.fold_in(jax.random.fold_in(key, 6), dim), (blocks,), jnp.float32, least / len(pieces), high / len(pieces))
        return jnp.repeat(jnp.exp(heights), extent[dim] // blocks).reshape((-1,) + (1,) * (len(extent) - dim - 1))

    loudness = one(*pieces[0])
    for cut in pieces[1:]:
        loudness = loudness * one(*cut)
    return loudness


def normal_values(rng, shape, scale, most, shards=(), held_as=jnp.bfloat16):
    gain = steps_of(rng, shape, shards, -0.22, 0.18) if shards else 1.0
    entries = jax.random.normal(rng, shape, jnp.float32) * scale * gain
    return jnp.minimum(jnp.maximum(entries, -most), most).astype(held_as)


def setup_inputs(seed: int = 0) -> dict:
    seeds = jax.random.split(jax.random.key(seed), 11)
    hidden = normal_values(seeds[0], (DOCS, SEQ_LEN, D), 1.0, 6.0, ((0, 8), (1, 16)))
    token_ids = draw_token_ids(jax.random.fold_in(seeds[10], 71), 0)
    w_query = normal_values(seeds[2], (D, D), (D // 8) ** -0.5, 0.625)
    w_keyval = normal_values(seeds[3], (D, 2 * D), D ** -0.5, 0.21875)
    w_out = normal_values(seeds[4], (D, D), D ** -0.5, 0.21875)
    x_query = normal_values(seeds[5], (D, D), D ** -0.5, 0.21875)
    x_out = normal_values(seeds[6], (D, D), D ** -0.5, 0.21875)
    shortlist = draw_shortlist(jax.random.fold_in(seeds[10], 71), 0)
    code_row = draw_code_row(jax.random.fold_in(seeds[10], 71), 0)
    code_cache = normal_values(seeds[9], (CODES, 2, DESC, D), 2.0, 10.0, ((0, 128),))
    return {"hidden": hidden, "token_ids": token_ids, "w_query": w_query, "w_keyval": w_keyval, "w_out": w_out, "x_query": x_query, "x_out": x_out, "shortlist": shortlist, "code_row": code_row, "code_cache": code_cache}


def layer_norm(values):
    centered = values - lax.optimization_barrier(jnp.mean(values, axis=-1, keepdims=True))
    spread = lax.optimization_barrier(jnp.mean(centered * centered, axis=-1, keepdims=True))
    return centered * lax.rsqrt(spread + 1e-05)

def attend(query, key_rows, value_rows, allowed, weigh):
    query_count = query.shape[0]
    key_count = key_rows.shape[0]
    head_size = query.shape[1] // HEADS
    score_scale = 1.0 / math.sqrt(head_size)
    query_heads = lax.optimization_barrier(query).astype(jnp.float32).reshape(query_count, HEADS, head_size)
    key_heads = lax.optimization_barrier(key_rows).astype(jnp.float32).reshape(key_count, HEADS, head_size)
    value_heads = lax.optimization_barrier(value_rows).astype(jnp.float32).reshape(key_count, HEADS, head_size)
    scores = jnp.einsum('qhd,khd->hqk', query_heads, key_heads) * score_scale
    expd = jnp.exp(scores)
    if allowed is not None:
        expd = jnp.where(allowed[None], expd, 0.0)
    weights = expd / lax.optimization_barrier(jnp.sum(expd, axis=-1, keepdims=True))
    probs = lax.optimization_barrier(weights.astype(jnp.bfloat16)).astype(jnp.float32)
    context = jnp.einsum('hqk,khd->qhd', probs, value_heads).reshape(query_count, HEADS * head_size)
    context = context.astype(jnp.bfloat16)
    if weigh is None:
        return (context, None)
    key_mass = lax.optimization_barrier(jnp.sum(jnp.where(weigh[None, :, None], weights, 0.0), axis=(0, 1)))
    return (context, key_mass)

def reference(hidden, token_ids, w_query, w_keyval, w_out, x_query, x_out, shortlist, code_row, code_cache):
    block_count = SEQ_LEN // TOK_DEV

    def one_document(operands):
        doc_hidden, doc_tokens, doc_shortlist = operands
        length = jnp.sum((doc_tokens != 0).astype(jnp.int32))
        normed = layer_norm(doc_hidden.astype(jnp.float32)).astype(jnp.bfloat16)
        query = jnp.dot(normed, w_query, preferred_element_type=jnp.float32).astype(jnp.bfloat16)
        keyval = jnp.dot(normed, w_keyval, preferred_element_type=jnp.float32).astype(jnp.bfloat16)
        padded = jnp.pad(keyval, ((HALF_WIN, HALF_WIN), (0, 0)))

        def window_block(block_index):
            first_row = (block_index * TOK_DEV).astype(jnp.int32)
            block_query = lax.dynamic_slice_in_dim(query, first_row, TOK_DEV, 0)
            block_keys = lax.dynamic_slice_in_dim(padded, first_row, TOK_DEV + 2 * HALF_WIN, 0)
            query_pos = first_row + jnp.arange(TOK_DEV, dtype=jnp.int32)
            key_pos = first_row - HALF_WIN + jnp.arange(TOK_DEV + 2 * HALF_WIN, dtype=jnp.int32)
            near = jnp.abs(query_pos[:, None] - key_pos[None, :]) <= HALF_WIN
            usable = ((key_pos >= 0) & (key_pos < length))[None, :] | (query_pos[:, None] == key_pos[None, :])
            context, unused = attend(block_query, block_keys[:, :D], block_keys[:, D:], near & usable, None)
            return context
        contexts = lax.map(window_block, jnp.arange(block_count, dtype=jnp.int32))
        context = contexts.reshape(SEQ_LEN, D)
        middle = (doc_hidden.astype(jnp.float32) + jnp.dot(context, w_out, preferred_element_type=jnp.float32)).astype(jnp.bfloat16)
        middle_wide = lax.optimization_barrier(middle).astype(jnp.float32)
        cross_normed = layer_norm(middle_wide).astype(jnp.bfloat16)
        cross_query = jnp.dot(cross_normed, x_query, preferred_element_type=jnp.float32).astype(jnp.bfloat16)
        cache_rows = code_cache[code_row[doc_shortlist]]
        cand_keys = cache_rows[:, 0].reshape(C * DESC, D)
        cand_values = cache_rows[:, 1].reshape(C * DESC, D)

        def cross_block(block_index):
            first_row = (block_index * TOK_DEV).astype(jnp.int32)
            block_query = lax.dynamic_slice_in_dim(cross_query, first_row, TOK_DEV, 0)
            query_pos = first_row + jnp.arange(TOK_DEV, dtype=jnp.int32)
            return attend(block_query, cand_keys, cand_values, None, query_pos < length)
        cross_contexts, masses = lax.map(cross_block, jnp.arange(block_count, dtype=jnp.int32))
        cross_context = cross_contexts.reshape(SEQ_LEN, D)
        refined = (middle_wide + jnp.dot(cross_context, x_out, preferred_element_type=jnp.float32)).astype(jnp.bfloat16)
        cand_mass = lax.optimization_barrier(jnp.sum(lax.optimization_barrier(jnp.sum(masses, axis=0)).reshape(C, DESC), axis=1))
        cand_score = C * cand_mass / (HEADS * length.astype(jnp.float32))
        return (refined, cand_score)
    return lax.map(one_document, (hidden, token_ids, shortlist))
```

```python
import functools
import math

import jax
import jax.numpy as jnp
from jax import lax
from jax.experimental import pallas as pl
from jax.experimental.pallas import tpu as pltpu
from jax.sharding import PartitionSpec as P

HEADS = 12
HALF_WIN = 256
DESC = 8
GRID = 4
LANES = 128
HALF = 64
SCALE = math.log2(math.e) / 8.0
BF = jnp.bfloat16
F32 = jnp.float32
I32 = jnp.int32


def iota(shape, dim):
    return lax.broadcasted_iota(I32, shape, dim)


def dot(a, b):
    return jnp.dot(a, b, preferred_element_type=F32)


def dot_t(a, b):
    return lax.dot_general(a, b, (((1,), (1,)), ((), ())), preferred_element_type=F32)


def params(mib):
    return pltpu.CompilerParams(vmem_limit_bytes=mib << 20)


def vmem():
    return pl.BlockSpec(memory_space=pltpu.VMEM)


def smem():
    return pl.BlockSpec(memory_space=pltpu.SMEM)


def cost(flops, exps, bytes_):
    return pl.CostEstimate(flops=flops, transcendentals=exps, bytes_accessed=bytes_)


def split_table(table):
    high = table >> 8
    return jnp.concatenate([high, table - (high << 8)], axis=1).astype(F32).astype(BF)


def look_up(code, table):
    n = code.shape[1]
    picks = (iota((table.shape[0], n), 0) == (code >> 7)).astype(F32).astype(BF)
    found = lax.dot_general(table, picks, (((0,), (0,)), ((), ())), preferred_element_type=F32)
    here = iota((LANES, n), 0) == (code & 127)
    value = jnp.where(here, found[:LANES] * 256.0 + found[LANES:], 0.0)
    return jnp.sum(value, axis=0, keepdims=True)


def ranks(row, count, code_dev, devices, upper):
    n = row.shape[1]
    owner = jnp.floor((row + 0.5) * (1.0 / code_dev))
    local = (row - owner * code_dev).astype(I32)
    owner = jnp.where(iota((1, n), 1) < count, owner.astype(I32), 2 * devices)
    sub = iota((devices, n), 0)
    mine = owner == sub
    starts = jnp.sum((owner < sub).astype(F32), axis=1, keepdims=True)
    before = dot(mine.astype(F32).astype(BF), upper)
    rank = jnp.sum(jnp.where(mine, starts + before, 0.0), axis=0, keepdims=True)
    return owner, local, rank.astype(I32), mine


def upper_ones(n):
    return (iota((n, n), 0) < iota((n, n), 1)).astype(F32).astype(BF)


def own_kernel(count, code_dev, devices, where_ref, code_ref, table_ref, slot_ref, pos_ref):
    n = code_ref.shape[1]
    row = look_up(code_ref[...], split_table(table_ref[...]))
    owner, local, rank, mine = ranks(row, count, code_dev, devices, upper_ones(n))
    part = rank & (GRID - 1)
    spot = rank >> 2
    live = jnp.where(part == where_ref[1], (spot + 1).astype(F32), 0.0)
    place = jnp.sum(jnp.where(mine, live, 0.0), axis=1, keepdims=True)
    width = devices * DESC
    spread = jnp.where(iota((devices, width), 0) == iota((devices, width), 1) // DESC, place, 0.0)
    spread = jnp.sum(spread, axis=0, keepdims=True).astype(I32)
    inner = iota((1, width), 1) & (DESC - 1)
    slot_ref[...] = jnp.where(spread > 0, (spread - 1) * DESC + inner, -1)
    pos_ref[...] = part * (count // GRID) + spot


def route_kernel(
    count, code_dev, devices, where_ref, codes_ref, table_ref, cache_ref, send_ref, rows, picks, picked, sems, sem
):
    docs, _, n = codes_ref.shape
    table = split_table(table_ref[...])
    upper = upper_ones(n)
    lane = iota((1, LANES), 1)
    for d in range(docs):
        row = look_up(codes_ref[d], table)
        owner, local, rank, _ = ranks(row, count, code_dev, devices, upper)
        wanted = jnp.where(owner == where_ref[0], local + 1, 0).astype(F32)
        part = rank & (GRID - 1)
        line = jnp.zeros((1, LANES), F32)
        for z in range(GRID):
            one = jnp.sum(jnp.where(part == z, wanted, 0.0), axis=1, keepdims=True)
            line = line + jnp.where(lane == z, one, 0.0)
        picks[pl.ds(d, 1), :] = jnp.maximum(line.astype(I32) - 1, 0)
    to_scalars = pltpu.make_async_copy(picks, picked, sem)
    to_scalars.start()
    to_scalars.wait()
    copies = []
    for d in range(docs):
        for z in range(GRID):
            k = d * GRID + z
            copies.append(pltpu.make_async_copy(cache_ref.at[picked[d, z]], rows.at[k], sems.at[k]))
            copies[-1].start()
    for copy in copies:
        copy.wait()
    low = iota((docs * GRID, DESC, LANES), 2) < HALF
    for p in range(HEADS // 2):
        cols = pl.ds(p * LANES, LANES)
        keys = rows[:, 0, :, cols].astype(F32)
        values = rows[:, 1, :, cols].astype(F32)
        keys_turned = pltpu.roll(keys, HALF, 2)
        values_turned = pltpu.roll(values, HALF, 2)
        for s in range(2):
            head = 2 * p + s
            group, inner = head // 3, head % 3
            key_low = keys if s == 0 else keys_turned
            key_high = keys_turned if s == 0 else keys
            value_low = values if s == 0 else values_turned
            value_high = values_turned if s == 0 else values
            if inner == 1:
                tile = jnp.where(low, value_low, key_high)
            else:
                tile = jnp.where(low, key_low, value_high)
            send_ref[:, group, :, pl.ds(inner * LANES, LANES)] = tile.astype(BF)


def compact_kernel(slot_ref, got_ref, *out_refs):
    rows = out_refs[0].shape[0]
    pick = (iota((rows, got_ref.shape[0]), 0) == slot_ref[...]).astype(F32).astype(BF)
    packed = dot(pick, got_ref[...]).astype(BF)
    for k, out in enumerate(out_refs):
        out[...] = packed[:, k * LANES : (k + 1) * LANES]


def layer_norm(values):
    centered = values - jnp.mean(values, axis=-1, keepdims=True)
    spread = jnp.mean(centered * centered, axis=-1, keepdims=True)
    return centered * lax.rsqrt(spread + 1e-05)


def window_kernel(
    low_ref, hidden_ref, high_ref, flag_ref, wq_ref, wkv_ref, wo_ref, xq_ref, middle_ref, query_ref, keys, values, queries, context, bias
):
    tok, width = hidden_ref.shape
    win = HALF_WIN
    span = 3 * win
    pairs = width // LANES
    wkv = wkv_ref[...]
    for ref, start, rows in ((low_ref, 0, win), (hidden_ref, win, tok), (high_ref, win + tok, win)):
        for r in range(0, rows, win):
            normed = layer_norm(ref[r : r + win, :].astype(F32)).astype(BF)
            keyval = dot(normed, wkv).astype(BF)
            at = start + r
            keys[at : at + win, :] = keyval[:, :width]
            for p in range(pairs):
                part = keyval[:, width + p * LANES : width + (p + 1) * LANES].astype(F32) * 2.0**-8
                values[at : at + win, 2 * p * LANES : (2 * p + 1) * LANES] = part.astype(BF)
                values[at : at + win, (2 * p + 1) * LANES : (2 * p + 2) * LANES] = jnp.ones((win, LANES), BF)
            if ref is hidden_ref:
                queries[r : r + win, :] = (dot(normed, wq_ref[...]) * SCALE).astype(BF)
    flags = jnp.concatenate(
        [low_ref[win : win + 1, :win].astype(F32), flag_ref[...], high_ref[win : win + 1, :win].astype(F32)], axis=1
    )
    gap = iota((win, span), 1) - iota((win, span), 0)
    near = (gap >= 0) & (gap <= 2 * win)
    for b in range(tok // win):
        usable = (flags[:, b * win : b * win + span] > 0.0) | (gap == win)
        bias[b] = jnp.where(near & usable, 0.0, -1e30)
    low = iota((win, LANES), 1) < HALF
    for b in range(tok // win):
        for p in range(pairs):
            cols = slice(p * LANES, (p + 1) * LANES)
            query = queries[b * win : (b + 1) * win, cols]
            key = keys[b * win : b * win + span, cols]
            value = values[b * win : b * win + span, 2 * p * LANES : (2 * p + 2) * LANES]
            both = []
            for s in range(2):
                one = jnp.where(low if s == 0 else ~low, query, jnp.zeros_like(query))
                expd = jnp.exp2(dot_t(one, key) + bias[b]).astype(BF)
                out = dot(expd, value)
                both.append(out[:, :LANES] / out[:, LANES:] * 256.0)
            context[b * win : (b + 1) * win, cols] = jnp.where(low, both[0], both[1]).astype(BF)
    valid = jnp.transpose(jnp.broadcast_to(flag_ref[...], (LANES, tok)))
    for b in range(tok // win):
        rows = slice(b * win, (b + 1) * win)
        mixed = hidden_ref[rows, :].astype(F32) + dot(context[rows, :], wo_ref[...])
        mixed = mixed.astype(BF)
        middle_ref[rows, :] = mixed
        cross = dot(layer_norm(mixed.astype(F32)).astype(BF), xq_ref[...]) * SCALE
        tiles = [cross[:, p * LANES : (p + 1) * LANES] for p in range(pairs)]
        turned = [pltpu.roll(t, HALF, 1) for t in tiles]

        def placed(head, upper):
            return (turned if (head % 2 == 1) != upper else tiles)[head // 2]

        for g in range(GRID):
            first = jnp.where(low, placed(3 * g, False), placed(3 * g + 1, True))
            second = jnp.where(low, placed(3 * g + 2, False), valid[rows, :])
            query_ref[g, rows, :LANES] = first.astype(BF)
            query_ref[g, rows, LANES:] = second.astype(BF)


def cross_kernel(inner, count, where_ref, pos_ref, query_ref, *refs):
    kv_refs, refs = refs[:GRID], refs[GRID:]
    before = refs[0] if inner else None
    refs = refs[1:] if inner else refs
    earlier = refs[0] if inner == 1 else None
    refs = refs[1:] if inner == 1 else refs
    out_ref, mass_ref, values, expds, total = refs
    keys_here = kv_refs[0].shape[0]
    step = 256
    groups, tok, _ = query_ref.shape
    value_low = inner == 1
    lane = iota((keys_here, LANES), 1)
    of_value = (lane < HALF) if value_low else (lane >= HALF)
    for c in range(GRID):
        scaled = kv_refs[c][...].astype(F32) * 2.0**-4
        values[c] = jnp.where(of_value, scaled, 1.0).astype(BF)
    if before is None:
        total[...] = jnp.zeros_like(total)
    else:
        total[...] = before[...]
    tile = LANES if inner == 2 else 0
    small = iota((step, LANES), 1)
    of_query = (small >= HALF) if value_low else (small < HALF)
    out_here = (small < HALF) if value_low else (small >= HALF)
    sum_lane = LANES - 1 if value_low else 0
    per = tok // step

    def body(i, carry):
        g = i // per
        rows = pl.ds(pl.multiple_of((i % per) * step, step), step)
        query = query_ref[g, rows, tile : tile + LANES]
        valid = query_ref[g, rows, 2 * LANES - 1 :].astype(F32)
        query = jnp.where(of_query, query, jnp.zeros_like(query))
        acc = jnp.zeros((step, LANES), F32)
        for c in range(GRID):
            expd = jnp.exp2(dot_t(query, kv_refs[c][...])).astype(BF)
            expds[c] = expd
            acc = acc + dot(expd, values[c])
        inverse = 1.0 / acc[:, sum_lane : sum_lane + 1]
        out = (acc * inverse) * 16.0
        rest = earlier[g, rows, :].astype(F32) if inner == 1 else jnp.zeros_like(out)
        out_ref[g, rows, :] = jnp.where(out_here, out, rest).astype(BF)
        share = inverse * valid
        for c in range(GRID):
            mass = jnp.sum(expds[c].astype(F32) * share, axis=0, keepdims=True)
            total[c : c + 1, :] = total[c : c + 1, :] + mass
        return carry

    lax.fori_loop(0, groups * per, body, 0)
    if inner < 2:
        mass_ref[...] = total[...]
        return
    score = jnp.zeros((8, pos_ref.shape[1]), F32)
    line = iota((8, keys_here), 0)
    for c in range(GRID):
        mass = jnp.broadcast_to(total[c : c + 1, :], (8, keys_here))
        first = mass.astype(BF).astype(F32)
        second = (mass - first).astype(BF).astype(F32)
        third = mass - first - second
        parts = jnp.where(line == 0, first, jnp.where(line == 1, second, jnp.where(line == 2, third, 0.0)))
        origin = (where_ref[1] + GRID - c) & (GRID - 1)
        at = iota((keys_here, pos_ref.shape[1]), 0) // DESC + origin * (count // GRID)
        score = score + dot(parts.astype(BF), (at == pos_ref[...]).astype(F32).astype(BF))
    mass_ref[...] = jnp.sum(score, axis=0, keepdims=True)


def final_kernel(middle_ref, first_ref, second_ref, weight_ref, out_ref):
    groups = first_ref.shape[0]
    size = 3 * HALF
    acc = middle_ref[...].astype(F32)
    for g in range(groups):
        at = g * size
        crossed = jnp.concatenate([weight_ref[at + HALF : at + 2 * HALF, :], weight_ref[at : at + HALF, :]], axis=0)
        acc = acc + dot(first_ref[g], crossed)
        acc = acc + dot(second_ref[g], weight_ref[at + HALF : at + size, :])
    out_ref[...] = acc.astype(BF)


def local(hidden, token_ids, w_query, w_keyval, w_out, x_query, x_out, shortlist, code_row, code_cache):
    doc_hidden = hidden[0]
    tok, width = doc_hidden.shape
    seq_count = lax.axis_size("seq")
    docs = lax.axis_size("doc")
    devices = docs * seq_count
    seq_index = lax.axis_index("seq")
    own = lax.axis_index("doc") * seq_count + seq_index
    where = jnp.stack([own, seq_index // GRID]).astype(I32)
    count = shortlist.shape[1]
    padded = -(-count // LANES) * LANES
    code_dev = code_cache.shape[0]
    held = count // GRID * DESC
    table = code_row.reshape(-1, LANES)

    codes = jnp.pad(shortlist, ((0, 0), (0, padded - count)), constant_values=-1)
    all_codes = lax.all_gather(codes, "doc", axis=0, tiled=False)

    flag = (token_ids != 0).astype(BF)
    rows8 = jnp.zeros((8, width), BF)
    forward = [(i, i + 1) for i in range(seq_count - 1)]
    backward = [(t, s) for s, t in forward]
    tail = jnp.concatenate([doc_hidden[tok - HALF_WIN :], rows8.at[:1, :HALF_WIN].set(flag[:, tok - HALF_WIN :])], axis=0)
    head = jnp.concatenate([doc_hidden[:HALF_WIN], rows8.at[:1, :HALF_WIN].set(flag[:, :HALF_WIN])], axis=0)
    low = lax.ppermute(tail, "seq", forward)
    high = lax.ppermute(head, "seq", backward)

    send = pl.pallas_call(
        functools.partial(route_kernel, count, code_dev, devices),
        name="route",
        out_shape=jax.ShapeDtypeStruct((docs * GRID, GRID, DESC, 3 * LANES), BF),
        in_specs=[smem(), vmem(), vmem(), pl.BlockSpec(memory_space=pl.ANY)],
        out_specs=vmem(),
        scratch_shapes=[
            pltpu.VMEM((docs * GRID, 2, DESC, width), BF),
            pltpu.VMEM((docs, LANES), I32),
            pltpu.SMEM((docs, LANES), I32),
            pltpu.SemaphoreType.DMA((docs * GRID,)),
            pltpu.SemaphoreType.DMA,
        ],
        compiler_params=params(24),
        cost_estimate=cost(10**9, 0, 2 * 10**6),
    )(where, all_codes, table, code_cache)
    got = lax.all_to_all(
        send.reshape(devices, DESC, 3 * LANES), ("doc", "seq"), split_axis=0, concat_axis=0, tiled=True
    )

    slots, pos = pl.pallas_call(
        functools.partial(own_kernel, count, code_dev, devices),
        name="own",
        out_shape=(
            jax.ShapeDtypeStruct((1, devices * DESC), I32),
            jax.ShapeDtypeStruct((1, padded), I32),
        ),
        in_specs=[smem(), vmem(), vmem()],
        out_specs=(vmem(), vmem()),
        compiler_params=params(16),
        cost_estimate=cost(10**8, 0, 2 * 10**5),
    )(where, codes, table)

    middle, queries = pl.pallas_call(
        window_kernel,
        name="window",
        out_shape=(
            jax.ShapeDtypeStruct((tok, width), BF),
            jax.ShapeDtypeStruct((GRID, tok, 2 * LANES), BF),
        ),
        in_specs=[vmem()] * 8,
        out_specs=(vmem(), vmem()),
        scratch_shapes=[
            pltpu.VMEM((tok + 2 * HALF_WIN, width), BF),
            pltpu.VMEM((tok + 2 * HALF_WIN, 2 * width), BF),
            pltpu.VMEM((tok, width), BF),
            pltpu.VMEM((tok, width), BF),
            pltpu.VMEM((tok // HALF_WIN, HALF_WIN, 3 * HALF_WIN), F32),
        ],
        compiler_params=params(48),
        cost_estimate=cost(12 * 10**9, 5 * 10**6, 10**7),
    )(low, doc_hidden, high, flag.astype(F32), w_query, w_keyval, w_out, x_query)

    lines = [[GRID * z + x for x in range(GRID)] for z in range(GRID)]

    def across(block):
        return lax.all_to_all(
            block, "seq", split_axis=0, concat_axis=0, axis_index_groups=lines, tiled=True
        )

    queries = across(queries)

    blocks = pl.pallas_call(
        compact_kernel,
        name="compact",
        out_shape=(jax.ShapeDtypeStruct((held, LANES), BF),) * 3,
        in_specs=[vmem()] * 2,
        out_specs=(vmem(),) * 3,
        compiler_params=params(24),
        cost_estimate=cost(10**9, 0, 2 * 10**6),
    )(slots, got.reshape(devices * DESC, 3 * LANES))

    gathered = []
    for block in blocks:
        parts = [block]
        for shift in range(1, GRID):
            pairs = [(i, (i + GRID * shift) % seq_count) for i in range(seq_count)]
            parts.append(lax.ppermute(block, "seq", pairs))
        gathered.append(parts)

    mass, first, second = (), None, None
    for inner in range(3):
        last = inner == 2
        extra = ((mass,) if inner else ()) + ((first,) if inner == 1 else ())
        out, mass = pl.pallas_call(
            functools.partial(cross_kernel, inner, count),
            name="cross",
            out_shape=(
                jax.ShapeDtypeStruct((GRID, tok, LANES), BF),
                jax.ShapeDtypeStruct((1, padded) if last else (8, held), F32),
            ),
            in_specs=[smem()] + [vmem()] * (2 + GRID + len(extra)),
            out_specs=(vmem(), vmem()),
            scratch_shapes=[
                pltpu.VMEM((GRID, held, LANES), BF),
                pltpu.VMEM((GRID, 256, held), BF),
                pltpu.VMEM((8, held), F32),
            ],
            compiler_params=params(32),
            cost_estimate=cost(6 * 10**9, 5 * 10**6, 4 * 10**6),
        )(where, pos, queries, *gathered[inner], *extra)
        if inner == 1:
            first = across(out)
        elif inner == 0:
            first = out
        else:
            second = across(out)

    tokens_here = jnp.sum((token_ids != 0).astype(F32), axis=1, keepdims=True)
    partial = jnp.where(jnp.arange(padded)[None, :] == count, tokens_here, mass)
    sums = jnp.sum(lax.all_gather(partial, "seq", axis=0, tiled=True), axis=0, keepdims=True)
    cand_score = count * sums[:, :count] / (HEADS * sums[:, count : count + 1])

    refined = pl.pallas_call(
        final_kernel,
        name="final",
        out_shape=jax.ShapeDtypeStruct((tok, width), BF),
        in_specs=[vmem()] * 4,
        out_specs=vmem(),
        compiler_params=params(16),
        cost_estimate=cost(10**9, 0, 4 * 10**6),
    )(middle, first, second, x_out)
    return (refined[None], cand_score)


def solution(mesh):
    return jax.shard_map(
        local,
        mesh=mesh,
        in_specs=(
            P("doc", "seq", None),
            P("doc", "seq"),
            P(),
            P(),
            P(),
            P(),
            P(),
            P("doc", None),
            P(),
            P(("doc", "seq"), None, None, None),
        ),
        out_specs=(P("doc", "seq", None), P("doc", None)),
        check_vma=False,
    )
```

```python
import functools
import math

import jax
import jax.numpy as jnp
from jax import lax
from jax.experimental import pallas as pl
from jax.experimental.pallas import tpu as pltpu
from jax.sharding import PartitionSpec as P

HEADS = 12
HALF_WIN = 256
DESC = 8
GRID = 4
LANES = 128
HALF = 64
SCALE = math.log2(math.e) / 8.0
BF = jnp.bfloat16
F32 = jnp.float32
I32 = jnp.int32


def iota(shape, dim):
    return lax.broadcasted_iota(I32, shape, dim)


def dot(a, b):
    return jnp.dot(a, b, preferred_element_type=F32)


def dot_t(a, b):
    return lax.dot_general(a, b, (((1,), (1,)), ((), ())), preferred_element_type=F32)


def params(mib):
    return pltpu.CompilerParams(vmem_limit_bytes=mib << 20)


def vmem():
    return pl.BlockSpec(memory_space=pltpu.VMEM)


def smem():
    return pl.BlockSpec(memory_space=pltpu.SMEM)


def cost(flops, exps, bytes_):
    return pl.CostEstimate(flops=flops, transcendentals=exps, bytes_accessed=bytes_)


def split_table(table):
    high = table >> 8
    return jnp.concatenate([high, table - (high << 8)], axis=1).astype(F32).astype(BF)


def look_up(code, table):
    n = code.shape[1]
    picks = (iota((table.shape[0], n), 0) == (code >> 7)).astype(F32).astype(BF)
    found = lax.dot_general(table, picks, (((0,), (0,)), ((), ())), preferred_element_type=F32)
    here = iota((LANES, n), 0) == (code & 127)
    value = jnp.where(here, found[:LANES] * 256.0 + found[LANES:], 0.0)
    return jnp.sum(value, axis=0, keepdims=True)


def ranks(row, count, code_dev, devices, upper):
    n = row.shape[1]
    owner = jnp.floor((row + 0.5) * (1.0 / code_dev))
    local = (row - owner * code_dev).astype(I32)
    owner = jnp.where(iota((1, n), 1) < count, owner.astype(I32), 2 * devices)
    sub = iota((devices, n), 0)
    mine = owner == sub
    starts = jnp.sum((owner < sub).astype(F32), axis=1, keepdims=True)
    before = dot(mine.astype(F32).astype(BF), upper)
    rank = jnp.sum(jnp.where(mine, starts + before, 0.0), axis=0, keepdims=True)
    return owner, local, rank.astype(I32)


def upper_ones(n):
    return (iota((n, n), 0) < iota((n, n), 1)).astype(F32).astype(BF)


def route_kernel(
    count, code_dev, devices, where_ref, codes_ref, table_ref, cache_ref, send_ref, slot_ref, pos_ref, table, rows, line, picks, picked, sems, sem
):
    docs = codes_ref.shape[0]
    n = line.shape[1]
    fetch = pltpu.make_async_copy(table_ref, table, sem.at[0])
    fetch.start()
    upper = upper_ones(n)
    lane = iota((1, LANES), 1)
    line[...] = jnp.full(line.shape, -1, I32)
    for d in range(docs):
        line[d : d + 1, :count] = codes_ref[d]
    fetch.wait()
    planes = split_table(table[...])
    doc = where_ref[2]
    owner_here = jnp.zeros((1, n), I32)
    rank_here = jnp.zeros((1, n), I32)
    for d in range(docs):
        row = look_up(line[d : d + 1, :], planes)
        owner, local, rank = ranks(row, count, code_dev, devices, upper)
        wanted = jnp.where(owner == where_ref[0], local + 1, 0).astype(F32)
        part = rank & (GRID - 1)
        found = jnp.zeros((1, LANES), F32)
        for z in range(GRID):
            one = jnp.sum(jnp.where(part == z, wanted, 0.0), axis=1, keepdims=True)
            found = found + jnp.where(lane == z, one, 0.0)
        picks[d : d + 1, :] = jnp.maximum(found.astype(I32) - 1, 0)
        owner_here = jnp.where(doc == d, owner, owner_here)
        rank_here = jnp.where(doc == d, rank, rank_here)
    to_scalars = pltpu.make_async_copy(picks, picked, sem.at[1])
    to_scalars.start()
    to_scalars.wait()
    copies = []
    for d in range(docs):
        for z in range(GRID):
            k = d * GRID + z
            copies.append(pltpu.make_async_copy(cache_ref.at[picked[d, z]], rows.at[k], sems.at[k]))
            copies[-1].start()

    part = rank_here & (GRID - 1)
    spot = rank_here >> 2
    live = jnp.where(part == where_ref[1], (spot + 1).astype(F32), 0.0)
    mine = owner_here == iota((devices, n), 0)
    place = jnp.sum(jnp.where(mine, live, 0.0), axis=1, keepdims=True)
    width = devices * DESC
    spread = jnp.where(iota((devices, width), 0) == iota((devices, width), 1) // DESC, place, 0.0)
    spread = jnp.sum(spread, axis=0, keepdims=True).astype(I32)
    inside = iota((1, width), 1) & (DESC - 1)
    slot_ref[...] = jnp.where(spread > 0, (spread - 1) * DESC + inside, -1)
    pos_ref[...] = part * (count // GRID) + spot

    low = iota((GRID, DESC, LANES), 2) < HALF
    for d in range(docs):
        for copy in copies[d * GRID : (d + 1) * GRID]:
            copy.wait()
        block = pl.ds(d * GRID, GRID)
        for p in range(HEADS // 2):
            cols = pl.ds(p * LANES, LANES)
            keys = rows[block, 0, :, cols].astype(F32)
            values = rows[block, 1, :, cols].astype(F32)
            keys_turned = pltpu.roll(keys, HALF, 2)
            values_turned = pltpu.roll(values, HALF, 2)
            for s in range(2):
                head = 2 * p + s
                group, inner = head // 3, head % 3
                key_low = keys if s == 0 else keys_turned
                key_high = keys_turned if s == 0 else keys
                value_low = values if s == 0 else values_turned
                value_high = values_turned if s == 0 else values
                if inner == 1:
                    tile = jnp.where(low, value_low, key_high)
                else:
                    tile = jnp.where(low, key_low, value_high)
                send_ref[block, group, :, pl.ds(inner * LANES, LANES)] = tile.astype(BF)


def compact_kernel(slot_ref, got_ref, first_ref, rest_ref):
    rows = first_ref.shape[0]
    pick = (iota((rows, got_ref.shape[0]), 0) == slot_ref[...]).astype(F32).astype(BF)
    packed = dot(pick, got_ref[...]).astype(BF)
    first_ref[...] = packed[:, :LANES]
    rest_ref[...] = packed[:, LANES:]


def layer_norm(values):
    centered = values - jnp.mean(values, axis=-1, keepdims=True)
    spread = jnp.mean(centered * centered, axis=-1, keepdims=True)
    return centered * lax.rsqrt(spread + 1e-05)


def window_kernel(
    low_ref, hidden_ref, high_ref, flag_ref, wkv_hbm, wq_hbm, wo_hbm, xq_hbm, middle_ref, query_ref, wkv_ref, wq_ref, wo_ref, xq_ref, normed, keys, values, queries, context, bias, sems
):
    tok, width = hidden_ref.shape
    win = HALF_WIN
    span = 3 * win
    total = tok + 2 * win
    pairs = width // LANES
    pieces = ((wkv_hbm, wkv_ref), (wq_hbm, wq_ref), (wo_hbm, wo_ref), (xq_hbm, xq_ref))
    copies = [pltpu.make_async_copy(src, dst, sems.at[k]) for k, (src, dst) in enumerate(pieces)]
    for copy in copies:
        copy.start()
    normed[:win, :] = layer_norm(low_ref[:win, :].astype(F32)).astype(BF)
    normed[win : win + tok, :] = layer_norm(hidden_ref[...].astype(F32)).astype(BF)
    normed[win + tok :, :] = layer_norm(high_ref[:win, :].astype(F32)).astype(BF)
    flags = jnp.concatenate(
        [low_ref[win : win + 1, :win].astype(F32), flag_ref[...], high_ref[win : win + 1, :win].astype(F32)], axis=1
    )
    gap = iota((win, span), 1) - iota((win, span), 0)
    near = (gap >= 0) & (gap <= 2 * win)
    for b in range(tok // win):
        usable = (flags[:, b * win : b * win + span] > 0.0) | (gap == win)
        bias[b] = jnp.where(near & usable, 0.0, -1e30)
    for p in range(pairs):
        values[:, (2 * p + 1) * LANES : (2 * p + 2) * LANES] = jnp.ones((total, LANES), BF)
    wide = 2 * LANES
    copies[0].wait()
    for c in range(0, width, wide):
        keys[:, c : c + wide] = dot(normed[...], wkv_ref[:, c : c + wide]).astype(BF)
    for c in range(0, width, wide):
        part = dot(normed[...], wkv_ref[:, width + c : width + c + wide]).astype(BF).astype(F32) * 2.0**-8
        part = part.astype(BF)
        values[:, 2 * c : 2 * c + LANES] = part[:, :LANES]
        values[:, 2 * c + wide : 2 * c + wide + LANES] = part[:, LANES:]
    copies[1].wait()
    for c in range(0, width, wide):
        queries[:, c : c + wide] = (dot(normed[win : win + tok, :], wq_ref[:, c : c + wide]) * SCALE).astype(BF)
    low = iota((win, LANES), 1) < HALF
    for b in range(tok // win):
        for p in range(pairs):
            cols = slice(p * LANES, (p + 1) * LANES)
            query = queries[b * win : (b + 1) * win, cols]
            key = keys[b * win : b * win + span, cols]
            value = values[b * win : b * win + span, 2 * p * LANES : (2 * p + 2) * LANES]
            nothing = jnp.zeros_like(query)
            both = jnp.concatenate([jnp.where(low, query, nothing), jnp.where(low, nothing, query)], axis=0)
            scores = dot_t(both, key).reshape(2, win, span) + bias[b][None]
            out = dot(jnp.exp2(scores).astype(BF).reshape(2 * win, span), value)
            out = out[:, :LANES] / out[:, LANES:] * 256.0
            context[b * win : (b + 1) * win, cols] = jnp.where(low, out[:win], out[win:]).astype(BF)
    copies[2].wait()
    copies[3].wait()
    valid = jnp.transpose(jnp.broadcast_to(flag_ref[...], (LANES, tok)))
    for b in range(tok // win):
        rows = slice(b * win, (b + 1) * win)
        mixed = hidden_ref[rows, :].astype(F32) + dot(context[rows, :], wo_ref[...])
        mixed = mixed.astype(BF)
        middle_ref[rows, :] = mixed
        cross = dot(layer_norm(mixed.astype(F32)).astype(BF), xq_ref[...]) * SCALE
        tiles = [cross[:, p * LANES : (p + 1) * LANES] for p in range(pairs)]
        turned = [pltpu.roll(t, HALF, 1) for t in tiles]

        def placed(head, upper):
            return (turned if (head % 2 == 1) != upper else tiles)[head // 2]

        for g in range(GRID):
            first = jnp.where(low, placed(3 * g, False), placed(3 * g + 1, True))
            second = jnp.where(low, placed(3 * g + 2, False), valid[rows, :])
            query_ref[g, rows, :LANES] = first.astype(BF)
            query_ref[g, rows, LANES:] = second.astype(BF)


def cross_kernel(heads, count, where_ref, pos_ref, query_ref, *refs):
    kv_refs, refs = refs[:GRID], refs[GRID:]
    last = 2 in heads
    if last:
        before_ref, earlier_ref, out_ref, keys, values, expds, total = refs
    else:
        out_ref, mass_ref, keys, values, expds, total = refs
    held = kv_refs[0].shape[0]
    groups, tok, _ = query_ref.shape
    small = iota((tok, LANES), 1) < HALF
    if last:
        total[...] = before_ref[...]
    else:
        total[...] = jnp.zeros_like(total)
    lower = iota((held, LANES), 1) < HALF
    for k, inner in enumerate(heads):
        for c in range(GRID):
            block = kv_refs[c][:, k * LANES : (k + 1) * LANES]
            scaled = block.astype(F32) * 2.0**-4
            keys[k, c * held : (c + 1) * held, :] = block
            values[k, c * held : (c + 1) * held, :] = jnp.where(lower == (inner == 1), scaled, 1.0).astype(BF)

    def one(g, k, slot):
        inner = heads[k]
        value_low = inner == 1
        tile = LANES if inner == 2 else 0
        query = query_ref[g, :, tile : tile + LANES]
        query = jnp.where(small != value_low, query, jnp.zeros_like(query))
        acc = jnp.zeros((tok, LANES), F32)
        for c in range(0, GRID * held, 512):
            expd = jnp.exp2(dot_t(query, keys[k, c : c + 512, :])).astype(BF)
            expds[slot, :, c : c + 512] = expd
            acc = acc + dot(expd, values[k, c : c + 512, :])
        at = LANES - 1 if value_low else 0
        inverse = 1.0 / acc[:, at : at + 1]
        out = jnp.where(small == value_low, (acc * inverse) * 16.0, 0.0)
        share = inverse * query_ref[g, :, 2 * LANES - 1 :].astype(F32)
        for c in range(0, GRID * held, 512):
            mass = jnp.sum(expds[slot, :, c : c + 512].astype(F32) * share, axis=0, keepdims=True)
            total[:1, c : c + 512] = total[:1, c : c + 512] + mass
        return out

    if not last:

        def body(i, carry):
            for u in range(2):
                out_ref[2 * i + u] = one(2 * i + u, 0, u).astype(BF)
            return carry

        lax.fori_loop(0, groups // 2, body, 0)
        mass_ref[...] = total[...]
        return

    def body(g, carry):
        first = jnp.where(small, one(g, 0, 0), earlier_ref[g].astype(F32))
        out_ref[g, :tok, :LANES] = first.astype(BF)
        out_ref[g, :tok, LANES:] = one(g, 1, 1).astype(BF)
        return carry

    lax.fori_loop(0, groups, body, 0)
    padded = pos_ref.shape[1]
    score = jnp.zeros((8, padded), F32)
    line = iota((8, held), 0)
    for c in range(GRID):
        mass = jnp.broadcast_to(total[:1, c * held : (c + 1) * held], (8, held))
        first, second, third = thirds(mass)
        parts = jnp.where(line == 0, first, jnp.where(line == 1, second, jnp.where(line == 2, third, 0.0)))
        origin = (where_ref[1] + GRID - c) & (GRID - 1)
        at = iota((held, padded), 0) // DESC + origin * (count // GRID)
        score = score + dot(parts.astype(BF), (at == pos_ref[...]).astype(F32).astype(BF))
    score = jnp.sum(score, axis=0, keepdims=True)
    tokens = jnp.zeros((1, 1), F32)
    for g in range(groups):
        tokens = tokens + jnp.sum(query_ref[g, :, 2 * LANES - 1 :].astype(F32), axis=0, keepdims=True)
    score = jnp.where(iota((1, padded), 1) == count, tokens, score)
    rest = out_ref.shape[1] - tok
    left = jnp.zeros((rest, 2 * LANES), F32)
    right = jnp.zeros((rest, LANES), F32)
    for k, part in enumerate(thirds(score)):
        left = jnp.where(iota(left.shape, 0) == k, part[:, : 2 * LANES], left)
        right = jnp.where(iota(right.shape, 0) == 3 + k, part[:, 2 * LANES :], right)
    tail = left + jnp.concatenate([right, jnp.zeros_like(right)], axis=1)
    for g in range(groups):
        out_ref[g, tok:, :] = tail.astype(BF)


def thirds(value):
    first = value.astype(BF).astype(F32)
    second = (value - first).astype(BF).astype(F32)
    return first, second, value - first - second


def mass_kernel(tail_ref, out_ref):
    tail = jnp.sum(tail_ref[...].astype(F32), axis=0)
    left = jnp.sum(tail[:3, :], axis=0, keepdims=True)
    right = jnp.sum(tail[3:6, :LANES], axis=0, keepdims=True)
    out_ref[...] = jnp.concatenate([left, right], axis=1)


def final_kernel(middle_ref, out_refs, weight_ref, out_ref):
    groups = out_refs.shape[0]
    tok = middle_ref.shape[0]
    size = 3 * HALF
    acc = middle_ref[...].astype(F32)
    for g in range(groups):
        at = g * size
        turned = jnp.concatenate(
            [
                weight_ref[at + HALF : at + 2 * HALF, :],
                weight_ref[at : at + HALF, :],
                weight_ref[at + HALF : at + size, :],
            ],
            axis=0,
        )
        acc = acc + dot(out_refs[g, :tok, :], turned)
    out_ref[...] = acc.astype(BF)


def local(hidden, token_ids, w_query, w_keyval, w_out, x_query, x_out, shortlist, code_row, code_cache):
    doc_hidden = hidden[0]
    tok, width = doc_hidden.shape
    seq_count = lax.axis_size("seq")
    docs = lax.axis_size("doc")
    devices = docs * seq_count
    seq_index = lax.axis_index("seq")
    own = lax.axis_index("doc") * seq_count + seq_index
    where = jnp.stack([own, seq_index // GRID, lax.axis_index("doc")]).astype(I32)
    count = shortlist.shape[1]
    padded = -(-count // LANES) * LANES
    code_dev = code_cache.shape[0]
    held = count // GRID * DESC
    table = code_row.reshape(-1, LANES)
    anywhere = pl.BlockSpec(memory_space=pl.ANY)

    all_codes = lax.all_gather(shortlist, "doc", axis=0, tiled=False)
    all_codes, doc_hidden, token_ids = lax.optimization_barrier((all_codes, doc_hidden, token_ids))

    flag = (token_ids != 0).astype(BF)
    forward = [(i, i + 1) for i in range(seq_count - 1)]
    backward = [(t, s) for s, t in forward]

    def with_flags(rows, flags):
        return jnp.concatenate([rows, jnp.pad(flags, ((0, 7), (0, width - HALF_WIN)))], axis=0)

    low = lax.ppermute(with_flags(doc_hidden[tok - HALF_WIN :], flag[:, tok - HALF_WIN :]), "seq", forward)
    high = lax.ppermute(with_flags(doc_hidden[:HALF_WIN], flag[:, :HALF_WIN]), "seq", backward)

    send, slots, pos = pl.pallas_call(
        functools.partial(route_kernel, count, code_dev, devices),
        name="route",
        out_shape=(
            jax.ShapeDtypeStruct((docs * GRID, GRID, DESC, 3 * LANES), BF),
            jax.ShapeDtypeStruct((1, devices * DESC), I32),
            jax.ShapeDtypeStruct((1, padded), I32),
        ),
        in_specs=[smem(), vmem(), anywhere, anywhere],
        out_specs=(vmem(),) * 3,
        scratch_shapes=[
            pltpu.VMEM(table.shape, I32),
            pltpu.VMEM((docs * GRID, 2, DESC, width), BF),
            pltpu.VMEM((docs, padded), I32),
            pltpu.VMEM((docs, LANES), I32),
            pltpu.SMEM((docs, LANES), I32),
            pltpu.SemaphoreType.DMA((docs * GRID,)),
            pltpu.SemaphoreType.DMA((2,)),
        ],
        compiler_params=params(24),
        cost_estimate=cost(10**9, 0, 2 * 10**6),
    )(where, all_codes, table, code_cache)
    got = lax.all_to_all(
        send.reshape(devices, DESC, 3 * LANES), ("doc", "seq"), split_axis=0, concat_axis=0, tiled=True
    )

    middle, queries = pl.pallas_call(
        window_kernel,
        name="window",
        out_shape=(
            jax.ShapeDtypeStruct((tok, width), BF),
            jax.ShapeDtypeStruct((GRID, tok, 2 * LANES), BF),
        ),
        in_specs=[vmem()] * 4 + [anywhere] * 4,
        out_specs=(vmem(), vmem()),
        scratch_shapes=[
            pltpu.VMEM((width, 2 * width), BF),
            pltpu.VMEM((width, width), BF),
            pltpu.VMEM((width, width), BF),
            pltpu.VMEM((width, width), BF),
            pltpu.VMEM((tok + 2 * HALF_WIN, width), BF),
            pltpu.VMEM((tok + 2 * HALF_WIN, width), BF),
            pltpu.VMEM((tok + 2 * HALF_WIN, 2 * width), BF),
            pltpu.VMEM((tok, width), BF),
            pltpu.VMEM((tok, width), BF),
            pltpu.VMEM((tok // HALF_WIN, HALF_WIN, 3 * HALF_WIN), F32),
            pltpu.SemaphoreType.DMA((4,)),
        ],
        compiler_params=params(48),
        cost_estimate=cost(12 * 10**9, 5 * 10**6, 10**7),
    )(low, doc_hidden, high, flag.astype(F32), w_keyval, w_query, w_out, x_query)

    lines = [[GRID * z + x for x in range(GRID)] for z in range(GRID)]

    def across(block):
        return lax.all_to_all(
            block, "seq", split_axis=0, concat_axis=0, axis_index_groups=lines, tiled=True
        )

    queries = across(queries)

    blocks = pl.pallas_call(
        compact_kernel,
        name="compact",
        out_shape=(jax.ShapeDtypeStruct((held, LANES), BF), jax.ShapeDtypeStruct((held, 2 * LANES), BF)),
        in_specs=[vmem()] * 2,
        out_specs=(vmem(),) * 2,
        compiler_params=params(24),
        cost_estimate=cost(10**9, 0, 2 * 10**6),
    )(slots, got.reshape(devices * DESC, 3 * LANES))

    def turns(block):
        parts = []
        for shift in range(1, GRID):
            pairs = [(i, (i + GRID * shift) % seq_count) for i in range(seq_count)]
            parts.append(lax.ppermute(block, "seq", pairs))
        return parts

    first, rest = [[block] + turns(block) for block in blocks]

    def cross(heads, parts, extra, outs):
        return pl.pallas_call(
            functools.partial(cross_kernel, heads, count),
            name="cross",
            out_shape=outs,
            in_specs=[smem()] + [vmem()] * (2 + GRID + len(extra)),
            out_specs=jax.tree.map(lambda _: vmem(), outs),
            scratch_shapes=[
                pltpu.VMEM((len(heads), GRID * held, LANES), BF),
                pltpu.VMEM((len(heads), GRID * held, LANES), BF),
                pltpu.VMEM((2, tok, GRID * held), BF),
                pltpu.VMEM((8, GRID * held), F32),
            ],
            compiler_params=params(40),
            cost_estimate=cost(len(heads) * 10**10, 5 * 10**6, 4 * 10**6),
        )(where, pos, queries, *parts, *extra)

    out, mass = cross(
        (0,),
        first,
        (),
        (jax.ShapeDtypeStruct((GRID, tok, LANES), BF), jax.ShapeDtypeStruct((8, GRID * held), F32)),
    )
    out = cross((1, 2), rest, (mass, out), jax.ShapeDtypeStruct((GRID, tok + 16, 2 * LANES), BF))
    out = across(out)

    mass = pl.pallas_call(
        mass_kernel,
        name="mass",
        grid=(1,),
        out_shape=jax.ShapeDtypeStruct((1, padded), F32),
        in_specs=[pl.BlockSpec((GRID, 16, 2 * LANES), lambda i: (0, tok // 16, 0))],
        out_specs=pl.BlockSpec((1, padded), lambda i: (0, 0)),
        cost_estimate=cost(10**5, 0, 10**5),
    )(out)
    one, two, three = turns(mass)
    sums = (mass + two) + (one + three)
    tokens = sums[:, count : count + 1] * (1.0 / GRID)
    cand_score = count * sums[:, :count] / (HEADS * tokens)

    refined = pl.pallas_call(
        final_kernel,
        name="final",
        out_shape=jax.ShapeDtypeStruct((tok, width), BF),
        in_specs=[vmem()] * 3,
        out_specs=vmem(),
        compiler_params=params(16),
        cost_estimate=cost(10**9, 0, 4 * 10**6),
    )(middle, out, x_out)
    return (refined[None], cand_score)


def solution(mesh):
    return jax.shard_map(
        local,
        mesh=mesh,
        in_specs=(
            P("doc", "seq", None),
            P("doc", "seq"),
            P(),
            P(),
            P(),
            P(),
            P(),
            P("doc", None),
            P(),
            P(("doc", "seq"), None, None, None),
        ),
        out_specs=(P("doc", "seq", None), P("doc", None)),
        check_vma=False,
    )
```

```python
import functools
import math

import jax
import jax.numpy as jnp
from jax import lax
from jax.experimental import pallas as pl
from jax.experimental.pallas import tpu as pltpu
from jax.sharding import PartitionSpec as P

HEADS = 12
HALF_WIN = 256
DESC = 8
GRID = 4
LANES = 128
HALF = 64
SCALE = math.log2(math.e) / 8.0
BF = jnp.bfloat16
F32 = jnp.float32
I32 = jnp.int32


def iota(shape, dim):
    return lax.broadcasted_iota(I32, shape, dim)


def dot(a, b):
    return jnp.dot(a, b, preferred_element_type=F32)


def dot_t(a, b):
    return lax.dot_general(a, b, (((1,), (1,)), ((), ())), preferred_element_type=F32)


def params(mib):
    return pltpu.CompilerParams(vmem_limit_bytes=mib << 20)


def vmem():
    return pl.BlockSpec(memory_space=pltpu.VMEM)


def smem():
    return pl.BlockSpec(memory_space=pltpu.SMEM)


def pinned(array):
    return pltpu.with_memory_space_constraint(array, pltpu.HBM)


def hbm():
    return pl.BlockSpec(memory_space=pltpu.HBM)


def cost(flops, exps, bytes_):
    return pl.CostEstimate(flops=flops, transcendentals=exps, bytes_accessed=bytes_)


def split_table(table):
    high = table >> 8
    return jnp.concatenate([high, table - (high << 8)], axis=1).astype(F32).astype(BF)


def look_up(code, table):
    n = code.shape[1]
    picks = (iota((table.shape[0], n), 0) == (code >> 7)).astype(F32).astype(BF)
    found = lax.dot_general(table, picks, (((0,), (0,)), ((), ())), preferred_element_type=F32)
    here = iota((LANES, n), 0) == (code & 127)
    value = jnp.where(here, found[:LANES] * 256.0 + found[LANES:], 0.0)
    return jnp.sum(value, axis=0, keepdims=True)


def ranks(row, count, code_dev, devices, upper):
    n = row.shape[1]
    owner = jnp.floor((row + 0.5) * (1.0 / code_dev))
    local = (row - owner * code_dev).astype(I32)
    owner = jnp.where(iota((1, n), 1) < count, owner.astype(I32), 2 * devices)
    sub = iota((devices, n), 0)
    mine = owner == sub
    starts = jnp.sum((owner < sub).astype(F32), axis=1, keepdims=True)
    before = dot(mine.astype(F32).astype(BF), upper)
    rank = jnp.sum(jnp.where(mine, starts + before, 0.0), axis=0, keepdims=True)
    return owner, local, rank.astype(I32)


def upper_ones(n):
    return (iota((n, n), 0) < iota((n, n), 1)).astype(F32).astype(BF)


def route_kernel(
    count, code_dev, devices, where_ref, codes_ref, table_ref, cache_ref, send_ref, slot_ref, pos_ref, table, rows, line, picks, picked, sems, sem
):
    docs = codes_ref.shape[0]
    n = line.shape[1]
    fetch = pltpu.make_async_copy(table_ref, table, sem.at[0])
    fetch.start()
    upper = upper_ones(n)
    lane = iota((1, LANES), 1)
    line[...] = jnp.full(line.shape, -1, I32)
    for d in range(docs):
        line[d : d + 1, :count] = codes_ref[d]
    fetch.wait()
    planes = split_table(table[...])
    doc = where_ref[2]
    owner_here = jnp.zeros((1, n), I32)
    rank_here = jnp.zeros((1, n), I32)
    for d in range(docs):
        row = look_up(line[d : d + 1, :], planes)
        owner, local, rank = ranks(row, count, code_dev, devices, upper)
        wanted = jnp.where(owner == where_ref[0], local + 1, 0).astype(F32)
        part = rank & (GRID - 1)
        found = jnp.zeros((1, LANES), F32)
        for z in range(GRID):
            one = jnp.sum(jnp.where(part == z, wanted, 0.0), axis=1, keepdims=True)
            found = found + jnp.where(lane == z, one, 0.0)
        picks[d : d + 1, :] = jnp.maximum(found.astype(I32) - 1, 0)
        owner_here = jnp.where(doc == d, owner, owner_here)
        rank_here = jnp.where(doc == d, rank, rank_here)
    to_scalars = pltpu.make_async_copy(picks, picked, sem.at[1])
    to_scalars.start()
    to_scalars.wait()
    copies = []
    for d in range(docs):
        for z in range(GRID):
            k = d * GRID + z
            copies.append(pltpu.make_async_copy(cache_ref.at[picked[d, z]], rows.at[k], sems.at[k]))
            copies[-1].start()

    part = rank_here & (GRID - 1)
    spot = rank_here >> 2
    live = jnp.where(part == where_ref[1], (spot + 1).astype(F32), 0.0)
    mine = owner_here == iota((devices, n), 0)
    place = jnp.sum(jnp.where(mine, live, 0.0), axis=1, keepdims=True)
    width = devices * DESC
    spread = jnp.where(iota((devices, width), 0) == iota((devices, width), 1) // DESC, place, 0.0)
    spread = jnp.sum(spread, axis=0, keepdims=True).astype(I32)
    inside = iota((1, width), 1) & (DESC - 1)
    slot_ref[...] = jnp.where(spread > 0, (spread - 1) * DESC + inside, -1)
    pos_ref[...] = part * (count // GRID) + spot

    low = iota((GRID, DESC, LANES), 2) < HALF
    for d in range(docs):
        for copy in copies[d * GRID : (d + 1) * GRID]:
            copy.wait()
        block = pl.ds(d * GRID, GRID)
        for p in range(HEADS // 2):
            cols = pl.ds(p * LANES, LANES)
            keys = rows[block, 0, :, cols].astype(F32)
            values = rows[block, 1, :, cols].astype(F32)
            keys_turned = pltpu.roll(keys, HALF, 2)
            values_turned = pltpu.roll(values, HALF, 2)
            for s in range(2):
                head = 2 * p + s
                group, inner = head // 3, head % 3
                key_low = keys if s == 0 else keys_turned
                key_high = keys_turned if s == 0 else keys
                value_low = values if s == 0 else values_turned
                value_high = values_turned if s == 0 else values
                if inner == 1:
                    tile = jnp.where(low, value_low, key_high)
                else:
                    tile = jnp.where(low, key_low, value_high)
                send_ref[block, group, :, pl.ds(inner * LANES, LANES)] = tile.astype(BF)


def compact_kernel(slot_ref, got_ref, first_ref, rest_ref):
    rows = first_ref.shape[0]
    pick = (iota((rows, got_ref.shape[0]), 0) == slot_ref[...]).astype(F32).astype(BF)
    packed = dot(pick, got_ref[...]).astype(BF)
    first_ref[...] = packed[:, :LANES]
    rest_ref[...] = packed[:, LANES:]


def layer_norm(values):
    centered = values - jnp.mean(values, axis=-1, keepdims=True)
    spread = jnp.mean(centered * centered, axis=-1, keepdims=True)
    return centered * lax.rsqrt(spread + 1e-05)


def halo_kernel(hidden_ref, tokens_ref, tail_ref, head_ref):
    tok, width = hidden_ref.shape
    win = HALF_WIN
    flags = (tokens_ref[...] != 0).astype(F32)
    for ref, start in ((tail_ref, tok - win), (head_ref, 0)):
        ref[:win, :] = hidden_ref[start : start + win, :]
        row = jnp.concatenate([flags[:, start : start + win], jnp.zeros((1, width - win), F32)], axis=1)
        ref[win:, :] = jnp.broadcast_to(row, (8, width)).astype(BF)


def window_kernel(
    low_ref, hidden_ref, high_ref, tokens_ref, wkv_hbm, wq_hbm, wo_hbm, xq_hbm, middle_ref, query_ref, wkv_ref, wq_ref, wo_ref, xq_ref, normed, keys, values, queries, context, bias, sems
):
    tok, width = hidden_ref.shape
    win = HALF_WIN
    span = 3 * win
    total = tok + 2 * win
    pairs = width // LANES
    pieces = ((wkv_hbm, wkv_ref), (wq_hbm, wq_ref), (wo_hbm, wo_ref), (xq_hbm, xq_ref))
    copies = [pltpu.make_async_copy(src, dst, sems.at[k]) for k, (src, dst) in enumerate(pieces)]
    for copy in copies:
        copy.start()
    normed[:win, :] = layer_norm(low_ref[:win, :].astype(F32)).astype(BF)
    normed[win : win + tok, :] = layer_norm(hidden_ref[...].astype(F32)).astype(BF)
    normed[win + tok :, :] = layer_norm(high_ref[:win, :].astype(F32)).astype(BF)
    own_flags = (tokens_ref[...] != 0).astype(F32)
    flags = jnp.concatenate(
        [low_ref[win : win + 1, :win].astype(F32), own_flags, high_ref[win : win + 1, :win].astype(F32)], axis=1
    )
    gap = iota((win, span), 1) - iota((win, span), 0)
    near = (gap >= 0) & (gap <= 2 * win)
    for b in range(tok // win):
        usable = (flags[:, b * win : b * win + span] > 0.0) | (gap == win)
        bias[b] = jnp.where(near & usable, 0.0, -1e30)
    for p in range(pairs):
        values[:, (2 * p + 1) * LANES : (2 * p + 2) * LANES] = jnp.ones((total, LANES), BF)
    wide = 2 * LANES
    copies[0].wait()
    for c in range(0, width, wide):
        keys[:, c : c + wide] = dot(normed[...], wkv_ref[:, c : c + wide]).astype(BF)
    for c in range(0, width, wide):
        part = dot(normed[...], wkv_ref[:, width + c : width + c + wide]).astype(BF).astype(F32) * 2.0**-8
        part = part.astype(BF)
        values[:, 2 * c : 2 * c + LANES] = part[:, :LANES]
        values[:, 2 * c + wide : 2 * c + wide + LANES] = part[:, LANES:]
    copies[1].wait()
    for c in range(0, width, wide):
        queries[:, c : c + wide] = (dot(normed[win : win + tok, :], wq_ref[:, c : c + wide]) * SCALE).astype(BF)
    low = iota((win, LANES), 1) < HALF
    for b in range(tok // win):
        for p in range(pairs):
            cols = slice(p * LANES, (p + 1) * LANES)
            query = queries[b * win : (b + 1) * win, cols]
            key = keys[b * win : b * win + span, cols]
            value = values[b * win : b * win + span, 2 * p * LANES : (2 * p + 2) * LANES]
            nothing = jnp.zeros_like(query)
            both = jnp.concatenate([jnp.where(low, query, nothing), jnp.where(low, nothing, query)], axis=0)
            scores = dot_t(both, key).reshape(2, win, span) + bias[b][None]
            out = dot(jnp.exp2(scores).astype(BF).reshape(2 * win, span), value)
            out = out[:, :LANES] / out[:, LANES:] * 256.0
            context[b * win : (b + 1) * win, cols] = jnp.where(low, out[:win], out[win:]).astype(BF)
    copies[2].wait()
    copies[3].wait()
    thirds_of = [[] for _ in range(GRID)]
    for b in range(tok // win):
        rows = slice(b * win, (b + 1) * win)
        mixed = hidden_ref[rows, :].astype(F32) + dot(context[rows, :], wo_ref[...])
        mixed = mixed.astype(BF)
        middle_ref[rows, :] = mixed
        cross = dot(layer_norm(mixed.astype(F32)).astype(BF), xq_ref[...]) * SCALE
        tiles = [cross[:, p * LANES : (p + 1) * LANES] for p in range(pairs)]
        turned = [pltpu.roll(t, HALF, 1) for t in tiles]

        def placed(head, upper):
            return (turned if (head % 2 == 1) != upper else tiles)[head // 2]

        for g in range(GRID):
            first = jnp.where(low, placed(3 * g, False), placed(3 * g + 1, True))
            query_ref[g, rows, :] = first.astype(BF)
            thirds_of[g].append(placed(3 * g + 2, b == 1))
    line = iota((16, LANES), 0)
    marks = jnp.zeros((16, LANES), F32)
    for k in range(tok // LANES):
        marks = jnp.where(line == k, own_flags[:, k * LANES : (k + 1) * LANES], marks)
    for g in range(GRID):
        query_ref[g, tok : tok + win, :] = jnp.where(low, thirds_of[g][0], thirds_of[g][1]).astype(BF)
        query_ref[g, tok + win :, :] = marks.astype(BF)


def cross_kernel(heads, count, where_ref, pos_ref, query_ref, *refs):
    kv_refs, refs = refs[:GRID], refs[GRID:]
    last = 2 in heads
    if last:
        before_ref, earlier_ref, out_ref, keys, values, expds, total, sems = refs
    else:
        out_ref, mass_ref, keys, values, expds, total, sems = refs
    held = kv_refs[0].shape[0]
    tok = expds.shape[1]
    groups = query_ref.shape[0]
    half = tok // 2
    copies = []
    for k in range(len(heads)):
        for c in range(GRID):
            source = kv_refs[c].at[:, pl.ds(k * LANES, LANES)]
            copy = pltpu.make_async_copy(source, keys.at[k, pl.ds(c * held, held), :], sems.at[k * GRID + c])
            copy.start()
            copies.append(copy)
    small = iota((tok, LANES), 1) < HALF
    low = iota((half, LANES), 1) < HALF
    if last:
        total[...] = before_ref[...]
    else:
        total[...] = jnp.zeros_like(total)
    lower = iota((held, LANES), 1) < HALF
    for k, inner in enumerate(heads):
        for c in range(GRID):
            copies[k * GRID + c].wait()
            rows = pl.ds(c * held, held)
            scaled = keys[k, rows, :].astype(F32) * 2.0**-4
            values[k, rows, :] = jnp.where(lower == (inner == 1), scaled, 1.0).astype(BF)

    def one(g, k, slot):
        inner = heads[k]
        value_low = inner == 1
        if inner == 2:
            packed = query_ref[g, tok : tok + half, :]
            turned = pltpu.roll(packed.astype(F32), HALF, 1).astype(BF)
            query = jnp.concatenate([packed, turned], axis=0)
        else:
            query = query_ref[g, :tok, :]
        query = jnp.where(small != value_low, query, jnp.zeros_like(query))
        acc = jnp.zeros((tok, LANES), F32)
        for c in range(0, GRID * held, 512):
            expd = jnp.exp2(dot_t(query, keys[k, c : c + 512, :])).astype(BF)
            expds[slot, :, c : c + 512] = expd
            acc = acc + dot(expd, values[k, c : c + 512, :])
        at = LANES - 1 if value_low else 0
        inverse = 1.0 / acc[:, at : at + 1]
        out = (acc * inverse) * 16.0
        share = jnp.where(iota((tok, 1), 0).astype(F32) < tokens_of(g), inverse, 0.0)
        for c in range(0, GRID * held, 512):
            mass = jnp.sum(expds[slot, :, c : c + 512].astype(F32) * share, axis=0, keepdims=True)
            total[:1, c : c + 512] = total[:1, c : c + 512] + mass
        return out

    def tokens_of(g):
        marks = query_ref[g, tok + half :, :].astype(F32)
        return jnp.sum(jnp.sum(marks, axis=0, keepdims=True), axis=1, keepdims=True)

    if not last:

        def body(i, carry):
            for u in range(2):
                out_ref[2 * i + u] = one(2 * i + u, 0, u).astype(BF)
            return carry

        lax.fori_loop(0, groups // 2, body, 0)
        mass_ref[...] = total[...]
        return

    def body(g, carry):
        out_ref[g, :tok, :] = jnp.where(small, one(g, 0, 0), earlier_ref[g].astype(F32)).astype(BF)
        out = one(g, 1, 1)
        out_ref[g, tok : tok + half, :] = jnp.where(low, pltpu.roll(out[:half], HALF, 1), out[half:]).astype(BF)
        return carry

    lax.fori_loop(0, groups, body, 0)
    padded = pos_ref.shape[1]
    score = jnp.zeros((8, padded), F32)
    line = iota((8, held), 0)
    for c in range(GRID):
        mass = jnp.broadcast_to(total[:1, c * held : (c + 1) * held], (8, held))
        first, second, third = thirds(mass)
        parts = jnp.where(line == 0, first, jnp.where(line == 1, second, jnp.where(line == 2, third, 0.0)))
        origin = (where_ref[1] + GRID - c) & (GRID - 1)
        at = iota((held, padded), 0) // DESC + origin * (count // GRID)
        score = score + dot(parts.astype(BF), (at == pos_ref[...]).astype(F32).astype(BF))
    score = jnp.sum(score, axis=0, keepdims=True)
    tokens = tokens_of(0)
    for g in range(1, groups):
        tokens = tokens + tokens_of(g)
    score = jnp.where(iota((1, padded), 1) == count, tokens, score)
    tail = jnp.zeros((16, LANES), F32)
    for k, part in enumerate(thirds(score)):
        for j in range(padded // LANES):
            tail = jnp.where(iota(tail.shape, 0) == 3 * j + k, part[:, j * LANES : (j + 1) * LANES], tail)
    for g in range(groups):
        out_ref[g, tok + half :, :] = tail.astype(BF)


def thirds(value):
    first = value.astype(BF).astype(F32)
    second = (value - first).astype(BF).astype(F32)
    return first, second, value - first - second


def mass_kernel(out_hbm, line_ref, tail, sem):
    groups, size, _ = tail.shape
    copy = pltpu.make_async_copy(out_hbm.at[:, pl.ds(out_hbm.shape[1] - size, size), :], tail, sem)
    copy.start()
    copy.wait()
    total = jnp.sum(tail[...].astype(F32), axis=0)
    for j in range(line_ref.shape[1] // LANES):
        line_ref[:, j * LANES : (j + 1) * LANES] = jnp.sum(total[3 * j : 3 * j + 3, :], axis=0, keepdims=True)


def final_kernel(middle_ref, got_ref, weight_ref, out_ref):
    tok = middle_ref.shape[0]
    half = tok // 2
    size = 3 * HALF
    low = iota((half, LANES), 1) < HALF
    acc = middle_ref[...].astype(F32)
    for g in range(got_ref.shape[0]):
        at = g * size
        heads = [weight_ref[at + k * HALF : at + (k + 1) * HALF, :] for k in (1, 0, 2, 2)]
        packed = got_ref[g, tok : tok + half, :]
        nothing = jnp.zeros_like(packed)
        third = jnp.concatenate([jnp.where(low, packed, nothing), jnp.where(low, nothing, packed)], axis=0)
        lhs = jnp.concatenate([got_ref[g, :tok, :], third], axis=1)
        acc = acc + dot(lhs, jnp.concatenate(heads, axis=0))
    out_ref[...] = acc.astype(BF)


def local(hidden, token_ids, w_query, w_keyval, w_out, x_query, x_out, shortlist, code_row, code_cache):
    doc_hidden = hidden[0]
    tok, width = doc_hidden.shape
    seq_count = lax.axis_size("seq")
    docs = lax.axis_size("doc")
    devices = docs * seq_count
    seq_index = lax.axis_index("seq")
    own = lax.axis_index("doc") * seq_count + seq_index
    where = jnp.stack([own, seq_index // GRID, lax.axis_index("doc")]).astype(I32)
    count = shortlist.shape[1]
    padded = -(-count // LANES) * LANES
    code_dev = code_cache.shape[0]
    held = count // GRID * DESC
    message = tok + tok // 2 + 16
    table = code_row.reshape(-1, LANES)

    asked = jnp.broadcast_to(shortlist[None], (docs, 1, count))
    asked, doc_hidden, token_ids = lax.optimization_barrier((asked, doc_hidden, token_ids))

    forward = [(i, i + 1) for i in range(seq_count - 1)]
    backward = [(t, s) for s, t in forward]
    all_codes = lax.all_to_all(asked, "doc", split_axis=0, concat_axis=0, tiled=True)
    tail, head = pl.pallas_call(
        halo_kernel,
        name="halo",
        out_shape=(jax.ShapeDtypeStruct((HALF_WIN + 8, width), BF),) * 2,
        in_specs=[vmem()] * 2,
        out_specs=(vmem(),) * 2,
        compiler_params=params(16),
        cost_estimate=cost(10**5, 0, 16 * 10**5),
    )(doc_hidden, token_ids)
    low = lax.ppermute(tail, "seq", forward)
    high = lax.ppermute(head, "seq", backward)

    send, slots, pos = pl.pallas_call(
        functools.partial(route_kernel, count, code_dev, devices),
        name="route",
        out_shape=(
            jax.ShapeDtypeStruct((docs * GRID, GRID, DESC, 3 * LANES), BF),
            jax.ShapeDtypeStruct((1, devices * DESC), I32),
            jax.ShapeDtypeStruct((1, padded), I32),
        ),
        in_specs=[smem(), vmem(), hbm(), hbm()],
        out_specs=(vmem(),) * 3,
        scratch_shapes=[
            pltpu.VMEM(table.shape, I32),
            pltpu.VMEM((docs * GRID, 2, DESC, width), BF),
            pltpu.VMEM((docs, padded), I32),
            pltpu.VMEM((docs, LANES), I32),
            pltpu.SMEM((docs, LANES), I32),
            pltpu.SemaphoreType.DMA((docs * GRID,)),
            pltpu.SemaphoreType.DMA((2,)),
        ],
        compiler_params=params(24),
        cost_estimate=cost(10**9, 0, 2 * 10**6),
    )(where, all_codes, pinned(table), pinned(code_cache))
    got = lax.all_to_all(
        send.reshape(devices, DESC, 3 * LANES), ("doc", "seq"), split_axis=0, concat_axis=0, tiled=True
    )

    middle, queries = pl.pallas_call(
        window_kernel,
        name="window",
        out_shape=(
            jax.ShapeDtypeStruct((tok, width), BF),
            jax.ShapeDtypeStruct((GRID, message, LANES), BF),
        ),
        in_specs=[vmem()] * 4 + [hbm()] * 4,
        out_specs=(vmem(), vmem()),
        scratch_shapes=[
            pltpu.VMEM((width, 2 * width), BF),
            pltpu.VMEM((width, width), BF),
            pltpu.VMEM((width, width), BF),
            pltpu.VMEM((width, width), BF),
            pltpu.VMEM((tok + 2 * HALF_WIN, width), BF),
            pltpu.VMEM((tok + 2 * HALF_WIN, width), BF),
            pltpu.VMEM((tok + 2 * HALF_WIN, 2 * width), BF),
            pltpu.VMEM((tok, width), BF),
            pltpu.VMEM((tok, width), BF),
            pltpu.VMEM((tok // HALF_WIN, HALF_WIN, 3 * HALF_WIN), F32),
            pltpu.SemaphoreType.DMA((4,)),
        ],
        compiler_params=params(32),
        cost_estimate=cost(12 * 10**9, 5 * 10**6, 10**7),
    )(low, doc_hidden, high, token_ids, *map(pinned, (w_keyval, w_query, w_out, x_query)))

    lines = [[GRID * z + x for x in range(GRID)] for z in range(GRID)]

    def across(block):
        return lax.all_to_all(
            block, "seq", split_axis=0, concat_axis=0, axis_index_groups=lines, tiled=True
        )

    queries = across(queries)

    blocks = pl.pallas_call(
        compact_kernel,
        name="compact",
        out_shape=(jax.ShapeDtypeStruct((held, LANES), BF), jax.ShapeDtypeStruct((held, 2 * LANES), BF)),
        in_specs=[vmem()] * 2,
        out_specs=(vmem(),) * 2,
        compiler_params=params(24),
        cost_estimate=cost(10**9, 0, 2 * 10**6),
    )(slots, got.reshape(devices * DESC, 3 * LANES))

    def turns(block):
        parts = []
        for shift in range(1, GRID):
            pairs = [(i, (i + GRID * shift) % seq_count) for i in range(seq_count)]
            parts.append(lax.ppermute(block, "seq", pairs))
        return parts

    first, rest = [[block] + turns(block) for block in blocks]

    def cross(heads, parts, extra, outs):
        return pl.pallas_call(
            functools.partial(cross_kernel, heads, count),
            name="cross",
            out_shape=outs,
            in_specs=[smem()] + [vmem()] * 2 + [hbm()] * GRID + [vmem()] * len(extra),
            out_specs=jax.tree.map(lambda _: vmem(), outs),
            scratch_shapes=[
                pltpu.VMEM((len(heads), GRID * held, LANES), BF),
                pltpu.VMEM((len(heads), GRID * held, LANES), BF),
                pltpu.VMEM((2, tok, GRID * held), BF),
                pltpu.VMEM((8, GRID * held), F32),
                pltpu.SemaphoreType.DMA((len(heads) * GRID,)),
            ],
            compiler_params=params(24),
            cost_estimate=cost(len(heads) * 10**10, 5 * 10**6, 4 * 10**6),
        )(where, pos, queries, *parts, *extra)

    out, mass = cross(
        (0,),
        first,
        (),
        (jax.ShapeDtypeStruct((GRID, tok, LANES), BF), jax.ShapeDtypeStruct((8, GRID * held), F32)),
    )
    out = cross((1, 2), rest, (mass, out), jax.ShapeDtypeStruct((GRID, message, LANES), BF))
    out = across(out)

    mass = pl.pallas_call(
        mass_kernel,
        name="mass",
        out_shape=jax.ShapeDtypeStruct((1, padded), F32),
        in_specs=[hbm()],
        out_specs=vmem(),
        scratch_shapes=[pltpu.VMEM((GRID, 16, LANES), BF), pltpu.SemaphoreType.DMA],
        cost_estimate=cost(10**5, 0, 10**5),
    )(out)
    one, two, three = turns(mass)
    sums = (mass + two) + (one + three)
    tokens = sums[:, count : count + 1] * (1.0 / GRID)
    cand_score = count * sums[:, :count] / (HEADS * tokens)

    refined = pl.pallas_call(
        final_kernel,
        name="final",
        out_shape=jax.ShapeDtypeStruct((tok, width), BF),
        in_specs=[vmem()] * 3,
        out_specs=vmem(),
        compiler_params=params(16),
        cost_estimate=cost(10**9, 0, 4 * 10**6),
    )(middle, out, x_out)
    return (refined[None], cand_score)


def solution(mesh):
    return jax.shard_map(
        local,
        mesh=mesh,
        in_specs=(
            P("doc", "seq", None),
            P("doc", "seq"),
            P(),
            P(),
            P(),
            P(),
            P(),
            P("doc", None),
            P(),
            P(("doc", "seq"), None, None, None),
        ),
        out_specs=(P("doc", "seq", None), P("doc", None)),
        check_vma=False,
    )
```

```python
import functools
import math

import jax
import jax.numpy as jnp
from jax import lax
from jax.experimental import pallas as pl
from jax.experimental.pallas import tpu as pltpu
from jax.sharding import PartitionSpec as P

HEADS = 12
HALF_WIN = 256
DESC = 8
GRID = 4
LANES = 128
HALF = 64
SCALE = math.log2(math.e) / 8.0
BF = jnp.bfloat16
F32 = jnp.float32
I32 = jnp.int32


def iota(shape, dim):
    return lax.broadcasted_iota(I32, shape, dim)


def dot(a, b):
    return jnp.dot(a, b, preferred_element_type=F32)


def dot_t(a, b):
    return lax.dot_general(a, b, (((1,), (1,)), ((), ())), preferred_element_type=F32)


def params(mib):
    return pltpu.CompilerParams(vmem_limit_bytes=mib << 20)


def vmem():
    return pl.BlockSpec(memory_space=pltpu.VMEM)


def smem():
    return pl.BlockSpec(memory_space=pltpu.SMEM)


def pinned(array):
    return pltpu.with_memory_space_constraint(array, pltpu.HBM)


def hbm():
    return pl.BlockSpec(memory_space=pltpu.HBM)


def cost(flops, exps, bytes_):
    return pl.CostEstimate(flops=flops, transcendentals=exps, bytes_accessed=bytes_)


def split_table(table):
    wide = jnp.transpose(table.astype(F32))
    high = jnp.floor(wide * (1.0 / 256.0))
    return jnp.concatenate([high, wide - high * 256.0], axis=0).astype(BF)


def look_up(code, table):
    n = code.shape[1]
    picks = (iota((table.shape[1], n), 0) == (code >> 7)).astype(F32).astype(BF)
    found = dot(table, picks)
    here = iota((LANES, n), 0) == (code & 127)
    value = jnp.where(here, found[:LANES] * 256.0 + found[LANES:], 0.0)
    return jnp.sum(value, axis=0, keepdims=True)


def ranks(row, count, code_dev, devices, upper):
    n = row.shape[1]
    owner = jnp.floor((row + 0.5) * (1.0 / code_dev))
    local = (row - owner * code_dev).astype(I32)
    owner = jnp.where(iota((1, n), 1) < count, owner.astype(I32), 2 * devices)
    sub = iota((devices, n), 0)
    mine = owner == sub
    starts = jnp.sum((owner < sub).astype(F32), axis=1, keepdims=True)
    before = dot(mine.astype(F32).astype(BF), upper)
    rank = jnp.sum(jnp.where(mine, starts + before, 0.0), axis=0, keepdims=True)
    return owner, local, rank.astype(I32)


def upper_ones(n):
    return (iota((n, n), 0) < iota((n, n), 1)).astype(F32).astype(BF)


def route_kernel(
    count, code_dev, devices, where_ref, codes_ref, table_ref, cache_ref, send_ref, slot_ref, pos_ref, table, rows, line, picks, picked, sems, sem
):
    docs = codes_ref.shape[0]
    n = line.shape[1]
    fetch = pltpu.make_async_copy(table_ref, table.at[pl.ds(0, table_ref.shape[0]), :], sem.at[0])
    fetch.start()
    upper = upper_ones(n)
    lane = iota((1, LANES), 1)
    table[table_ref.shape[0] :, :] = jnp.zeros((table.shape[0] - table_ref.shape[0], LANES), I32)
    line[...] = jnp.full(line.shape, -1, I32)
    for d in range(docs):
        line[d : d + 1, :count] = codes_ref[d]
    fetch.wait()
    planes = split_table(table[...])
    doc = where_ref[2]
    owner_here = jnp.zeros((1, n), I32)
    rank_here = jnp.zeros((1, n), I32)
    for d in range(docs):
        row = look_up(line[d : d + 1, :], planes)
        owner, local, rank = ranks(row, count, code_dev, devices, upper)
        wanted = jnp.where(owner == where_ref[0], local + 1, 0).astype(F32)
        part = rank & (GRID - 1)
        found = jnp.zeros((1, LANES), F32)
        for z in range(GRID):
            one = jnp.sum(jnp.where(part == z, wanted, 0.0), axis=1, keepdims=True)
            found = found + jnp.where(lane == z, one, 0.0)
        picks[d : d + 1, :] = jnp.maximum(found.astype(I32) - 1, 0)
        owner_here = jnp.where(doc == d, owner, owner_here)
        rank_here = jnp.where(doc == d, rank, rank_here)
    to_scalars = pltpu.make_async_copy(picks, picked, sem.at[1])
    to_scalars.start()
    to_scalars.wait()
    copies = []
    for d in range(docs):
        for z in range(GRID):
            k = d * GRID + z
            copies.append(pltpu.make_async_copy(cache_ref.at[picked[d, z]], rows.at[k], sems.at[k]))
            copies[-1].start()

    part = rank_here & (GRID - 1)
    spot = rank_here >> 2
    live = jnp.where(part == where_ref[1], (spot + 1).astype(F32), 0.0)
    mine = owner_here == iota((devices, n), 0)
    place = jnp.sum(jnp.where(mine, live, 0.0), axis=1, keepdims=True)
    width = devices * DESC
    spread = jnp.where(iota((devices, width), 0) == iota((devices, width), 1) // DESC, place, 0.0)
    spread = jnp.sum(spread, axis=0, keepdims=True).astype(I32)
    inside = iota((1, width), 1) & (DESC - 1)
    slot_ref[...] = jnp.where(spread > 0, (spread - 1) * DESC + inside, -1)
    pos_ref[...] = part * (count // GRID) + spot

    low = iota((GRID, DESC, LANES), 2) < HALF
    for d in range(docs):
        for copy in copies[d * GRID : (d + 1) * GRID]:
            copy.wait()
        block = pl.ds(d * GRID, GRID)
        for p in range(HEADS // 2):
            cols = pl.ds(p * LANES, LANES)
            keys = rows[block, 0, :, cols].astype(F32)
            values = rows[block, 1, :, cols].astype(F32)
            keys_turned = pltpu.roll(keys, HALF, 2)
            values_turned = pltpu.roll(values, HALF, 2)
            for s in range(2):
                head = 2 * p + s
                group, inner = head // 3, head % 3
                key_low = keys if s == 0 else keys_turned
                key_high = keys_turned if s == 0 else keys
                value_low = values if s == 0 else values_turned
                value_high = values_turned if s == 0 else values
                if inner == 1:
                    tile = jnp.where(low, value_low, key_high)
                else:
                    tile = jnp.where(low, key_low, value_high)
                send_ref[block, group, :, pl.ds(inner * LANES, LANES)] = tile.astype(BF)


def compact_kernel(slot_ref, got_ref, first_ref, rest_ref):
    rows = first_ref.shape[0]
    pick = (iota((rows, got_ref.shape[0]), 0) == slot_ref[...]).astype(F32).astype(BF)
    packed = dot(pick, got_ref[...]).astype(BF)
    first_ref[...] = packed[:, :LANES]
    rest_ref[...] = packed[:, LANES:]


def layer_norm(values):
    centered = values - jnp.mean(values, axis=-1, keepdims=True)
    spread = jnp.mean(centered * centered, axis=-1, keepdims=True)
    return centered * lax.rsqrt(spread + 1e-05)


def halo_kernel(hidden_ref, tokens_ref, tail_ref, head_ref):
    tok, width = hidden_ref.shape
    win = HALF_WIN
    flags = (tokens_ref[...] != 0).astype(F32)
    for ref, start in ((tail_ref, tok - win), (head_ref, 0)):
        ref[:win, :] = hidden_ref[start : start + win, :]
        row = jnp.concatenate([flags[:, start : start + win], jnp.zeros((1, width - win), F32)], axis=1)
        ref[win:, :] = jnp.broadcast_to(row, (8, width)).astype(BF)


def window_kernel(
    low_ref, hidden_ref, high_ref, tokens_ref, wkv_hbm, wq_hbm, wo_hbm, xq_hbm, middle_ref, query_ref, wkv_ref, wq_ref, wo_ref, xq_ref, normed, keys, values, queries, context, bias, sems
):
    tok, width = hidden_ref.shape
    win = HALF_WIN
    span = 3 * win
    total = tok + 2 * win
    pairs = width // LANES
    pieces = ((wkv_hbm, wkv_ref), (wq_hbm, wq_ref), (wo_hbm, wo_ref), (xq_hbm, xq_ref))
    copies = [pltpu.make_async_copy(src, dst, sems.at[k]) for k, (src, dst) in enumerate(pieces)]
    for copy in copies:
        copy.start()
    normed[:win, :] = layer_norm(low_ref[:win, :].astype(F32)).astype(BF)
    normed[win : win + tok, :] = layer_norm(hidden_ref[...].astype(F32)).astype(BF)
    normed[win + tok :, :] = layer_norm(high_ref[:win, :].astype(F32)).astype(BF)
    own_flags = (tokens_ref[...] != 0).astype(F32)
    flags = jnp.concatenate(
        [low_ref[win : win + 1, :win].astype(F32), own_flags, high_ref[win : win + 1, :win].astype(F32)], axis=1
    )
    gap = iota((win, span), 1) - iota((win, span), 0)
    near = (gap >= 0) & (gap <= 2 * win)
    for b in range(tok // win):
        usable = (flags[:, b * win : b * win + span] > 0.0) | (gap == win)
        bias[b] = jnp.where(near & usable, 0.0, -1e30)
    for p in range(pairs):
        values[:, (2 * p + 1) * LANES : (2 * p + 2) * LANES] = jnp.ones((total, LANES), BF)
    wide = 2 * LANES
    copies[0].wait()
    for c in range(0, width, wide):
        keys[:, c : c + wide] = dot(normed[...], wkv_ref[:, c : c + wide]).astype(BF)
    for c in range(0, width, wide):
        part = dot(normed[...], wkv_ref[:, width + c : width + c + wide]).astype(BF).astype(F32) * 2.0**-8
        part = part.astype(BF)
        values[:, 2 * c : 2 * c + LANES] = part[:, :LANES]
        values[:, 2 * c + wide : 2 * c + wide + LANES] = part[:, LANES:]
    copies[1].wait()
    for c in range(0, width, wide):
        queries[:, c : c + wide] = (dot(normed[win : win + tok, :], wq_ref[:, c : c + wide]) * SCALE).astype(BF)
    low = iota((win, LANES), 1) < HALF
    for b in range(tok // win):
        for p in range(pairs):
            cols = slice(p * LANES, (p + 1) * LANES)
            query = queries[b * win : (b + 1) * win, cols]
            key = keys[b * win : b * win + span, cols]
            value = values[b * win : b * win + span, 2 * p * LANES : (2 * p + 2) * LANES]
            nothing = jnp.zeros_like(query)
            both = jnp.concatenate([jnp.where(low, query, nothing), jnp.where(low, nothing, query)], axis=0)
            scores = dot_t(both, key).reshape(2, win, span) + bias[b][None]
            out = dot(jnp.exp2(scores).astype(BF).reshape(2 * win, span), value)
            out = out[:, :LANES] / out[:, LANES:] * 256.0
            context[b * win : (b + 1) * win, cols] = jnp.where(low, out[:win], out[win:]).astype(BF)
    copies[2].wait()
    copies[3].wait()
    thirds_of = [[] for _ in range(GRID)]
    for b in range(tok // win):
        rows = slice(b * win, (b + 1) * win)
        mixed = hidden_ref[rows, :].astype(F32) + dot(context[rows, :], wo_ref[...])
        mixed = mixed.astype(BF)
        middle_ref[rows, :] = mixed
        cross = dot(layer_norm(mixed.astype(F32)).astype(BF), xq_ref[...]) * SCALE
        tiles = [cross[:, p * LANES : (p + 1) * LANES] for p in range(pairs)]
        turned = [pltpu.roll(t, HALF, 1) for t in tiles]

        def placed(head, upper):
            return (turned if (head % 2 == 1) != upper else tiles)[head // 2]

        for g in range(GRID):
            first = jnp.where(low, placed(3 * g, False), placed(3 * g + 1, True))
            query_ref[g, rows, :] = first.astype(BF)
            thirds_of[g].append(placed(3 * g + 2, b == 1))
    line = iota((16, LANES), 0)
    marks = jnp.zeros((16, LANES), F32)
    for k in range(tok // LANES):
        marks = jnp.where(line == k, own_flags[:, k * LANES : (k + 1) * LANES], marks)
    for g in range(GRID):
        query_ref[g, tok : tok + win, :] = jnp.where(low, thirds_of[g][0], thirds_of[g][1]).astype(BF)
        query_ref[g, tok + win :, :] = marks.astype(BF)


def cross_kernel(heads, count, where_ref, pos_ref, query_ref, *refs):
    kv_refs, refs = refs[:GRID], refs[GRID:]
    last = 2 in heads
    if last:
        before_ref, earlier_ref, out_ref, score_ref, keys, values, expds, total, sems = refs
    else:
        out_ref, mass_ref, keys, values, expds, total, sems = refs
    held = kv_refs[0].shape[0]
    tok = expds.shape[1]
    groups = query_ref.shape[0]
    half = tok // 2
    copies = []
    for k in range(len(heads)):
        for c in range(GRID):
            source = kv_refs[c].at[:, pl.ds(k * LANES, LANES)]
            copy = pltpu.make_async_copy(source, keys.at[k, pl.ds(c * held, held), :], sems.at[k * GRID + c])
            copy.start()
            copies.append(copy)
    small = iota((tok, LANES), 1) < HALF
    low = iota((half, LANES), 1) < HALF
    if last:
        total[...] = before_ref[...]
    else:
        total[...] = jnp.zeros_like(total)
    lower = iota((held, LANES), 1) < HALF
    for k, inner in enumerate(heads):
        for c in range(GRID):
            copies[k * GRID + c].wait()
            rows = pl.ds(c * held, held)
            scaled = keys[k, rows, :].astype(F32) * 2.0**-4
            values[k, rows, :] = jnp.where(lower == (inner == 1), scaled, 1.0).astype(BF)

    def one(g, k, slot):
        inner = heads[k]
        value_low = inner == 1
        if inner == 2:
            packed = query_ref[g, tok : tok + half, :]
            turned = pltpu.roll(packed.astype(F32), HALF, 1).astype(BF)
            query = jnp.concatenate([packed, turned], axis=0)
        else:
            query = query_ref[g, :tok, :]
        query = jnp.where(small != value_low, query, jnp.zeros_like(query))
        acc = jnp.zeros((tok, LANES), F32)
        for c in range(0, GRID * held, 512):
            expd = jnp.exp2(dot_t(query, keys[k, c : c + 512, :])).astype(BF)
            expds[slot, :, c : c + 512] = expd
            acc = acc + dot(expd, values[k, c : c + 512, :])
        at = LANES - 1 if value_low else 0
        inverse = 1.0 / acc[:, at : at + 1]
        out = (acc * inverse) * 16.0
        share = jnp.where(iota((tok, 1), 0).astype(F32) < tokens_of(g), inverse, 0.0)
        for c in range(0, GRID * held, 512):
            mass = jnp.sum(expds[slot, :, c : c + 512].astype(F32) * share, axis=0, keepdims=True)
            total[:1, c : c + 512] = total[:1, c : c + 512] + mass
        return out

    def tokens_of(g):
        marks = query_ref[g, tok + half :, :].astype(F32)
        return jnp.sum(jnp.sum(marks, axis=0, keepdims=True), axis=1, keepdims=True)

    if not last:

        def body(i, carry):
            for u in range(2):
                out_ref[2 * i + u] = one(2 * i + u, 0, u).astype(BF)
            return carry

        lax.fori_loop(0, groups // 2, body, 0)
        mass_ref[...] = total[...]
        return

    def body(g, carry):
        out_ref[g, :tok, :] = jnp.where(small, one(g, 0, 0), earlier_ref[g].astype(F32)).astype(BF)
        out = one(g, 1, 1)
        out_ref[g, tok : tok + half, :] = jnp.where(low, pltpu.roll(out[:half], HALF, 1), out[half:]).astype(BF)
        return carry

    lax.fori_loop(0, groups, body, 0)
    padded = pos_ref.shape[1]
    score = jnp.zeros((8, padded), F32)
    line = iota((8, held), 0)
    for c in range(GRID):
        mass = jnp.broadcast_to(total[:1, c * held : (c + 1) * held], (8, held))
        first, second, third = thirds(mass)
        parts = jnp.where(line == 0, first, jnp.where(line == 1, second, jnp.where(line == 2, third, 0.0)))
        origin = (where_ref[1] + GRID - c) & (GRID - 1)
        at = iota((held, padded), 0) // DESC + origin * (count // GRID)
        score = score + dot(parts.astype(BF), (at == pos_ref[...]).astype(F32).astype(BF))
    score = jnp.sum(score, axis=0, keepdims=True)
    tokens = tokens_of(0)
    for g in range(1, groups):
        tokens = tokens + tokens_of(g)
    score = jnp.where(iota((1, padded), 1) == count, tokens, score)
    score_ref[...] = score


def thirds(value):
    first = value.astype(BF).astype(F32)
    second = (value - first).astype(BF).astype(F32)
    return first, second, value - first - second


def final_kernel(middle_ref, got_hbm, weight_hbm, out_ref, got_ref, weight_ref, sems):
    tok = middle_ref.shape[0]
    groups = got_ref.shape[0]
    whole = pltpu.make_async_copy(weight_hbm, weight_ref, sems.at[groups])
    whole.start()
    copies = [pltpu.make_async_copy(got_hbm.at[g], got_ref.at[g], sems.at[g]) for g in range(groups)]
    for copy in copies:
        copy.start()
    whole.wait()
    half = tok // 2
    size = 3 * HALF
    low = iota((half, LANES), 1) < HALF
    acc = middle_ref[...].astype(F32)
    for g in range(groups):
        copies[g].wait()
        at = g * size
        heads = [weight_ref[at + k * HALF : at + (k + 1) * HALF, :] for k in (1, 0, 2, 2)]
        packed = got_ref[g, tok : tok + half, :]
        nothing = jnp.zeros_like(packed)
        third = jnp.concatenate([jnp.where(low, packed, nothing), jnp.where(low, nothing, packed)], axis=0)
        lhs = jnp.concatenate([got_ref[g, :tok, :], third], axis=1)
        acc = acc + dot(lhs, jnp.concatenate(heads, axis=0))
    out_ref[...] = acc.astype(BF)


def local(hidden, token_ids, w_query, w_keyval, w_out, x_query, x_out, shortlist, code_row, code_cache):
    doc_hidden = hidden[0]
    tok, width = doc_hidden.shape
    seq_count = lax.axis_size("seq")
    docs = lax.axis_size("doc")
    devices = docs * seq_count
    seq_index = lax.axis_index("seq")
    own = lax.axis_index("doc") * seq_count + seq_index
    where = jnp.stack([own, seq_index // GRID, lax.axis_index("doc")]).astype(I32)
    count = shortlist.shape[1]
    padded = -(-count // LANES) * LANES
    code_dev = code_cache.shape[0]
    held = count // GRID * DESC
    message = tok + tok // 2 + 16
    table = code_row.reshape(-1, LANES)

    asked = jnp.broadcast_to(shortlist[None], (docs, 1, count))
    asked, doc_hidden, token_ids = lax.optimization_barrier((asked, doc_hidden, token_ids))

    forward = [(i, i + 1) for i in range(seq_count - 1)]
    backward = [(t, s) for s, t in forward]
    all_codes = lax.all_to_all(asked, "doc", split_axis=0, concat_axis=0, tiled=True)
    tail, head = pl.pallas_call(
        halo_kernel,
        name="halo",
        out_shape=(jax.ShapeDtypeStruct((HALF_WIN + 8, width), BF),) * 2,
        in_specs=[vmem()] * 2,
        out_specs=(vmem(),) * 2,
        compiler_params=params(16),
        cost_estimate=cost(10**5, 0, 16 * 10**5),
    )(doc_hidden, token_ids)
    low = lax.ppermute(tail, "seq", forward)
    high = lax.ppermute(head, "seq", backward)

    send, slots, pos = pl.pallas_call(
        functools.partial(route_kernel, count, code_dev, devices),
        name="route",
        out_shape=(
            jax.ShapeDtypeStruct((docs * GRID, GRID, DESC, 3 * LANES), BF),
            jax.ShapeDtypeStruct((1, devices * DESC), I32),
            jax.ShapeDtypeStruct((1, padded), I32),
        ),
        in_specs=[smem(), vmem(), hbm(), hbm()],
        out_specs=(vmem(),) * 3,
        scratch_shapes=[
            pltpu.VMEM((-(-table.shape[0] // LANES) * LANES, LANES), I32),
            pltpu.VMEM((docs * GRID, 2, DESC, width), BF),
            pltpu.VMEM((docs, padded), I32),
            pltpu.VMEM((docs, LANES), I32),
            pltpu.SMEM((docs, LANES), I32),
            pltpu.SemaphoreType.DMA((docs * GRID,)),
            pltpu.SemaphoreType.DMA((2,)),
        ],
        compiler_params=params(24),
        cost_estimate=cost(10**9, 0, 2 * 10**6),
    )(where, all_codes, pinned(table), pinned(code_cache))
    got = lax.all_to_all(
        send.reshape(devices, DESC, 3 * LANES), ("doc", "seq"), split_axis=0, concat_axis=0, tiled=True
    )

    middle, queries = pl.pallas_call(
        window_kernel,
        name="window",
        out_shape=(
            jax.ShapeDtypeStruct((tok, width), BF),
            jax.ShapeDtypeStruct((GRID, message, LANES), BF),
        ),
        in_specs=[vmem()] * 4 + [hbm()] * 4,
        out_specs=(vmem(), vmem()),
        scratch_shapes=[
            pltpu.VMEM((width, 2 * width), BF),
            pltpu.VMEM((width, width), BF),
            pltpu.VMEM((width, width), BF),
            pltpu.VMEM((width, width), BF),
            pltpu.VMEM((tok + 2 * HALF_WIN, width), BF),
            pltpu.VMEM((tok + 2 * HALF_WIN, width), BF),
            pltpu.VMEM((tok + 2 * HALF_WIN, 2 * width), BF),
            pltpu.VMEM((tok, width), BF),
            pltpu.VMEM((tok, width), BF),
            pltpu.VMEM((tok // HALF_WIN, HALF_WIN, 3 * HALF_WIN), F32),
            pltpu.SemaphoreType.DMA((4,)),
        ],
        compiler_params=params(32),
        cost_estimate=cost(12 * 10**9, 5 * 10**6, 10**7),
    )(low, doc_hidden, high, token_ids, *map(pinned, (w_keyval, w_query, w_out, x_query)))

    lines = [[GRID * z + x for x in range(GRID)] for z in range(GRID)]

    def across(block):
        return lax.all_to_all(
            block, "seq", split_axis=0, concat_axis=0, axis_index_groups=lines, tiled=True
        )

    queries = across(queries)

    blocks = pl.pallas_call(
        compact_kernel,
        name="compact",
        out_shape=(jax.ShapeDtypeStruct((held, LANES), BF), jax.ShapeDtypeStruct((held, 2 * LANES), BF)),
        in_specs=[vmem()] * 2,
        out_specs=(vmem(),) * 2,
        compiler_params=params(24),
        cost_estimate=cost(10**9, 0, 2 * 10**6),
    )(slots, got.reshape(devices * DESC, 3 * LANES))

    def turns(block):
        parts = []
        for shift in range(1, GRID):
            pairs = [(i, (i + GRID * shift) % seq_count) for i in range(seq_count)]
            parts.append(lax.ppermute(block, "seq", pairs))
        return parts

    first, rest = [[block] + turns(block) for block in blocks]

    def cross(heads, parts, extra, outs):
        return pl.pallas_call(
            functools.partial(cross_kernel, heads, count),
            name="cross",
            out_shape=outs,
            in_specs=[smem()] + [vmem()] * 2 + [hbm()] * GRID + [vmem()] * len(extra),
            out_specs=jax.tree.map(lambda _: vmem(), outs),
            scratch_shapes=[
                pltpu.VMEM((len(heads), GRID * held, LANES), BF),
                pltpu.VMEM((len(heads), GRID * held, LANES), BF),
                pltpu.VMEM((2, tok, GRID * held), BF),
                pltpu.VMEM((8, GRID * held), F32),
                pltpu.SemaphoreType.DMA((len(heads) * GRID,)),
            ],
            compiler_params=params(24),
            cost_estimate=cost(len(heads) * 10**10, 5 * 10**6, 4 * 10**6),
        )(where, pos, queries, *parts, *extra)

    out, mass = cross(
        (0,),
        first,
        (),
        (jax.ShapeDtypeStruct((GRID, tok, LANES), BF), jax.ShapeDtypeStruct((8, GRID * held), F32)),
    )
    out, score = cross(
        (1, 2),
        rest,
        (mass, out),
        (jax.ShapeDtypeStruct((GRID, message, LANES), BF), jax.ShapeDtypeStruct((1, padded), F32)),
    )

    across_x = [[(i, GRID * (i // GRID) + (i + shift) % GRID) for i in range(seq_count)] for shift in range(1, GRID)]
    one, two, three = [lax.ppermute(score, "seq", pairs) for pairs in across_x]
    score = (score + two) + (one + three)
    one, two, three = turns(score)
    sums = (score + two) + (one + three)
    out = across(out)
    tokens = sums[:, count : count + 1] * (1.0 / GRID)
    cand_score = count * sums[:, :count] / (HEADS * tokens)

    refined = pl.pallas_call(
        final_kernel,
        name="final",
        out_shape=jax.ShapeDtypeStruct((tok, width), BF),
        in_specs=[vmem(), hbm(), hbm()],
        out_specs=vmem(),
        scratch_shapes=[
            pltpu.VMEM((GRID, message, LANES), BF),
            pltpu.VMEM((width, width), BF),
            pltpu.SemaphoreType.DMA((GRID + 1,)),
        ],
        compiler_params=params(16),
        cost_estimate=cost(10**9, 0, 4 * 10**6),
    )(middle, out, pinned(x_out))
    return (refined[None], cand_score)


def solution(mesh):
    return jax.shard_map(
        local,
        mesh=mesh,
        in_specs=(
            P("doc", "seq", None),
            P("doc", "seq"),
            P(),
            P(),
            P(),
            P(),
            P(),
            P("doc", None),
            P(),
            P(("doc", "seq"), None, None, None),
        ),
        out_specs=(P("doc", "seq", None), P("doc", None)),
        check_vma=False,
    )
```

```python
import functools
import math

import jax
import jax.numpy as jnp
from jax import lax
from jax.experimental import pallas as pl
from jax.experimental.pallas import tpu as pltpu
from jax.sharding import PartitionSpec as P

HEADS = 12
HALF_WIN = 256
DESC = 8
GRID = 4
LANES = 128
HALF = 64
SCALE = math.log2(math.e) / 8.0
BF = jnp.bfloat16
F32 = jnp.float32
I32 = jnp.int32


def iota(shape, dim):
    return lax.broadcasted_iota(I32, shape, dim)


def dot(a, b):
    return jnp.dot(a, b, preferred_element_type=F32)


def dot_t(a, b):
    return lax.dot_general(a, b, (((1,), (1,)), ((), ())), preferred_element_type=F32)


def params(mib):
    return pltpu.CompilerParams(vmem_limit_bytes=mib << 20)


def vmem():
    return pl.BlockSpec(memory_space=pltpu.VMEM)


def smem():
    return pl.BlockSpec(memory_space=pltpu.SMEM)


def pinned(array):
    return pltpu.with_memory_space_constraint(array, pltpu.HBM)


def hbm():
    return pl.BlockSpec(memory_space=pltpu.HBM)


def cost(flops, exps, bytes_):
    return pl.CostEstimate(flops=flops, transcendentals=exps, bytes_accessed=bytes_)


def planes_kernel(table_ref, planes_ref):
    missing = planes_ref.shape[1] - table_ref.shape[0]
    rows = jnp.concatenate([table_ref[...].astype(F32), jnp.zeros((missing, LANES), F32)], axis=0)
    wide = jnp.transpose(rows)
    high = jnp.floor(wide * (1.0 / 256.0))
    planes_ref[:LANES, :] = high.astype(BF)
    planes_ref[LANES:, :] = (wide - high * 256.0).astype(BF)


def look_up(code, table):
    n = code.shape[1]
    picks = (iota((table.shape[1], n), 0) == (code >> 7)).astype(F32).astype(BF)
    found = dot(table, picks)
    here = iota((LANES, n), 0) == (code & 127)
    value = jnp.where(here, found[:LANES] * 256.0 + found[LANES:], 0.0)
    return jnp.sum(value, axis=0, keepdims=True)


def ranks(row, count, code_dev, devices, upper):
    n = row.shape[1]
    owner = jnp.floor((row + 0.5) * (1.0 / code_dev))
    local = (row - owner * code_dev).astype(I32)
    owner = jnp.where(iota((1, n), 1) < count, owner.astype(I32), 2 * devices)
    sub = iota((devices, n), 0)
    mine = owner == sub
    starts = jnp.sum((owner < sub).astype(F32), axis=1, keepdims=True)
    before = dot(mine.astype(F32).astype(BF), upper)
    rank = jnp.sum(jnp.where(mine, starts + before, 0.0), axis=0, keepdims=True)
    return owner, local, rank.astype(I32)


def upper_ones(n):
    return (iota((n, n), 0) < iota((n, n), 1)).astype(F32).astype(BF)


def route_kernel(
    count, code_dev, devices, where_ref, codes_ref, planes_ref, cache_ref, send_hbm, slot_ref, pos_ref, send_ref, rows, line, picks, picked, sems, sem
):
    docs = codes_ref.shape[0]
    n = line.shape[1]
    upper = upper_ones(n)
    lane = iota((1, LANES), 1)
    line[...] = jnp.full(line.shape, -1, I32)
    for d in range(docs):
        line[d : d + 1, :count] = codes_ref[d]
    planes = planes_ref[...]
    doc = where_ref[2]
    owner_here = jnp.zeros((1, n), I32)
    rank_here = jnp.zeros((1, n), I32)
    for d in range(docs):
        row = look_up(line[d : d + 1, :], planes)
        owner, local, rank = ranks(row, count, code_dev, devices, upper)
        wanted = jnp.where(owner == where_ref[0], local + 1, 0).astype(F32)
        part = rank & (GRID - 1)
        found = jnp.zeros((1, LANES), F32)
        for z in range(GRID):
            one = jnp.sum(jnp.where(part == z, wanted, 0.0), axis=1, keepdims=True)
            found = found + jnp.where(lane == z, one, 0.0)
        picks[d : d + 1, :] = jnp.maximum(found.astype(I32) - 1, 0)
        owner_here = jnp.where(doc == d, owner, owner_here)
        rank_here = jnp.where(doc == d, rank, rank_here)
    to_scalars = pltpu.make_async_copy(picks, picked, sem.at[docs])
    to_scalars.start()
    to_scalars.wait()
    copies = []
    for d in range(docs):
        for z in range(GRID):
            k = d * GRID + z
            copies.append(pltpu.make_async_copy(cache_ref.at[picked[d, z]], rows.at[k], sems.at[k]))
            copies[-1].start()

    part = rank_here & (GRID - 1)
    spot = rank_here >> 2
    live = jnp.where(part == where_ref[1], (spot + 1).astype(F32), 0.0)
    mine = owner_here == iota((devices, n), 0)
    place = jnp.sum(jnp.where(mine, live, 0.0), axis=1, keepdims=True)
    width = devices * DESC
    spread = jnp.where(iota((devices, width), 0) == iota((devices, width), 1) // DESC, place, 0.0)
    spread = jnp.sum(spread, axis=0, keepdims=True).astype(I32)
    inside = iota((1, width), 1) & (DESC - 1)
    slot_ref[...] = jnp.where(spread > 0, (spread - 1) * DESC + inside, -1)
    pos_ref[...] = part * (count // GRID) + spot

    low = iota((GRID, DESC, LANES), 2) < HALF
    sent = []
    for d in range(docs):
        for copy in copies[d * GRID : (d + 1) * GRID]:
            copy.wait()
        block = pl.ds(d * GRID, GRID)
        for p in range(HEADS // 2):
            cols = pl.ds(p * LANES, LANES)
            keys = rows[block, 0, :, cols].astype(F32)
            values = rows[block, 1, :, cols].astype(F32)
            keys_turned = pltpu.roll(keys, HALF, 2)
            values_turned = pltpu.roll(values, HALF, 2)
            for s in range(2):
                head = 2 * p + s
                group, inner = head // 3, head % 3
                key_low = keys if s == 0 else keys_turned
                key_high = keys_turned if s == 0 else keys
                value_low = values if s == 0 else values_turned
                value_high = values_turned if s == 0 else values
                if inner == 1:
                    tile = jnp.where(low, value_low, key_high)
                else:
                    tile = jnp.where(low, key_low, value_high)
                send_ref[block, group, :, pl.ds(inner * LANES, LANES)] = tile.astype(BF)
        sent.append(pltpu.make_async_copy(send_ref.at[block], send_hbm.at[block], sem.at[d]))
        sent[-1].start()
    for copy in sent:
        copy.wait()


def compact_kernel(slot_ref, got_ref, first_ref, rest_ref):
    rows = first_ref.shape[0]
    pick = (iota((rows, got_ref.shape[0]), 0) == slot_ref[...]).astype(F32).astype(BF)
    packed = dot(pick, got_ref[...]).astype(BF)
    first_ref[...] = packed[:, :LANES]
    rest_ref[...] = packed[:, LANES:]


def layer_norm(values):
    centered = values - jnp.mean(values, axis=-1, keepdims=True)
    spread = jnp.mean(centered * centered, axis=-1, keepdims=True)
    return centered * lax.rsqrt(spread + 1e-05)


def halo_kernel(hidden_hbm, tokens_ref, wanted_ref, tail_ref, head_ref, asked_ref, sems):
    tok, width = hidden_hbm.shape
    win = HALF_WIN
    places = ((tail_ref, tok - win), (head_ref, 0))
    copies = []
    for k, (ref, start) in enumerate(places):
        copies.append(pltpu.make_async_copy(hidden_hbm.at[pl.ds(start, win), :], ref.at[pl.ds(0, win), :], sems.at[k]))
        copies[-1].start()
    for d in range(asked_ref.shape[0]):
        asked_ref[d] = wanted_ref[...]
    flags = (tokens_ref[...] != 0).astype(F32)
    for ref, start in places:
        row = jnp.concatenate([flags[:, start : start + win], jnp.zeros((1, width - win), F32)], axis=1)
        ref[win:, :] = jnp.broadcast_to(row, (8, width)).astype(BF)
    for copy in copies:
        copy.wait()


def window_kernel(
    low_ref, hidden_ref, high_ref, tokens_ref, wkv_hbm, wq_hbm, wo_hbm, xq_hbm, middle_ref, query_ref, wkv_ref, wq_ref, wo_ref, xq_ref, normed, keys, values, queries, context, bias, sems
):
    tok, width = hidden_ref.shape
    win = HALF_WIN
    span = 3 * win
    total = tok + 2 * win
    pairs = width // LANES
    pieces = ((wkv_hbm, wkv_ref), (wq_hbm, wq_ref), (wo_hbm, wo_ref), (xq_hbm, xq_ref))
    copies = [pltpu.make_async_copy(src, dst, sems.at[k]) for k, (src, dst) in enumerate(pieces)]
    for copy in copies:
        copy.start()
    normed[:win, :] = layer_norm(low_ref[:win, :].astype(F32)).astype(BF)
    normed[win : win + tok, :] = layer_norm(hidden_ref[...].astype(F32)).astype(BF)
    normed[win + tok :, :] = layer_norm(high_ref[:win, :].astype(F32)).astype(BF)
    own_flags = (tokens_ref[...] != 0).astype(F32)
    flags = jnp.concatenate(
        [low_ref[win : win + 1, :win].astype(F32), own_flags, high_ref[win : win + 1, :win].astype(F32)], axis=1
    )
    gap = iota((win, span), 1) - iota((win, span), 0)
    near = (gap >= 0) & (gap <= 2 * win)
    for b in range(tok // win):
        usable = (flags[:, b * win : b * win + span] > 0.0) | (gap == win)
        bias[b] = jnp.where(near & usable, 0.0, -1e30)
    for p in range(pairs):
        values[:, (2 * p + 1) * LANES : (2 * p + 2) * LANES] = jnp.ones((total, LANES), BF)
    wide = 2 * LANES
    copies[0].wait()
    for c in range(0, width, wide):
        keys[:, c : c + wide] = dot(normed[...], wkv_ref[:, c : c + wide]).astype(BF)
    for c in range(0, width, wide):
        part = dot(normed[...], wkv_ref[:, width + c : width + c + wide]).astype(BF).astype(F32) * 2.0**-8
        part = part.astype(BF)
        values[:, 2 * c : 2 * c + LANES] = part[:, :LANES]
        values[:, 2 * c + wide : 2 * c + wide + LANES] = part[:, LANES:]
    copies[1].wait()
    for c in range(0, width, wide):
        queries[:, c : c + wide] = (dot(normed[win : win + tok, :], wq_ref[:, c : c + wide]) * SCALE).astype(BF)
    low = iota((win, LANES), 1) < HALF
    for b in range(tok // win):
        for p in range(pairs):
            cols = slice(p * LANES, (p + 1) * LANES)
            query = queries[b * win : (b + 1) * win, cols]
            key = keys[b * win : b * win + span, cols]
            value = values[b * win : b * win + span, 2 * p * LANES : (2 * p + 2) * LANES]
            nothing = jnp.zeros_like(query)
            both = jnp.concatenate([jnp.where(low, query, nothing), jnp.where(low, nothing, query)], axis=0)
            scores = dot_t(both, key).reshape(2, win, span) + bias[b][None]
            out = dot(jnp.exp2(scores).astype(BF).reshape(2 * win, span), value)
            out = out[:, :LANES] / out[:, LANES:] * 256.0
            context[b * win : (b + 1) * win, cols] = jnp.where(low, out[:win], out[win:]).astype(BF)
    copies[2].wait()
    copies[3].wait()
    thirds_of = [[] for _ in range(GRID)]
    for b in range(tok // win):
        rows = slice(b * win, (b + 1) * win)
        mixed = hidden_ref[rows, :].astype(F32) + dot(context[rows, :], wo_ref[...])
        mixed = mixed.astype(BF)
        middle_ref[rows, :] = mixed
        cross = dot(layer_norm(mixed.astype(F32)).astype(BF), xq_ref[...]) * SCALE
        tiles = [cross[:, p * LANES : (p + 1) * LANES] for p in range(pairs)]
        turned = [pltpu.roll(t, HALF, 1) for t in tiles]

        def placed(head, upper):
            return (turned if (head % 2 == 1) != upper else tiles)[head // 2]

        for g in range(GRID):
            first = jnp.where(low, placed(3 * g, False), placed(3 * g + 1, True))
            query_ref[g, rows, :] = first.astype(BF)
            thirds_of[g].append(placed(3 * g + 2, b == 1))
    line = iota((16, LANES), 0)
    marks = jnp.zeros((16, LANES), F32)
    for k in range(tok // LANES):
        marks = jnp.where(line == k, own_flags[:, k * LANES : (k + 1) * LANES], marks)
    for g in range(GRID):
        query_ref[g, tok : tok + win, :] = jnp.where(low, thirds_of[g][0], thirds_of[g][1]).astype(BF)
        query_ref[g, tok + win :, :] = marks.astype(BF)


def cross_kernel(heads, count, where_ref, pos_ref, query_ref, *refs):
    kv_refs, refs = refs[:GRID], refs[GRID:]
    last = 2 in heads
    if last:
        before_ref, earlier_ref, out_ref, score_ref, keys, values, expds, total = refs
    else:
        out_ref, mass_ref, keys, values, expds, total = refs
    held = kv_refs[0].shape[0]
    tok = expds.shape[1]
    groups = query_ref.shape[0]
    half = tok // 2
    small = iota((tok, LANES), 1) < HALF
    low = iota((half, LANES), 1) < HALF
    if last:
        total[...] = before_ref[...]
    else:
        total[...] = jnp.zeros_like(total)
    lower = iota((held, LANES), 1) < HALF
    for k, inner in enumerate(heads):
        for c in range(GRID):
            rows = pl.ds(c * held, held)
            block = kv_refs[c][:, k * LANES : (k + 1) * LANES]
            keys[k, rows, :] = block
            scaled = block.astype(F32) * 2.0**-4
            values[k, rows, :] = jnp.where(lower == (inner == 1), scaled, 1.0).astype(BF)

    def one(g, k, slot):
        inner = heads[k]
        value_low = inner == 1
        if inner == 2:
            packed = query_ref[g, tok : tok + half, :]
            turned = pltpu.roll(packed.astype(F32), HALF, 1).astype(BF)
            query = jnp.concatenate([packed, turned], axis=0)
        else:
            query = query_ref[g, :tok, :]
        query = jnp.where(small != value_low, query, jnp.zeros_like(query))
        acc = jnp.zeros((tok, LANES), F32)
        for c in range(0, GRID * held, 512):
            expd = jnp.exp2(dot_t(query, keys[k, c : c + 512, :])).astype(BF)
            expds[slot, :, c : c + 512] = expd
            acc = acc + dot(expd, values[k, c : c + 512, :])
        at = LANES - 1 if value_low else 0
        inverse = 1.0 / acc[:, at : at + 1]
        out = (acc * inverse) * 16.0
        share = jnp.where(iota((tok, 1), 0).astype(F32) < tokens_of(g), inverse, 0.0)
        for c in range(0, GRID * held, 512):
            mass = jnp.sum(expds[slot, :, c : c + 512].astype(F32) * share, axis=0, keepdims=True)
            total[:1, c : c + 512] = total[:1, c : c + 512] + mass
        return out

    def tokens_of(g):
        marks = query_ref[g, tok + half :, :].astype(F32)
        return jnp.sum(jnp.sum(marks, axis=0, keepdims=True), axis=1, keepdims=True)

    if not last:

        def body(i, carry):
            for u in range(2):
                out_ref[2 * i + u] = one(2 * i + u, 0, u).astype(BF)
            return carry

        lax.fori_loop(0, groups // 2, body, 0)
        mass_ref[...] = total[...]
        return

    def body(g, carry):
        out_ref[g, :tok, :] = jnp.where(small, one(g, 0, 0), earlier_ref[g].astype(F32)).astype(BF)
        out = one(g, 1, 1)
        out_ref[g, tok : tok + half, :] = jnp.where(low, pltpu.roll(out[:half], HALF, 1), out[half:]).astype(BF)
        return carry

    lax.fori_loop(0, groups, body, 0)
    padded = pos_ref.shape[1]
    score = jnp.zeros((8, padded), F32)
    line = iota((8, held), 0)
    for c in range(GRID):
        mass = jnp.broadcast_to(total[:1, c * held : (c + 1) * held], (8, held))
        first, second, third = thirds(mass)
        parts = jnp.where(line == 0, first, jnp.where(line == 1, second, jnp.where(line == 2, third, 0.0)))
        origin = (where_ref[1] + GRID - c) & (GRID - 1)
        at = iota((held, padded), 0) // DESC + origin * (count // GRID)
        score = score + dot(parts.astype(BF), (at == pos_ref[...]).astype(F32).astype(BF))
    score = jnp.sum(score, axis=0, keepdims=True)
    tokens = tokens_of(0)
    for g in range(1, groups):
        tokens = tokens + tokens_of(g)
    score = jnp.where(iota((1, padded), 1) == count, tokens, score)
    score_ref[...] = score


def thirds(value):
    first = value.astype(BF).astype(F32)
    second = (value - first).astype(BF).astype(F32)
    return first, second, value - first - second


def final_kernel(middle_ref, got_ref, weight_ref, out_ref):
    tok = middle_ref.shape[0]
    groups = got_ref.shape[0]
    half = tok // 2
    size = 3 * HALF
    low = iota((half, LANES), 1) < HALF
    acc = middle_ref[...].astype(F32)
    for g in range(groups):
        at = g * size
        heads = [weight_ref[at + k * HALF : at + (k + 1) * HALF, :] for k in (1, 0, 2, 2)]
        packed = got_ref[g, tok : tok + half, :]
        nothing = jnp.zeros_like(packed)
        third = jnp.concatenate([jnp.where(low, packed, nothing), jnp.where(low, nothing, packed)], axis=0)
        lhs = jnp.concatenate([got_ref[g, :tok, :], third], axis=1)
        acc = acc + dot(lhs, jnp.concatenate(heads, axis=0))
    out_ref[...] = acc.astype(BF)


def local(hidden, token_ids, w_query, w_keyval, w_out, x_query, x_out, shortlist, code_row, code_cache):
    doc_hidden = hidden[0]
    tok, width = doc_hidden.shape
    seq_count = lax.axis_size("seq")
    docs = lax.axis_size("doc")
    devices = docs * seq_count
    seq_index = lax.axis_index("seq")
    own = lax.axis_index("doc") * seq_count + seq_index
    where = jnp.stack([own, seq_index // GRID, lax.axis_index("doc")]).astype(I32)
    count = shortlist.shape[1]
    padded = -(-count // LANES) * LANES
    code_dev = code_cache.shape[0]
    held = count // GRID * DESC
    message = tok + tok // 2 + 16
    table = code_row.reshape(-1, LANES)

    forward = [(i, i + 1) for i in range(seq_count - 1)]
    backward = [(t, s) for s, t in forward]
    tail, head, asked = pl.pallas_call(
        halo_kernel,
        name="halo",
        out_shape=(jax.ShapeDtypeStruct((HALF_WIN + 8, width), BF),) * 2
        + (jax.ShapeDtypeStruct((docs, 1, count), I32),),
        in_specs=[hbm(), vmem(), vmem()],
        out_specs=(vmem(),) * 3,
        scratch_shapes=[pltpu.SemaphoreType.DMA((2,))],
        compiler_params=params(16),
        cost_estimate=cost(10**5, 0, 16 * 10**5),
    )(pinned(doc_hidden), token_ids, shortlist)
    all_codes = lax.all_to_all(asked, "doc", split_axis=0, concat_axis=0, tiled=True)
    table, head = lax.optimization_barrier((table, head))
    planes = pl.pallas_call(
        planes_kernel,
        name="planes",
        out_shape=jax.ShapeDtypeStruct((2 * LANES, -(-table.shape[0] // LANES) * LANES), BF),
        in_specs=[vmem()],
        out_specs=vmem(),
        compiler_params=params(16),
        cost_estimate=cost(10**5, 0, 2 * 10**5),
    )(table)
    low = lax.ppermute(tail, "seq", forward)
    high = lax.ppermute(head, "seq", backward)

    send, slots, pos = pl.pallas_call(
        functools.partial(route_kernel, count, code_dev, devices),
        name="route",
        out_shape=(
            jax.ShapeDtypeStruct((docs * GRID, GRID, DESC, 3 * LANES), BF),
            jax.ShapeDtypeStruct((1, devices * DESC), I32),
            jax.ShapeDtypeStruct((1, padded), I32),
        ),
        in_specs=[smem(), vmem(), vmem(), hbm()],
        out_specs=(hbm(), vmem(), vmem()),
        scratch_shapes=[
            pltpu.VMEM((docs * GRID, GRID, DESC, 3 * LANES), BF),
            pltpu.VMEM((docs * GRID, 2, DESC, width), BF),
            pltpu.VMEM((docs, padded), I32),
            pltpu.VMEM((docs, LANES), I32),
            pltpu.SMEM((docs, LANES), I32),
            pltpu.SemaphoreType.DMA((docs * GRID,)),
            pltpu.SemaphoreType.DMA((docs + 1,)),
        ],
        compiler_params=params(24),
        cost_estimate=cost(10**9, 0, 2 * 10**6),
    )(where, all_codes, planes, pinned(code_cache))
    got = lax.all_to_all(
        send.reshape(devices, DESC, 3 * LANES), ("doc", "seq"), split_axis=0, concat_axis=0, tiled=True
    )

    middle, queries = pl.pallas_call(
        window_kernel,
        name="window",
        out_shape=(
            jax.ShapeDtypeStruct((tok, width), BF),
            jax.ShapeDtypeStruct((GRID, message, LANES), BF),
        ),
        in_specs=[vmem()] * 4 + [hbm()] * 4,
        out_specs=(vmem(), vmem()),
        scratch_shapes=[
            pltpu.VMEM((width, 2 * width), BF),
            pltpu.VMEM((width, width), BF),
            pltpu.VMEM((width, width), BF),
            pltpu.VMEM((width, width), BF),
            pltpu.VMEM((tok + 2 * HALF_WIN, width), BF),
            pltpu.VMEM((tok + 2 * HALF_WIN, width), BF),
            pltpu.VMEM((tok + 2 * HALF_WIN, 2 * width), BF),
            pltpu.VMEM((tok, width), BF),
            pltpu.VMEM((tok, width), BF),
            pltpu.VMEM((tok // HALF_WIN, HALF_WIN, 3 * HALF_WIN), F32),
            pltpu.SemaphoreType.DMA((4,)),
        ],
        compiler_params=params(32),
        cost_estimate=cost(12 * 10**9, 5 * 10**6, 10**7),
    )(low, doc_hidden, high, token_ids, *map(pinned, (w_keyval, w_query, w_out, x_query)))

    lines = [[GRID * z + x for x in range(GRID)] for z in range(GRID)]

    def across(block):
        return lax.all_to_all(
            block, "seq", split_axis=0, concat_axis=0, axis_index_groups=lines, tiled=True
        )

    queries = across(queries)

    blocks = pl.pallas_call(
        compact_kernel,
        name="compact",
        out_shape=(jax.ShapeDtypeStruct((held, LANES), BF), jax.ShapeDtypeStruct((held, 2 * LANES), BF)),
        in_specs=[vmem()] * 2,
        out_specs=(vmem(),) * 2,
        compiler_params=params(24),
        cost_estimate=cost(10**9, 0, 2 * 10**6),
    )(slots, got.reshape(devices * DESC, 3 * LANES))

    def turns(block):
        parts = []
        for shift in range(1, GRID):
            pairs = [(i, (i + GRID * shift) % seq_count) for i in range(seq_count)]
            parts.append(lax.ppermute(block, "seq", pairs))
        return parts

    first, rest = [[block] + turns(block) for block in blocks]

    def cross(heads, parts, extra, outs):
        return pl.pallas_call(
            functools.partial(cross_kernel, heads, count),
            name="cross",
            out_shape=outs,
            in_specs=[smem()] + [vmem()] * (2 + GRID + len(extra)),
            out_specs=jax.tree.map(lambda _: vmem(), outs),
            scratch_shapes=[
                pltpu.VMEM((len(heads), GRID * held, LANES), BF),
                pltpu.VMEM((len(heads), GRID * held, LANES), BF),
                pltpu.VMEM((2, tok, GRID * held), BF),
                pltpu.VMEM((8, GRID * held), F32),
            ],
            compiler_params=params(24),
            cost_estimate=cost(len(heads) * 10**10, 5 * 10**6, 4 * 10**6),
        )(where, pos, queries, *parts, *extra)

    out, mass = cross(
        (0,),
        first,
        (),
        (jax.ShapeDtypeStruct((GRID, tok, LANES), BF), jax.ShapeDtypeStruct((8, GRID * held), F32)),
    )
    out, score = cross(
        (1, 2),
        rest,
        (mass, out),
        (jax.ShapeDtypeStruct((GRID, message, LANES), BF), jax.ShapeDtypeStruct((1, padded), F32)),
    )

    across_x = [[(i, GRID * (i // GRID) + (i + shift) % GRID) for i in range(seq_count)] for shift in range(1, GRID)]
    one, two, three = [lax.ppermute(score, "seq", pairs) for pairs in across_x]
    score = (score + two) + (one + three)
    one, two, three = turns(score)

    refined = pl.pallas_call(
        final_kernel,
        name="final",
        out_shape=jax.ShapeDtypeStruct((tok, width), BF),
        in_specs=[vmem()] * 3,
        out_specs=vmem(),
        compiler_params=params(16),
        cost_estimate=cost(10**9, 0, 4 * 10**6),
    )(middle, across(out), x_out)
    one, two, three, refined = lax.optimization_barrier((one, two, three, refined))
    sums = (score + two) + (one + three)
    tokens = sums[:, count : count + 1] * (1.0 / GRID)
    cand_score = count * sums[:, :count] / (HEADS * tokens)
    return (refined[None], cand_score)


def solution(mesh):
    return jax.shard_map(
        local,
        mesh=mesh,
        in_specs=(
            P("doc", "seq", None),
            P("doc", "seq"),
            P(),
            P(),
            P(),
            P(),
            P(),
            P("doc", None),
            P(),
            P(("doc", "seq"), None, None, None),
        ),
        out_specs=(P("doc", "seq", None), P("doc", None)),
        check_vma=False,
    )
```

```python
import functools
import math

import jax
import jax.numpy as jnp
from jax import lax
from jax.experimental import pallas as pl
from jax.experimental.pallas import tpu as pltpu
from jax.sharding import PartitionSpec as P

HEADS = 12
HALF_WIN = 256
DESC = 8
GRID = 4
LANES = 128
HALF = 64
SCALE = math.log2(math.e) / 8.0
BF = jnp.bfloat16
F32 = jnp.float32
I32 = jnp.int32


def iota(shape, dim):
    return lax.broadcasted_iota(I32, shape, dim)


def dot(a, b):
    return jnp.dot(a, b, preferred_element_type=F32)


def dot_t(a, b):
    return lax.dot_general(a, b, (((1,), (1,)), ((), ())), preferred_element_type=F32)


def params(mib):
    return pltpu.CompilerParams(vmem_limit_bytes=mib << 20)


def vmem():
    return pl.BlockSpec(memory_space=pltpu.VMEM)


def smem():
    return pl.BlockSpec(memory_space=pltpu.SMEM)


def pinned(array):
    return pltpu.with_memory_space_constraint(array, pltpu.HBM)


def hbm():
    return pl.BlockSpec(memory_space=pltpu.HBM)


def cost(flops, exps, bytes_):
    return pl.CostEstimate(flops=flops, transcendentals=exps, bytes_accessed=bytes_)


def planes_kernel(table_ref, planes_ref):
    missing = planes_ref.shape[1] - table_ref.shape[0]
    rows = jnp.concatenate([table_ref[...].astype(F32), jnp.zeros((missing, LANES), F32)], axis=0)
    wide = jnp.transpose(rows)
    high = jnp.floor(wide * (1.0 / 256.0))
    planes_ref[:LANES, :] = high.astype(BF)
    planes_ref[LANES:, :] = (wide - high * 256.0).astype(BF)


def look_up(code, table):
    n = code.shape[1]
    picks = (iota((table.shape[1], n), 0) == (code >> 7)).astype(F32).astype(BF)
    found = dot(table, picks)
    here = iota((LANES, n), 0) == (code & 127)
    value = jnp.where(here, found[:LANES] * 256.0 + found[LANES:], 0.0)
    return jnp.sum(value, axis=0, keepdims=True)


def ranks(row, count, code_dev, devices, upper):
    n = row.shape[1]
    owner = jnp.floor((row + 0.5) * (1.0 / code_dev))
    local = (row - owner * code_dev).astype(I32)
    owner = jnp.where(iota((1, n), 1) < count, owner.astype(I32), 2 * devices)
    sub = iota((devices, n), 0)
    mine = owner == sub
    starts = jnp.sum((owner < sub).astype(F32), axis=1, keepdims=True)
    before = dot(mine.astype(F32).astype(BF), upper)
    rank = jnp.sum(jnp.where(mine, starts + before, 0.0), axis=0, keepdims=True)
    return owner, local, rank.astype(I32)


def upper_ones(n):
    return (iota((n, n), 0) < iota((n, n), 1)).astype(F32).astype(BF)


def route_kernel(
    count, code_dev, devices, where_ref, codes_ref, planes_ref, cache_ref, send_hbm, slot_ref, pos_ref, send_ref, rows, line, picks, picked, sems, sem
):
    docs = codes_ref.shape[0]
    n = line.shape[1]
    upper = upper_ones(n)
    lane = iota((1, LANES), 1)
    line[...] = jnp.full(line.shape, -1, I32)
    for d in range(docs):
        line[d : d + 1, :count] = codes_ref[d]
    planes = planes_ref[...]
    doc = where_ref[2]
    owner_here = jnp.zeros((1, n), I32)
    rank_here = jnp.zeros((1, n), I32)
    for d in range(docs):
        row = look_up(line[d : d + 1, :], planes)
        owner, local, rank = ranks(row, count, code_dev, devices, upper)
        wanted = jnp.where(owner == where_ref[0], local + 1, 0).astype(F32)
        part = rank & (GRID - 1)
        found = jnp.zeros((1, LANES), F32)
        for z in range(GRID):
            one = jnp.sum(jnp.where(part == z, wanted, 0.0), axis=1, keepdims=True)
            found = found + jnp.where(lane == z, one, 0.0)
        picks[d : d + 1, :] = jnp.maximum(found.astype(I32) - 1, 0)
        owner_here = jnp.where(doc == d, owner, owner_here)
        rank_here = jnp.where(doc == d, rank, rank_here)
    to_scalars = pltpu.make_async_copy(picks, picked, sem.at[docs])
    to_scalars.start()
    to_scalars.wait()
    copies = []
    for d in range(docs):
        for z in range(GRID):
            k = d * GRID + z
            copies.append(pltpu.make_async_copy(cache_ref.at[picked[d, z]], rows.at[k], sems.at[k]))
            copies[-1].start()

    part = rank_here & (GRID - 1)
    spot = rank_here >> 2
    live = jnp.where(part == where_ref[1], (spot + 1).astype(F32), 0.0)
    mine = owner_here == iota((devices, n), 0)
    place = jnp.sum(jnp.where(mine, live, 0.0), axis=1, keepdims=True)
    width = devices * DESC
    spread = jnp.where(iota((devices, width), 0) == iota((devices, width), 1) // DESC, place, 0.0)
    spread = jnp.sum(spread, axis=0, keepdims=True).astype(I32)
    inside = iota((1, width), 1) & (DESC - 1)
    slot_ref[...] = jnp.where(spread > 0, (spread - 1) * DESC + inside, -1)
    pos_ref[...] = part * (count // GRID) + spot

    low = iota((GRID, DESC, LANES), 2) < HALF
    sent = []
    for d in range(docs):
        for copy in copies[d * GRID : (d + 1) * GRID]:
            copy.wait()
        block = pl.ds(d * GRID, GRID)
        for p in range(HEADS // 2):
            cols = pl.ds(p * LANES, LANES)
            keys = rows[block, 0, :, cols].astype(F32)
            values = rows[block, 1, :, cols].astype(F32)
            keys_turned = pltpu.roll(keys, HALF, 2)
            values_turned = pltpu.roll(values, HALF, 2)
            for s in range(2):
                head = 2 * p + s
                group, inner = head // 3, head % 3
                key_low = keys if s == 0 else keys_turned
                key_high = keys_turned if s == 0 else keys
                value_low = values if s == 0 else values_turned
                value_high = values_turned if s == 0 else values
                if inner == 1:
                    tile = jnp.where(low, value_low, key_high)
                else:
                    tile = jnp.where(low, key_low, value_high)
                send_ref[block, group, :, pl.ds(inner * LANES, LANES)] = tile.astype(BF)
        sent.append(pltpu.make_async_copy(send_ref.at[block], send_hbm.at[block], sem.at[d]))
        sent[-1].start()
    for copy in sent:
        copy.wait()


def compact_kernel(slot_ref, got_ref, first_ref, rest_ref):
    rows = first_ref.shape[0]
    pick = (iota((rows, got_ref.shape[0]), 0) == slot_ref[...]).astype(F32).astype(BF)
    packed = dot(pick, got_ref[...]).astype(BF)
    first_ref[...] = packed[:, :LANES]
    rest_ref[...] = packed[:, LANES:]


def layer_norm(values):
    centered = values - jnp.mean(values, axis=-1, keepdims=True)
    spread = jnp.mean(centered * centered, axis=-1, keepdims=True)
    return centered * lax.rsqrt(spread + 1e-05)


def halo_kernel(hidden_hbm, tokens_hbm, wanted_hbm, tail_ref, head_ref, asked_ref, tokens_ref, wanted_ref, sems):
    tok, width = hidden_hbm.shape
    win = HALF_WIN
    places = ((tail_ref, tok - win), (head_ref, 0))
    copies = []
    for k, (ref, start) in enumerate(places):
        copies.append(pltpu.make_async_copy(hidden_hbm.at[pl.ds(start, win), :], ref.at[pl.ds(0, win), :], sems.at[k]))
        copies[-1].start()
    small = [
        pltpu.make_async_copy(wanted_hbm, wanted_ref, sems.at[2]),
        pltpu.make_async_copy(tokens_hbm, tokens_ref, sems.at[3]),
    ]
    for copy in small:
        copy.start()
    small[0].wait()
    for d in range(asked_ref.shape[0]):
        asked_ref[d] = wanted_ref[...]
    small[1].wait()
    flags = (tokens_ref[...] != 0).astype(F32)
    for ref, start in places:
        row = jnp.concatenate([flags[:, start : start + win], jnp.zeros((1, width - win), F32)], axis=1)
        ref[win:, :] = jnp.broadcast_to(row, (8, width)).astype(BF)
    for copy in copies:
        copy.wait()


def window_kernel(
    low_ref, hidden_ref, high_ref, tokens_ref, wkv_hbm, wq_hbm, wo_hbm, xq_hbm, middle_ref, query_ref, wkv_ref, wq_ref, wo_ref, xq_ref, normed, keys, values, queries, context, bias, sems
):
    tok, width = hidden_ref.shape
    win = HALF_WIN
    span = 3 * win
    total = tok + 2 * win
    pairs = width // LANES
    pieces = ((wkv_hbm, wkv_ref), (wq_hbm, wq_ref), (wo_hbm, wo_ref), (xq_hbm, xq_ref))
    copies = [pltpu.make_async_copy(src, dst, sems.at[k]) for k, (src, dst) in enumerate(pieces)]
    for copy in copies:
        copy.start()
    normed[:win, :] = layer_norm(low_ref[:win, :].astype(F32)).astype(BF)
    normed[win : win + tok, :] = layer_norm(hidden_ref[...].astype(F32)).astype(BF)
    normed[win + tok :, :] = layer_norm(high_ref[:win, :].astype(F32)).astype(BF)
    own_flags = (tokens_ref[...] != 0).astype(F32)
    flags = jnp.concatenate(
        [low_ref[win : win + 1, :win].astype(F32), own_flags, high_ref[win : win + 1, :win].astype(F32)], axis=1
    )
    gap = iota((win, span), 1) - iota((win, span), 0)
    near = (gap >= 0) & (gap <= 2 * win)
    for b in range(tok // win):
        usable = (flags[:, b * win : b * win + span] > 0.0) | (gap == win)
        bias[b] = jnp.where(near & usable, 0.0, -1e30)
    for p in range(pairs):
        values[:, (2 * p + 1) * LANES : (2 * p + 2) * LANES] = jnp.ones((total, LANES), BF)
    wide = 2 * LANES
    copies[0].wait()
    for c in range(0, width, wide):
        keys[:, c : c + wide] = dot(normed[...], wkv_ref[:, c : c + wide]).astype(BF)
    for c in range(0, width, wide):
        part = dot(normed[...], wkv_ref[:, width + c : width + c + wide]).astype(BF).astype(F32) * 2.0**-8
        part = part.astype(BF)
        values[:, 2 * c : 2 * c + LANES] = part[:, :LANES]
        values[:, 2 * c + wide : 2 * c + wide + LANES] = part[:, LANES:]
    copies[1].wait()
    for c in range(0, width, wide):
        queries[:, c : c + wide] = (dot(normed[win : win + tok, :], wq_ref[:, c : c + wide]) * SCALE).astype(BF)
    low = iota((win, LANES), 1) < HALF
    for b in range(tok // win):
        for p in range(pairs):
            cols = slice(p * LANES, (p + 1) * LANES)
            query = queries[b * win : (b + 1) * win, cols]
            key = keys[b * win : b * win + span, cols]
            value = values[b * win : b * win + span, 2 * p * LANES : (2 * p + 2) * LANES]
            nothing = jnp.zeros_like(query)
            both = jnp.concatenate([jnp.where(low, query, nothing), jnp.where(low, nothing, query)], axis=0)
            scores = dot_t(both, key).reshape(2, win, span) + bias[b][None]
            out = dot(jnp.exp2(scores).astype(BF).reshape(2 * win, span), value)
            out = out[:, :LANES] / out[:, LANES:] * 256.0
            context[b * win : (b + 1) * win, cols] = jnp.where(low, out[:win], out[win:]).astype(BF)
    copies[2].wait()
    copies[3].wait()
    thirds_of = [[] for _ in range(GRID)]
    for b in range(tok // win):
        rows = slice(b * win, (b + 1) * win)
        mixed = hidden_ref[rows, :].astype(F32) + dot(context[rows, :], wo_ref[...])
        mixed = mixed.astype(BF)
        middle_ref[rows, :] = mixed
        cross = dot(layer_norm(mixed.astype(F32)).astype(BF), xq_ref[...]) * SCALE
        tiles = [cross[:, p * LANES : (p + 1) * LANES] for p in range(pairs)]
        turned = [pltpu.roll(t, HALF, 1) for t in tiles]

        def placed(head, upper):
            return (turned if (head % 2 == 1) != upper else tiles)[head // 2]

        for g in range(GRID):
            first = jnp.where(low, placed(3 * g, False), placed(3 * g + 1, True))
            query_ref[g, rows, :] = first.astype(BF)
            thirds_of[g].append(placed(3 * g + 2, b == 1))
    line = iota((16, LANES), 0)
    marks = jnp.zeros((16, LANES), F32)
    for k in range(tok // LANES):
        marks = jnp.where(line == k, own_flags[:, k * LANES : (k + 1) * LANES], marks)
    for g in range(GRID):
        query_ref[g, tok : tok + win, :] = jnp.where(low, thirds_of[g][0], thirds_of[g][1]).astype(BF)
        query_ref[g, tok + win :, :] = marks.astype(BF)


def cross_kernel(heads, count, where_ref, pos_ref, query_ref, *refs):
    kv_refs, refs = refs[:GRID], refs[GRID:]
    last = 2 in heads
    if last:
        before_ref, earlier_ref, out_ref, score_ref, keys, values, expds, total = refs
    else:
        out_ref, mass_ref, keys, values, expds, total = refs
    held = kv_refs[0].shape[0]
    tok = expds.shape[1]
    groups = query_ref.shape[0]
    half = tok // 2
    small = iota((tok, LANES), 1) < HALF
    low = iota((half, LANES), 1) < HALF
    if last:
        total[...] = before_ref[...]
    else:
        total[...] = jnp.zeros_like(total)
    lower = iota((held, LANES), 1) < HALF
    for k, inner in enumerate(heads):
        for c in range(GRID):
            rows = pl.ds(c * held, held)
            block = kv_refs[c][:, k * LANES : (k + 1) * LANES]
            keys[k, rows, :] = block
            scaled = block.astype(F32) * 2.0**-4
            values[k, rows, :] = jnp.where(lower == (inner == 1), scaled, 1.0).astype(BF)

    def one(g, k, slot):
        inner = heads[k]
        value_low = inner == 1
        if inner == 2:
            packed = query_ref[g, tok : tok + half, :]
            turned = pltpu.roll(packed.astype(F32), HALF, 1).astype(BF)
            query = jnp.concatenate([packed, turned], axis=0)
        else:
            query = query_ref[g, :tok, :]
        query = jnp.where(small != value_low, query, jnp.zeros_like(query))
        acc = jnp.zeros((tok, LANES), F32)
        for c in range(0, GRID * held, 512):
            expd = jnp.exp2(dot_t(query, keys[k, c : c + 512, :])).astype(BF)
            expds[slot, :, c : c + 512] = expd
            acc = acc + dot(expd, values[k, c : c + 512, :])
        at = LANES - 1 if value_low else 0
        inverse = 1.0 / acc[:, at : at + 1]
        out = (acc * inverse) * 16.0
        share = jnp.where(iota((tok, 1), 0).astype(F32) < tokens_of(g), inverse, 0.0)
        for c in range(0, GRID * held, 512):
            mass = jnp.sum(expds[slot, :, c : c + 512].astype(F32) * share, axis=0, keepdims=True)
            total[:1, c : c + 512] = total[:1, c : c + 512] + mass
        return out

    def tokens_of(g):
        marks = query_ref[g, tok + half :, :].astype(F32)
        return jnp.sum(jnp.sum(marks, axis=0, keepdims=True), axis=1, keepdims=True)

    if not last:

        def body(i, carry):
            for u in range(2):
                out_ref[2 * i + u] = one(2 * i + u, 0, u).astype(BF)
            return carry

        lax.fori_loop(0, groups // 2, body, 0)
        mass_ref[...] = total[...]
        return

    def body(g, carry):
        out_ref[g, :tok, :] = jnp.where(small, one(g, 0, 0), earlier_ref[g].astype(F32)).astype(BF)
        out = one(g, 1, 1)
        out_ref[g, tok : tok + half, :] = jnp.where(low, pltpu.roll(out[:half], HALF, 1), out[half:]).astype(BF)
        return carry

    lax.fori_loop(0, groups, body, 0)
    padded = pos_ref.shape[1]
    score = jnp.zeros((8, padded), F32)
    line = iota((8, held), 0)
    for c in range(GRID):
        mass = jnp.broadcast_to(total[:1, c * held : (c + 1) * held], (8, held))
        first, second, third = thirds(mass)
        parts = jnp.where(line == 0, first, jnp.where(line == 1, second, jnp.where(line == 2, third, 0.0)))
        origin = (where_ref[1] + GRID - c) & (GRID - 1)
        at = iota((held, padded), 0) // DESC + origin * (count // GRID)
        score = score + dot(parts.astype(BF), (at == pos_ref[...]).astype(F32).astype(BF))
    score = jnp.sum(score, axis=0, keepdims=True)
    tokens = tokens_of(0)
    for g in range(1, groups):
        tokens = tokens + tokens_of(g)
    score = jnp.where(iota((1, padded), 1) == count, tokens, score)
    score_ref[...] = score


def thirds(value):
    first = value.astype(BF).astype(F32)
    second = (value - first).astype(BF).astype(F32)
    return first, second, value - first - second


def final_kernel(middle_ref, got_ref, weight_ref, out_ref):
    tok = middle_ref.shape[0]
    groups = got_ref.shape[0]
    half = tok // 2
    size = 3 * HALF
    low = iota((half, LANES), 1) < HALF
    acc = middle_ref[...].astype(F32)
    for g in range(groups):
        at = g * size
        heads = [weight_ref[at + k * HALF : at + (k + 1) * HALF, :] for k in (1, 0, 2, 2)]
        packed = got_ref[g, tok : tok + half, :]
        nothing = jnp.zeros_like(packed)
        third = jnp.concatenate([jnp.where(low, packed, nothing), jnp.where(low, nothing, packed)], axis=0)
        lhs = jnp.concatenate([got_ref[g, :tok, :], third], axis=1)
        acc = acc + dot(lhs, jnp.concatenate(heads, axis=0))
    out_ref[...] = acc.astype(BF)


def local(hidden, token_ids, w_query, w_keyval, w_out, x_query, x_out, shortlist, code_row, code_cache):
    doc_hidden = hidden[0]
    tok, width = doc_hidden.shape
    seq_count = lax.axis_size("seq")
    docs = lax.axis_size("doc")
    devices = docs * seq_count
    seq_index = lax.axis_index("seq")
    own = lax.axis_index("doc") * seq_count + seq_index
    where = jnp.stack([own, seq_index // GRID, lax.axis_index("doc")]).astype(I32)
    count = shortlist.shape[1]
    padded = -(-count // LANES) * LANES
    code_dev = code_cache.shape[0]
    held = count // GRID * DESC
    message = tok + tok // 2 + 16
    table = code_row.reshape(-1, LANES)

    forward = [(i, i + 1) for i in range(seq_count - 1)]
    backward = [(t, s) for s, t in forward]
    tail, head, asked = pl.pallas_call(
        halo_kernel,
        name="halo",
        out_shape=(jax.ShapeDtypeStruct((HALF_WIN + 8, width), BF),) * 2
        + (jax.ShapeDtypeStruct((docs, 1, count), I32),),
        in_specs=[hbm()] * 3,
        out_specs=(vmem(),) * 3,
        scratch_shapes=[pltpu.VMEM((1, tok), I32), pltpu.VMEM((1, count), I32), pltpu.SemaphoreType.DMA((4,))],
        compiler_params=params(16),
        cost_estimate=cost(10**5, 0, 16 * 10**5),
    )(*map(pinned, (doc_hidden, token_ids, shortlist)))
    all_codes = lax.all_to_all(asked, "doc", split_axis=0, concat_axis=0, tiled=True)
    table, head = lax.optimization_barrier((table, head))
    planes = pl.pallas_call(
        planes_kernel,
        name="planes",
        out_shape=jax.ShapeDtypeStruct((2 * LANES, -(-table.shape[0] // LANES) * LANES), BF),
        in_specs=[vmem()],
        out_specs=vmem(),
        compiler_params=params(16),
        cost_estimate=cost(10**5, 0, 2 * 10**5),
    )(table)
    low = lax.ppermute(tail, "seq", forward)
    high = lax.ppermute(head, "seq", backward)

    send, slots, pos = pl.pallas_call(
        functools.partial(route_kernel, count, code_dev, devices),
        name="route",
        out_shape=(
            jax.ShapeDtypeStruct((docs * GRID, GRID, DESC, 3 * LANES), BF),
            jax.ShapeDtypeStruct((1, devices * DESC), I32),
            jax.ShapeDtypeStruct((1, padded), I32),
        ),
        in_specs=[smem(), vmem(), vmem(), hbm()],
        out_specs=(hbm(), vmem(), vmem()),
        scratch_shapes=[
            pltpu.VMEM((docs * GRID, GRID, DESC, 3 * LANES), BF),
            pltpu.VMEM((docs * GRID, 2, DESC, width), BF),
            pltpu.VMEM((docs, padded), I32),
            pltpu.VMEM((docs, LANES), I32),
            pltpu.SMEM((docs, LANES), I32),
            pltpu.SemaphoreType.DMA((docs * GRID,)),
            pltpu.SemaphoreType.DMA((docs + 1,)),
        ],
        compiler_params=params(24),
        cost_estimate=cost(10**9, 0, 2 * 10**6),
    )(where, all_codes, planes, pinned(code_cache))
    got = lax.all_to_all(
        send.reshape(devices, DESC, 3 * LANES), ("doc", "seq"), split_axis=0, concat_axis=0, tiled=True
    )

    middle, queries = pl.pallas_call(
        window_kernel,
        name="window",
        out_shape=(
            jax.ShapeDtypeStruct((tok, width), BF),
            jax.ShapeDtypeStruct((GRID, message, LANES), BF),
        ),
        in_specs=[vmem()] * 4 + [hbm()] * 4,
        out_specs=(vmem(), vmem()),
        scratch_shapes=[
            pltpu.VMEM((width, 2 * width), BF),
            pltpu.VMEM((width, width), BF),
            pltpu.VMEM((width, width), BF),
            pltpu.VMEM((width, width), BF),
            pltpu.VMEM((tok + 2 * HALF_WIN, width), BF),
            pltpu.VMEM((tok + 2 * HALF_WIN, width), BF),
            pltpu.VMEM((tok + 2 * HALF_WIN, 2 * width), BF),
            pltpu.VMEM((tok, width), BF),
            pltpu.VMEM((tok, width), BF),
            pltpu.VMEM((tok // HALF_WIN, HALF_WIN, 3 * HALF_WIN), F32),
            pltpu.SemaphoreType.DMA((4,)),
        ],
        compiler_params=params(26),
        cost_estimate=cost(12 * 10**9, 5 * 10**6, 10**7),
    )(low, doc_hidden, high, token_ids, *map(pinned, (w_keyval, w_query, w_out, x_query)))

    lines = [[GRID * z + x for x in range(GRID)] for z in range(GRID)]

    def across(block):
        return lax.all_to_all(
            block, "seq", split_axis=0, concat_axis=0, axis_index_groups=lines, tiled=True
        )

    queries = across(queries)

    blocks = pl.pallas_call(
        compact_kernel,
        name="compact",
        out_shape=(jax.ShapeDtypeStruct((held, LANES), BF), jax.ShapeDtypeStruct((held, 2 * LANES), BF)),
        in_specs=[vmem()] * 2,
        out_specs=(vmem(),) * 2,
        compiler_params=params(24),
        cost_estimate=cost(10**9, 0, 2 * 10**6),
    )(slots, got.reshape(devices * DESC, 3 * LANES))

    def turns(block):
        parts = []
        for shift in range(1, GRID):
            pairs = [(i, (i + GRID * shift) % seq_count) for i in range(seq_count)]
            parts.append(lax.ppermute(block, "seq", pairs))
        return parts

    block, rest_block = blocks
    *arrived, rest_block = lax.optimization_barrier((*turns(block), rest_block))
    first, rest = [block] + arrived, [rest_block] + turns(rest_block)

    def cross(heads, parts, extra, outs):
        return pl.pallas_call(
            functools.partial(cross_kernel, heads, count),
            name="cross",
            out_shape=outs,
            in_specs=[smem()] + [vmem()] * (2 + GRID + len(extra)),
            out_specs=jax.tree.map(lambda _: vmem(), outs),
            scratch_shapes=[
                pltpu.VMEM((len(heads), GRID * held, LANES), BF),
                pltpu.VMEM((len(heads), GRID * held, LANES), BF),
                pltpu.VMEM((2, tok, GRID * held), BF),
                pltpu.VMEM((8, GRID * held), F32),
            ],
            compiler_params=params(18),
            cost_estimate=cost(len(heads) * 10**10, 5 * 10**6, 4 * 10**6),
        )(where, pos, queries, *parts, *extra)

    out, mass = cross(
        (0,),
        first,
        (),
        (jax.ShapeDtypeStruct((GRID, tok, LANES), BF), jax.ShapeDtypeStruct((8, GRID * held), F32)),
    )
    out, score = cross(
        (1, 2),
        rest,
        (mass, out),
        (jax.ShapeDtypeStruct((GRID, message, LANES), BF), jax.ShapeDtypeStruct((1, padded), F32)),
    )

    across_x = [[(i, GRID * (i // GRID) + (i + shift) % GRID) for i in range(seq_count)] for shift in range(1, GRID)]
    one, two, three = [lax.ppermute(score, "seq", pairs) for pairs in across_x]
    score = (score + two) + (one + three)
    one, two, three = turns(score)
    sums = (score + two) + (one + three)
    tokens = sums[:, count : count + 1] * (1.0 / GRID)
    cand_score = count * sums[:, :count] / (HEADS * tokens)
    out = across(out)

    refined = pl.pallas_call(
        final_kernel,
        name="final",
        out_shape=jax.ShapeDtypeStruct((tok, width), BF),
        in_specs=[vmem()] * 3,
        out_specs=vmem(),
        compiler_params=params(16),
        cost_estimate=cost(10**9, 0, 4 * 10**6),
    )(middle, out, x_out)
    return (refined[None], cand_score)


def solution(mesh):
    return jax.shard_map(
        local,
        mesh=mesh,
        in_specs=(
            P("doc", "seq", None),
            P("doc", "seq"),
            P(),
            P(),
            P(),
            P(),
            P(),
            P("doc", None),
            P(),
            P(("doc", "seq"), None, None, None),
        ),
        out_specs=(P("doc", "seq", None), P("doc", None)),
        check_vma=False,
    )
```

```python
import functools
import math

import jax
import jax.numpy as jnp
from jax import lax
from jax.experimental import pallas as pl
from jax.experimental.pallas import tpu as pltpu
from jax.sharding import PartitionSpec as P

HEADS = 12
HALF_WIN = 256
DESC = 8
GRID = 4
LANES = 128
HALF = 64
SCALE = math.log2(math.e) / 8.0
BF = jnp.bfloat16
F32 = jnp.float32
I32 = jnp.int32


def iota(shape, dim):
    return lax.broadcasted_iota(I32, shape, dim)


def dot(a, b):
    return jnp.dot(a, b, preferred_element_type=F32)


def dot_t(a, b):
    return lax.dot_general(a, b, (((1,), (1,)), ((), ())), preferred_element_type=F32)


def params(mib):
    return pltpu.CompilerParams(vmem_limit_bytes=mib << 20)


def vmem():
    return pl.BlockSpec(memory_space=pltpu.VMEM)


def smem():
    return pl.BlockSpec(memory_space=pltpu.SMEM)


def pinned(array):
    return pltpu.with_memory_space_constraint(array, pltpu.HBM)


def hbm():
    return pl.BlockSpec(memory_space=pltpu.HBM)


def cost(flops, exps, bytes_):
    return pl.CostEstimate(flops=flops, transcendentals=exps, bytes_accessed=bytes_)


def planes_kernel(table_ref, planes_ref):
    missing = planes_ref.shape[1] - table_ref.shape[0]
    rows = jnp.concatenate([table_ref[...].astype(F32), jnp.zeros((missing, LANES), F32)], axis=0)
    wide = jnp.transpose(rows)
    high = jnp.floor(wide * (1.0 / 256.0))
    planes_ref[:LANES, :] = high.astype(BF)
    planes_ref[LANES:, :] = (wide - high * 256.0).astype(BF)


def look_up(code, table):
    n = code.shape[1]
    picks = (iota((table.shape[1], n), 0) == (code >> 7)).astype(F32).astype(BF)
    found = dot(table, picks)
    here = iota((LANES, n), 0) == (code & 127)
    value = jnp.where(here, found[:LANES] * 256.0 + found[LANES:], 0.0)
    return jnp.sum(value, axis=0, keepdims=True)


def ranks(row, count, code_dev, devices, upper):
    n = row.shape[1]
    owner = jnp.floor((row + 0.5) * (1.0 / code_dev))
    local = (row - owner * code_dev).astype(I32)
    owner = jnp.where(iota((1, n), 1) < count, owner.astype(I32), 2 * devices)
    sub = iota((devices, n), 0)
    mine = owner == sub
    starts = jnp.sum((owner < sub).astype(F32), axis=1, keepdims=True)
    before = dot(mine.astype(F32).astype(BF), upper)
    rank = jnp.sum(jnp.where(mine, starts + before, 0.0), axis=0, keepdims=True)
    return owner, local, rank.astype(I32)


def upper_ones(n):
    return (iota((n, n), 0) < iota((n, n), 1)).astype(F32).astype(BF)


def route_kernel(
    count, code_dev, devices, where_ref, codes_ref, planes_ref, cache_ref, send_hbm, slot_ref, pos_ref, send_ref, rows, line, picks, picked, sems, sem
):
    docs = codes_ref.shape[0]
    n = line.shape[1]
    upper = upper_ones(n)
    lane = iota((1, LANES), 1)
    line[...] = jnp.full(line.shape, -1, I32)
    for d in range(docs):
        line[d : d + 1, :count] = codes_ref[d]
    planes = planes_ref[...]
    doc = where_ref[2]
    owner_here = jnp.zeros((1, n), I32)
    rank_here = jnp.zeros((1, n), I32)
    for d in range(docs):
        row = look_up(line[d : d + 1, :], planes)
        owner, local, rank = ranks(row, count, code_dev, devices, upper)
        wanted = jnp.where(owner == where_ref[0], local + 1, 0).astype(F32)
        part = rank & (GRID - 1)
        found = jnp.zeros((1, LANES), F32)
        for z in range(GRID):
            one = jnp.sum(jnp.where(part == z, wanted, 0.0), axis=1, keepdims=True)
            found = found + jnp.where(lane == z, one, 0.0)
        picks[d : d + 1, :] = jnp.maximum(found.astype(I32) - 1, 0)
        owner_here = jnp.where(doc == d, owner, owner_here)
        rank_here = jnp.where(doc == d, rank, rank_here)
    to_scalars = pltpu.make_async_copy(picks, picked, sem.at[docs])
    to_scalars.start()
    to_scalars.wait()
    copies = []
    for d in range(docs):
        for z in range(GRID):
            k = d * GRID + z
            copies.append(pltpu.make_async_copy(cache_ref.at[picked[d, z]], rows.at[k], sems.at[k]))
            copies[-1].start()

    part = rank_here & (GRID - 1)
    spot = rank_here >> 2
    live = jnp.where(part == where_ref[1], (spot + 1).astype(F32), 0.0)
    mine = owner_here == iota((devices, n), 0)
    place = jnp.sum(jnp.where(mine, live, 0.0), axis=1, keepdims=True)
    width = devices * DESC
    spread = jnp.where(iota((devices, width), 0) == iota((devices, width), 1) // DESC, place, 0.0)
    spread = jnp.sum(spread, axis=0, keepdims=True).astype(I32)
    inside = iota((1, width), 1) & (DESC - 1)
    slot_ref[...] = jnp.where(spread > 0, (spread - 1) * DESC + inside, -1)
    pos_ref[...] = part * (count // GRID) + spot

    low = iota((GRID, DESC, LANES), 2) < HALF
    sent = []
    for d in range(docs):
        for copy in copies[d * GRID : (d + 1) * GRID]:
            copy.wait()
        block = pl.ds(d * GRID, GRID)
        for p in range(HEADS // 2):
            cols = pl.ds(p * LANES, LANES)
            keys = rows[block, 0, :, cols].astype(F32)
            values = rows[block, 1, :, cols].astype(F32)
            keys_turned = pltpu.roll(keys, HALF, 2)
            values_turned = pltpu.roll(values, HALF, 2)
            for s in range(2):
                head = 2 * p + s
                group, inner = head // 3, head % 3
                key_low = keys if s == 0 else keys_turned
                key_high = keys_turned if s == 0 else keys
                value_low = values if s == 0 else values_turned
                value_high = values_turned if s == 0 else values
                if inner == 1:
                    tile = jnp.where(low, value_low, key_high)
                else:
                    tile = jnp.where(low, key_low, value_high)
                send_ref[block, group, :, pl.ds(inner * LANES, LANES)] = tile.astype(BF)
        sent.append(pltpu.make_async_copy(send_ref.at[block], send_hbm.at[block], sem.at[d]))
        sent[-1].start()
    for copy in sent:
        copy.wait()


def compact_kernel(slot_ref, got_ref, first_ref, rest_ref):
    rows = first_ref.shape[0]
    pick = (iota((rows, got_ref.shape[0]), 0) == slot_ref[...]).astype(F32).astype(BF)
    packed = dot(pick, got_ref[...]).astype(BF)
    first_ref[...] = packed[:, :LANES]
    rest_ref[...] = packed[:, LANES:]


def layer_norm(values):
    centered = values - jnp.mean(values, axis=-1, keepdims=True)
    spread = jnp.mean(centered * centered, axis=-1, keepdims=True)
    return centered * lax.rsqrt(spread + 1e-05)


def halo_kernel(hidden_hbm, tokens_hbm, wanted_hbm, tail_ref, head_ref, asked_ref, tokens_ref, wanted_ref, sems):
    tok, width = hidden_hbm.shape
    win = HALF_WIN
    places = ((tail_ref, tok - win), (head_ref, 0))
    copies = []
    for k, (ref, start) in enumerate(places):
        copies.append(pltpu.make_async_copy(hidden_hbm.at[pl.ds(start, win), :], ref.at[pl.ds(0, win), :], sems.at[k]))
        copies[-1].start()
    small = [
        pltpu.make_async_copy(wanted_hbm, wanted_ref, sems.at[2]),
        pltpu.make_async_copy(tokens_hbm, tokens_ref, sems.at[3]),
    ]
    for copy in small:
        copy.start()
    small[0].wait()
    for d in range(asked_ref.shape[0]):
        asked_ref[d] = wanted_ref[...]
    small[1].wait()
    flags = (tokens_ref[...] != 0).astype(F32)
    for ref, start in places:
        row = jnp.concatenate([flags[:, start : start + win], jnp.zeros((1, width - win), F32)], axis=1)
        ref[win:, :] = jnp.broadcast_to(row, (8, width)).astype(BF)
    for copy in copies:
        copy.wait()


def window_kernel(
    low_ref, hidden_ref, high_ref, tokens_ref, wkv_hbm, wq_hbm, wo_hbm, xq_hbm, middle_ref, query_ref, wkv_ref, wq_ref, wo_ref, xq_ref, normed, keys, values, queries, context, bias, sems
):
    tok, width = hidden_ref.shape
    win = HALF_WIN
    span = 3 * win
    total = tok + 2 * win
    pairs = width // LANES
    pieces = ((wkv_hbm, wkv_ref), (wq_hbm, wq_ref), (wo_hbm, wo_ref), (xq_hbm, xq_ref))
    copies = [pltpu.make_async_copy(src, dst, sems.at[k]) for k, (src, dst) in enumerate(pieces)]
    for copy in copies:
        copy.start()
    normed[:win, :] = layer_norm(low_ref[:win, :].astype(F32)).astype(BF)
    normed[win : win + tok, :] = layer_norm(hidden_ref[...].astype(F32)).astype(BF)
    normed[win + tok :, :] = layer_norm(high_ref[:win, :].astype(F32)).astype(BF)
    own_flags = (tokens_ref[...] != 0).astype(F32)
    flags = jnp.concatenate(
        [low_ref[win : win + 1, :win].astype(F32), own_flags, high_ref[win : win + 1, :win].astype(F32)], axis=1
    )
    gap = iota((win, span), 1) - iota((win, span), 0)
    near = (gap >= 0) & (gap <= 2 * win)
    for b in range(tok // win):
        usable = (flags[:, b * win : b * win + span] > 0.0) | (gap == win)
        bias[b] = jnp.where(near & usable, 0.0, -1e30)
    for p in range(pairs):
        values[:, (2 * p + 1) * LANES : (2 * p + 2) * LANES] = jnp.ones((total, LANES), BF)
    wide = 2 * LANES
    copies[0].wait()
    for c in range(0, width, wide):
        keys[:, c : c + wide] = dot(normed[...], wkv_ref[:, c : c + wide]).astype(BF)
    for c in range(0, width, wide):
        part = dot(normed[...], wkv_ref[:, width + c : width + c + wide]).astype(BF).astype(F32) * 2.0**-8
        part = part.astype(BF)
        values[:, 2 * c : 2 * c + LANES] = part[:, :LANES]
        values[:, 2 * c + wide : 2 * c + wide + LANES] = part[:, LANES:]
    copies[1].wait()
    for c in range(0, width, wide):
        queries[:, c : c + wide] = (dot(normed[win : win + tok, :], wq_ref[:, c : c + wide]) * SCALE).astype(BF)
    low = iota((win, LANES), 1) < HALF
    for b in range(tok // win):
        for p in range(pairs):
            cols = slice(p * LANES, (p + 1) * LANES)
            query = queries[b * win : (b + 1) * win, cols]
            key = keys[b * win : b * win + span, cols]
            value = values[b * win : b * win + span, 2 * p * LANES : (2 * p + 2) * LANES]
            nothing = jnp.zeros_like(query)
            both = jnp.concatenate([jnp.where(low, query, nothing), jnp.where(low, nothing, query)], axis=0)
            scores = dot_t(both, key).reshape(2, win, span) + bias[b][None]
            out = dot(jnp.exp2(scores).astype(BF).reshape(2 * win, span), value)
            out = out[:, :LANES] / out[:, LANES:] * 256.0
            context[b * win : (b + 1) * win, cols] = jnp.where(low, out[:win], out[win:]).astype(BF)
    copies[2].wait()
    copies[3].wait()
    thirds_of = [[] for _ in range(GRID)]
    for b in range(tok // win):
        rows = slice(b * win, (b + 1) * win)
        mixed = hidden_ref[rows, :].astype(F32) + dot(context[rows, :], wo_ref[...])
        mixed = mixed.astype(BF)
        middle_ref[rows, :] = mixed
        cross = dot(layer_norm(mixed.astype(F32)).astype(BF), xq_ref[...]) * SCALE
        tiles = [cross[:, p * LANES : (p + 1) * LANES] for p in range(pairs)]
        turned = [pltpu.roll(t, HALF, 1) for t in tiles]

        def placed(head, upper):
            return (turned if (head % 2 == 1) != upper else tiles)[head // 2]

        for g in range(GRID):
            first = jnp.where(low, placed(3 * g, False), placed(3 * g + 1, True))
            query_ref[g, rows, :] = first.astype(BF)
            thirds_of[g].append(placed(3 * g + 2, b == 1))
    line = iota((16, LANES), 0)
    marks = jnp.zeros((16, LANES), F32)
    for k in range(tok // LANES):
        marks = jnp.where(line == k, own_flags[:, k * LANES : (k + 1) * LANES], marks)
    for g in range(GRID):
        query_ref[g, tok : tok + win, :] = jnp.where(low, thirds_of[g][0], thirds_of[g][1]).astype(BF)
        query_ref[g, tok + win :, :] = marks.astype(BF)


def cross_kernel(heads, count, where_ref, pos_ref, query_ref, *refs):
    last = 2 in heads
    pieces = 1 if last else GRID
    kv_refs, refs = refs[:pieces], refs[pieces:]
    if last:
        before_ref, earlier_hbm, out_ref, score_ref, keys, values, expds, total, earlier_ref, sems = refs
    else:
        out_ref, mass_ref, keys, values, expds, total = refs
    held = keys.shape[1] // GRID
    tok = expds.shape[1]
    groups = query_ref.shape[0]
    half = tok // 2
    copies = []
    if last:
        for k in range(len(heads)):
            for c in range(GRID):
                origin = (where_ref[1] + GRID - c) & (GRID - 1)
                rows = pl.ds(pl.multiple_of(origin * held, held), held)
                source = kv_refs[0].at[rows, pl.ds(k * LANES, LANES)]
                target = keys.at[k, pl.ds(c * held, held), :]
                copies.append(pltpu.make_async_copy(source, target, sems.at[k * GRID + c]))
        copies.append(pltpu.make_async_copy(earlier_hbm, earlier_ref, sems.at[len(copies)]))
    for copy in copies:
        copy.start()
    small = iota((tok, LANES), 1) < HALF
    low = iota((half, LANES), 1) < HALF
    if last:
        total[...] = before_ref[...]
    else:
        total[...] = jnp.zeros_like(total)
    lower = iota((held, LANES), 1) < HALF
    for k, inner in enumerate(heads):
        for c in range(GRID):
            rows = pl.ds(c * held, held)
            if last:
                copies[k * GRID + c].wait()
                block = keys[k, rows, :]
            else:
                block = kv_refs[c][...]
                keys[k, rows, :] = block
            scaled = block.astype(F32) * 2.0**-4
            values[k, rows, :] = jnp.where(lower == (inner == 1), scaled, 1.0).astype(BF)

    def one(g, k, slot):
        inner = heads[k]
        value_low = inner == 1
        if inner == 2:
            packed = query_ref[g, tok : tok + half, :]
            turned = pltpu.roll(packed.astype(F32), HALF, 1).astype(BF)
            query = jnp.concatenate([packed, turned], axis=0)
        else:
            query = query_ref[g, :tok, :]
        query = jnp.where(small != value_low, query, jnp.zeros_like(query))
        acc = jnp.zeros((tok, LANES), F32)
        for c in range(0, GRID * held, 512):
            expd = jnp.exp2(dot_t(query, keys[k, c : c + 512, :])).astype(BF)
            expds[slot, :, c : c + 512] = expd
            acc = acc + dot(expd, values[k, c : c + 512, :])
        at = LANES - 1 if value_low else 0
        inverse = 1.0 / acc[:, at : at + 1]
        out = (acc * inverse) * 16.0
        share = jnp.where(iota((tok, 1), 0).astype(F32) < tokens_of(g), inverse, 0.0)
        for c in range(0, GRID * held, 512):
            mass = jnp.sum(expds[slot, :, c : c + 512].astype(F32) * share, axis=0, keepdims=True)
            total[:1, c : c + 512] = total[:1, c : c + 512] + mass
        return out

    def tokens_of(g):
        marks = query_ref[g, tok + half :, :].astype(F32)
        return jnp.sum(jnp.sum(marks, axis=0, keepdims=True), axis=1, keepdims=True)

    if not last:

        def body(i, carry):
            for u in range(2):
                out_ref[2 * i + u] = one(2 * i + u, 0, u).astype(BF)
            return carry

        lax.fori_loop(0, groups // 2, body, 0)
        mass_ref[...] = total[...]
        return

    copies[-1].wait()

    def body(g, carry):
        out_ref[g, :tok, :] = jnp.where(small, one(g, 0, 0), earlier_ref[g].astype(F32)).astype(BF)
        out = one(g, 1, 1)
        out_ref[g, tok : tok + half, :] = jnp.where(low, pltpu.roll(out[:half], HALF, 1), out[half:]).astype(BF)
        return carry

    lax.fori_loop(0, groups, body, 0)
    padded = pos_ref.shape[1]
    score = jnp.zeros((8, padded), F32)
    line = iota((8, held), 0)
    for c in range(GRID):
        mass = jnp.broadcast_to(total[:1, c * held : (c + 1) * held], (8, held))
        first, second, third = thirds(mass)
        parts = jnp.where(line == 0, first, jnp.where(line == 1, second, jnp.where(line == 2, third, 0.0)))
        origin = (where_ref[1] + GRID - c) & (GRID - 1)
        at = iota((held, padded), 0) // DESC + origin * (count // GRID)
        score = score + dot(parts.astype(BF), (at == pos_ref[...]).astype(F32).astype(BF))
    score = jnp.sum(score, axis=0, keepdims=True)
    tokens = tokens_of(0)
    for g in range(1, groups):
        tokens = tokens + tokens_of(g)
    score = jnp.where(iota((1, padded), 1) == count, tokens, score)
    score_ref[...] = score


def thirds(value):
    first = value.astype(BF).astype(F32)
    second = (value - first).astype(BF).astype(F32)
    return first, second, value - first - second


def final_kernel(middle_ref, got_ref, weight_ref, out_ref):
    tok = middle_ref.shape[0]
    groups = got_ref.shape[0]
    half = tok // 2
    size = 3 * HALF
    low = iota((half, LANES), 1) < HALF
    acc = middle_ref[...].astype(F32)
    for g in range(groups):
        at = g * size
        heads = [weight_ref[at + k * HALF : at + (k + 1) * HALF, :] for k in (1, 0, 2, 2)]
        packed = got_ref[g, tok : tok + half, :]
        nothing = jnp.zeros_like(packed)
        third = jnp.concatenate([jnp.where(low, packed, nothing), jnp.where(low, nothing, packed)], axis=0)
        lhs = jnp.concatenate([got_ref[g, :tok, :], third], axis=1)
        acc = acc + dot(lhs, jnp.concatenate(heads, axis=0))
    out_ref[...] = acc.astype(BF)


def local(hidden, token_ids, w_query, w_keyval, w_out, x_query, x_out, shortlist, code_row, code_cache):
    doc_hidden = hidden[0]
    tok, width = doc_hidden.shape
    seq_count = lax.axis_size("seq")
    docs = lax.axis_size("doc")
    devices = docs * seq_count
    seq_index = lax.axis_index("seq")
    own = lax.axis_index("doc") * seq_count + seq_index
    where = jnp.stack([own, seq_index // GRID, lax.axis_index("doc")]).astype(I32)
    count = shortlist.shape[1]
    padded = -(-count // LANES) * LANES
    code_dev = code_cache.shape[0]
    held = count // GRID * DESC
    message = tok + tok // 2 + 16
    table = code_row.reshape(-1, LANES)

    forward = [(i, i + 1) for i in range(seq_count - 1)]
    backward = [(t, s) for s, t in forward]
    tail, head, asked = pl.pallas_call(
        halo_kernel,
        name="halo",
        out_shape=(jax.ShapeDtypeStruct((HALF_WIN + 8, width), BF),) * 2
        + (jax.ShapeDtypeStruct((docs, 1, count), I32),),
        in_specs=[hbm()] * 3,
        out_specs=(vmem(),) * 3,
        scratch_shapes=[pltpu.VMEM((1, tok), I32), pltpu.VMEM((1, count), I32), pltpu.SemaphoreType.DMA((4,))],
        compiler_params=params(16),
        cost_estimate=cost(10**5, 0, 16 * 10**5),
    )(*map(pinned, (doc_hidden, token_ids, shortlist)))
    all_codes = lax.all_to_all(asked, "doc", split_axis=0, concat_axis=0, tiled=True)
    table, head = lax.optimization_barrier((table, head))
    planes = pl.pallas_call(
        planes_kernel,
        name="planes",
        out_shape=jax.ShapeDtypeStruct((2 * LANES, -(-table.shape[0] // LANES) * LANES), BF),
        in_specs=[vmem()],
        out_specs=vmem(),
        compiler_params=params(16),
        cost_estimate=cost(10**5, 0, 2 * 10**5),
    )(table)
    low = lax.ppermute(tail, "seq", forward)
    high = lax.ppermute(head, "seq", backward)

    send, slots, pos = pl.pallas_call(
        functools.partial(route_kernel, count, code_dev, devices),
        name="route",
        out_shape=(
            jax.ShapeDtypeStruct((docs * GRID, GRID, DESC, 3 * LANES), BF),
            jax.ShapeDtypeStruct((1, devices * DESC), I32),
            jax.ShapeDtypeStruct((1, padded), I32),
        ),
        in_specs=[smem(), vmem(), vmem(), hbm()],
        out_specs=(hbm(), vmem(), vmem()),
        scratch_shapes=[
            pltpu.VMEM((docs * GRID, GRID, DESC, 3 * LANES), BF),
            pltpu.VMEM((docs * GRID, 2, DESC, width), BF),
            pltpu.VMEM((docs, padded), I32),
            pltpu.VMEM((docs, LANES), I32),
            pltpu.SMEM((docs, LANES), I32),
            pltpu.SemaphoreType.DMA((docs * GRID,)),
            pltpu.SemaphoreType.DMA((docs + 1,)),
        ],
        compiler_params=params(24),
        cost_estimate=cost(10**9, 0, 2 * 10**6),
    )(where, all_codes, planes, pinned(code_cache))
    got = lax.all_to_all(
        send.reshape(devices, DESC, 3 * LANES), ("doc", "seq"), split_axis=0, concat_axis=0, tiled=True
    )

    middle, queries = pl.pallas_call(
        window_kernel,
        name="window",
        out_shape=(
            jax.ShapeDtypeStruct((tok, width), BF),
            jax.ShapeDtypeStruct((GRID, message, LANES), BF),
        ),
        in_specs=[vmem()] * 4 + [hbm()] * 4,
        out_specs=(vmem(), vmem()),
        scratch_shapes=[
            pltpu.VMEM((width, 2 * width), BF),
            pltpu.VMEM((width, width), BF),
            pltpu.VMEM((width, width), BF),
            pltpu.VMEM((width, width), BF),
            pltpu.VMEM((tok + 2 * HALF_WIN, width), BF),
            pltpu.VMEM((tok + 2 * HALF_WIN, width), BF),
            pltpu.VMEM((tok + 2 * HALF_WIN, 2 * width), BF),
            pltpu.VMEM((tok, width), BF),
            pltpu.VMEM((tok, width), BF),
            pltpu.VMEM((tok // HALF_WIN, HALF_WIN, 3 * HALF_WIN), F32),
            pltpu.SemaphoreType.DMA((4,)),
        ],
        compiler_params=params(26),
        cost_estimate=cost(12 * 10**9, 5 * 10**6, 10**7),
    )(low, doc_hidden, high, token_ids, *map(pinned, (w_keyval, w_query, w_out, x_query)))

    lines = [[GRID * z + x for x in range(GRID)] for z in range(GRID)]

    def across(block):
        return lax.all_to_all(
            block, "seq", split_axis=0, concat_axis=0, axis_index_groups=lines, tiled=True
        )

    blocks = pl.pallas_call(
        compact_kernel,
        name="compact",
        out_shape=(jax.ShapeDtypeStruct((held, LANES), BF), jax.ShapeDtypeStruct((held, 2 * LANES), BF)),
        in_specs=[vmem()] * 2,
        out_specs=(vmem(),) * 2,
        compiler_params=params(24),
        cost_estimate=cost(10**9, 0, 2 * 10**6),
    )(slots, got.reshape(devices * DESC, 3 * LANES))

    def turns(block):
        parts = []
        for shift in range(1, GRID):
            pairs = [(i, (i + GRID * shift) % seq_count) for i in range(seq_count)]
            parts.append(lax.ppermute(block, "seq", pairs))
        return parts

    *blocks, queries = lax.optimization_barrier((*blocks, queries))
    block, rest_block = blocks
    queries = across(queries)
    first = [block] + turns(block)
    columns = [[GRID * z + x for z in range(GRID)] for x in range(GRID)]
    rest = lax.all_gather(rest_block, "seq", axis=0, axis_index_groups=columns, tiled=True)

    def cross(heads, parts, extra, outs):
        last = 2 in heads
        scratch = [
            pltpu.VMEM((len(heads), GRID * held, LANES), BF),
            pltpu.VMEM((len(heads), GRID * held, LANES), BF),
            pltpu.VMEM((2, tok, GRID * held), BF),
            pltpu.VMEM((8, GRID * held), F32),
        ]
        kv_specs = [vmem()] * len(parts)
        if last:
            scratch += [pltpu.VMEM((GRID, tok, LANES), BF), pltpu.SemaphoreType.DMA((len(heads) * GRID + 1,))]
            kv_specs = [hbm(), vmem(), hbm()]
        return pl.pallas_call(
            functools.partial(cross_kernel, heads, count),
            name="cross",
            out_shape=outs,
            in_specs=[smem(), vmem(), vmem(), *kv_specs],
            out_specs=jax.tree.map(lambda _: vmem(), outs),
            scratch_shapes=scratch,
            compiler_params=params(18),
            cost_estimate=cost(len(heads) * 10**10, 5 * 10**6, 4 * 10**6),
        )(where, pos, queries, *parts, *extra)

    out, mass = cross(
        (0,),
        first,
        (),
        (jax.ShapeDtypeStruct((GRID, tok, LANES), BF), jax.ShapeDtypeStruct((8, GRID * held), F32)),
    )
    out, score = cross(
        (1, 2),
        [pinned(rest)],
        (mass, pinned(out)),
        (jax.ShapeDtypeStruct((GRID, message, LANES), BF), jax.ShapeDtypeStruct((1, padded), F32)),
    )

    across_x = [[(i, GRID * (i // GRID) + (i + shift) % GRID) for i in range(seq_count)] for shift in range(1, GRID)]
    one, two, three = [lax.ppermute(score, "seq", pairs) for pairs in across_x]
    score = (score + two) + (one + three)
    one, two, three = turns(score)
    sums = (score + two) + (one + three)
    tokens = sums[:, count : count + 1] * (1.0 / GRID)
    cand_score = count * sums[:, :count] / (HEADS * tokens)
    out = across(out)

    refined = pl.pallas_call(
        final_kernel,
        name="final",
        out_shape=jax.ShapeDtypeStruct((tok, width), BF),
        in_specs=[vmem()] * 3,
        out_specs=vmem(),
        compiler_params=params(16),
        cost_estimate=cost(10**9, 0, 4 * 10**6),
    )(middle, out, x_out)
    return (refined[None], cand_score)


def solution(mesh):
    return jax.shard_map(
        local,
        mesh=mesh,
        in_specs=(
            P("doc", "seq", None),
            P("doc", "seq"),
            P(),
            P(),
            P(),
            P(),
            P(),
            P("doc", None),
            P(),
            P(("doc", "seq"), None, None, None),
        ),
        out_specs=(P("doc", "seq", None), P("doc", None)),
        check_vma=False,
    )
```

```python
import functools
import math

import jax
import jax.numpy as jnp
from jax import lax
from jax.experimental import pallas as pl
from jax.experimental.pallas import tpu as pltpu
from jax.sharding import PartitionSpec as P

HEADS = 12
HALF_WIN = 256
DESC = 8
GRID = 4
LANES = 128
HALF = 64
SCALE = math.log2(math.e) / 8.0
BF = jnp.bfloat16
F32 = jnp.float32
I32 = jnp.int32


def iota(shape, dim):
    return lax.broadcasted_iota(I32, shape, dim)


def dot(a, b):
    return jnp.dot(a, b, preferred_element_type=F32)


def dot_t(a, b):
    return lax.dot_general(a, b, (((1,), (1,)), ((), ())), preferred_element_type=F32)


def params(mib):
    return pltpu.CompilerParams(vmem_limit_bytes=mib << 20)


def vmem():
    return pl.BlockSpec(memory_space=pltpu.VMEM)


def smem():
    return pl.BlockSpec(memory_space=pltpu.SMEM)


def pinned(array):
    return pltpu.with_memory_space_constraint(array, pltpu.HBM)


def hbm():
    return pl.BlockSpec(memory_space=pltpu.HBM)


def cost(flops, exps, bytes_):
    return pl.CostEstimate(flops=flops, transcendentals=exps, bytes_accessed=bytes_)


def planes_kernel(table_ref, planes_ref):
    missing = planes_ref.shape[1] - table_ref.shape[0]
    rows = jnp.concatenate([table_ref[...].astype(F32), jnp.zeros((missing, LANES), F32)], axis=0)
    wide = jnp.transpose(rows)
    high = jnp.floor(wide * (1.0 / 256.0))
    planes_ref[:LANES, :] = high.astype(BF)
    planes_ref[LANES:, :] = (wide - high * 256.0).astype(BF)


def look_up(code, table):
    n = code.shape[1]
    picks = (iota((table.shape[1], n), 0) == (code >> 7)).astype(F32).astype(BF)
    found = dot(table, picks)
    here = iota((LANES, n), 0) == (code & 127)
    value = jnp.where(here, found[:LANES] * 256.0 + found[LANES:], 0.0)
    return jnp.sum(value, axis=0, keepdims=True)


def ranks(row, count, code_dev, devices, upper):
    n = row.shape[1]
    owner = jnp.floor((row + 0.5) * (1.0 / code_dev))
    local = (row - owner * code_dev).astype(I32)
    owner = jnp.where(iota((1, n), 1) < count, owner.astype(I32), 2 * devices)
    sub = iota((devices, n), 0)
    mine = owner == sub
    starts = jnp.sum((owner < sub).astype(F32), axis=1, keepdims=True)
    before = dot(mine.astype(F32).astype(BF), upper)
    rank = jnp.sum(jnp.where(mine, starts + before, 0.0), axis=0, keepdims=True)
    return owner, local, rank.astype(I32)


def upper_ones(n):
    return (iota((n, n), 0) < iota((n, n), 1)).astype(F32).astype(BF)


def route_kernel(
    count, code_dev, devices, where_ref, codes_ref, planes_ref, cache_ref, send_hbm, slot_ref, pos_ref, send_ref, rows, line, picks, picked, sems, sem
):
    docs = codes_ref.shape[0]
    n = line.shape[1]
    upper = upper_ones(n)
    lane = iota((1, LANES), 1)
    line[...] = jnp.full(line.shape, -1, I32)
    for d in range(docs):
        line[d : d + 1, :count] = codes_ref[d]
    planes = planes_ref[...]
    doc = where_ref[2]
    owner_here = jnp.zeros((1, n), I32)
    rank_here = jnp.zeros((1, n), I32)
    for d in range(docs):
        row = look_up(line[d : d + 1, :], planes)
        owner, local, rank = ranks(row, count, code_dev, devices, upper)
        wanted = jnp.where(owner == where_ref[0], local + 1, 0).astype(F32)
        part = rank & (GRID - 1)
        found = jnp.zeros((1, LANES), F32)
        for z in range(GRID):
            one = jnp.sum(jnp.where(part == z, wanted, 0.0), axis=1, keepdims=True)
            found = found + jnp.where(lane == z, one, 0.0)
        picks[d : d + 1, :] = jnp.maximum(found.astype(I32) - 1, 0)
        owner_here = jnp.where(doc == d, owner, owner_here)
        rank_here = jnp.where(doc == d, rank, rank_here)
    to_scalars = pltpu.make_async_copy(picks, picked, sem.at[docs])
    to_scalars.start()
    to_scalars.wait()
    copies = []
    for d in range(docs):
        for z in range(GRID):
            k = d * GRID + z
            copies.append(pltpu.make_async_copy(cache_ref.at[picked[d, z]], rows.at[k], sems.at[k]))
            copies[-1].start()

    part = rank_here & (GRID - 1)
    spot = rank_here >> 2
    live = jnp.where(part == where_ref[1], (spot + 1).astype(F32), 0.0)
    mine = owner_here == iota((devices, n), 0)
    place = jnp.sum(jnp.where(mine, live, 0.0), axis=1, keepdims=True)
    width = devices * DESC
    spread = jnp.where(iota((devices, width), 0) == iota((devices, width), 1) // DESC, place, 0.0)
    spread = jnp.sum(spread, axis=0, keepdims=True).astype(I32)
    inside = iota((1, width), 1) & (DESC - 1)
    slot_ref[...] = jnp.where(spread > 0, (spread - 1) * DESC + inside, -1)
    pos_ref[...] = part * (count // GRID) + spot

    low = iota((GRID, DESC, LANES), 2) < HALF
    sent = []
    for d in range(docs):
        for copy in copies[d * GRID : (d + 1) * GRID]:
            copy.wait()
        block = pl.ds(d * GRID, GRID)
        for p in range(HEADS // 2):
            cols = pl.ds(p * LANES, LANES)
            keys = rows[block, 0, :, cols].astype(F32)
            values = rows[block, 1, :, cols].astype(F32)
            keys_turned = pltpu.roll(keys, HALF, 2)
            values_turned = pltpu.roll(values, HALF, 2)
            for s in range(2):
                head = 2 * p + s
                group, inner = head // 3, head % 3
                key_low = keys if s == 0 else keys_turned
                key_high = keys_turned if s == 0 else keys
                value_low = values if s == 0 else values_turned
                value_high = values_turned if s == 0 else values
                if inner == 1:
                    tile = jnp.where(low, value_low, key_high)
                else:
                    tile = jnp.where(low, key_low, value_high)
                send_ref[block, group, :, pl.ds(inner * LANES, LANES)] = tile.astype(BF)
        sent.append(pltpu.make_async_copy(send_ref.at[block], send_hbm.at[block], sem.at[d]))
        sent[-1].start()
    for copy in sent:
        copy.wait()


def compact_kernel(slot_ref, got_ref, first_ref, rest_ref):
    rows = first_ref.shape[0]
    pick = (iota((rows, got_ref.shape[0]), 0) == slot_ref[...]).astype(F32).astype(BF)
    packed = dot(pick, got_ref[...]).astype(BF)
    first_ref[...] = packed[:, :LANES]
    rest_ref[...] = packed[:, LANES:]


def layer_norm(values):
    centered = values - jnp.mean(values, axis=-1, keepdims=True)
    spread = jnp.mean(centered * centered, axis=-1, keepdims=True)
    return centered * lax.rsqrt(spread + 1e-05)


def halo_kernel(hidden_hbm, tokens_hbm, wanted_hbm, tail_ref, head_ref, asked_ref, tokens_ref, wanted_ref, sems):
    tok, width = hidden_hbm.shape
    win = HALF_WIN
    places = ((tail_ref, tok - win), (head_ref, 0))
    copies = []
    for k, (ref, start) in enumerate(places):
        copies.append(pltpu.make_async_copy(hidden_hbm.at[pl.ds(start, win), :], ref.at[pl.ds(0, win), :], sems.at[k]))
        copies[-1].start()
    small = [
        pltpu.make_async_copy(wanted_hbm, wanted_ref, sems.at[2]),
        pltpu.make_async_copy(tokens_hbm, tokens_ref, sems.at[3]),
    ]
    for copy in small:
        copy.start()
    small[0].wait()
    for d in range(asked_ref.shape[0]):
        asked_ref[d] = wanted_ref[...]
    small[1].wait()
    flags = (tokens_ref[...] != 0).astype(F32)
    for ref, start in places:
        row = jnp.concatenate([flags[:, start : start + win], jnp.zeros((1, width - win), F32)], axis=1)
        ref[win:, :] = jnp.broadcast_to(row, (8, width)).astype(BF)
    for copy in copies:
        copy.wait()


def window_kernel(
    low_ref, hidden_ref, high_ref, tokens_ref, wkv_hbm, wq_hbm, wo_hbm, xq_hbm, middle_ref, query_ref, wkv_ref, wq_ref, wo_ref, xq_ref, normed, keys, values, queries, context, bias, sems
):
    tok, width = hidden_ref.shape
    win = HALF_WIN
    span = 3 * win
    total = tok + 2 * win
    pairs = width // LANES
    pieces = ((wkv_hbm, wkv_ref), (wq_hbm, wq_ref), (wo_hbm, wo_ref), (xq_hbm, xq_ref))
    copies = [pltpu.make_async_copy(src, dst, sems.at[k]) for k, (src, dst) in enumerate(pieces)]
    for copy in copies:
        copy.start()
    normed[:win, :] = layer_norm(low_ref[:win, :].astype(F32)).astype(BF)
    normed[win : win + tok, :] = layer_norm(hidden_ref[...].astype(F32)).astype(BF)
    normed[win + tok :, :] = layer_norm(high_ref[:win, :].astype(F32)).astype(BF)
    own_flags = (tokens_ref[...] != 0).astype(F32)
    flags = jnp.concatenate(
        [low_ref[win : win + 1, :win].astype(F32), own_flags, high_ref[win : win + 1, :win].astype(F32)], axis=1
    )
    gap = iota((win, span), 1) - iota((win, span), 0)
    near = (gap >= 0) & (gap <= 2 * win)
    for b in range(tok // win):
        usable = (flags[:, b * win : b * win + span] > 0.0) | (gap == win)
        bias[b] = jnp.where(near & usable, 0.0, -1e30)
    for p in range(pairs):
        values[:, (2 * p + 1) * LANES : (2 * p + 2) * LANES] = jnp.ones((total, LANES), BF)
    wide = 2 * LANES
    copies[0].wait()
    for c in range(0, width, wide):
        keys[:, c : c + wide] = dot(normed[...], wkv_ref[:, c : c + wide]).astype(BF)
    for c in range(0, width, wide):
        part = dot(normed[...], wkv_ref[:, width + c : width + c + wide]).astype(BF).astype(F32) * 2.0**-8
        part = part.astype(BF)
        values[:, 2 * c : 2 * c + LANES] = part[:, :LANES]
        values[:, 2 * c + wide : 2 * c + wide + LANES] = part[:, LANES:]
    copies[1].wait()
    for c in range(0, width, wide):
        queries[:, c : c + wide] = (dot(normed[win : win + tok, :], wq_ref[:, c : c + wide]) * SCALE).astype(BF)
    low = iota((win, LANES), 1) < HALF
    for b in range(tok // win):
        for p in range(pairs):
            cols = slice(p * LANES, (p + 1) * LANES)
            query = queries[b * win : (b + 1) * win, cols]
            key = keys[b * win : b * win + span, cols]
            value = values[b * win : b * win + span, 2 * p * LANES : (2 * p + 2) * LANES]
            nothing = jnp.zeros_like(query)
            both = jnp.concatenate([jnp.where(low, query, nothing), jnp.where(low, nothing, query)], axis=0)
            scores = dot_t(both, key).reshape(2, win, span) + bias[b][None]
            out = dot(jnp.exp2(scores).astype(BF).reshape(2 * win, span), value)
            out = out[:, :LANES] / out[:, LANES:] * 256.0
            context[b * win : (b + 1) * win, cols] = jnp.where(low, out[:win], out[win:]).astype(BF)
    copies[2].wait()
    copies[3].wait()
    thirds_of = [[] for _ in range(GRID)]
    for b in range(tok // win):
        rows = slice(b * win, (b + 1) * win)
        mixed = hidden_ref[rows, :].astype(F32) + dot(context[rows, :], wo_ref[...])
        mixed = mixed.astype(BF)
        middle_ref[rows, :] = mixed
        cross = dot(layer_norm(mixed.astype(F32)).astype(BF), xq_ref[...]) * SCALE
        tiles = [cross[:, p * LANES : (p + 1) * LANES] for p in range(pairs)]
        turned = [pltpu.roll(t, HALF, 1) for t in tiles]

        def placed(head, upper):
            return (turned if (head % 2 == 1) != upper else tiles)[head // 2]

        for g in range(GRID):
            first = jnp.where(low, placed(3 * g, False), placed(3 * g + 1, True))
            query_ref[g, rows, :] = first.astype(BF)
            thirds_of[g].append(placed(3 * g + 2, b == 1))
    line = iota((16, LANES), 0)
    marks = jnp.zeros((16, LANES), F32)
    for k in range(tok // LANES):
        marks = jnp.where(line == k, own_flags[:, k * LANES : (k + 1) * LANES], marks)
    for g in range(GRID):
        query_ref[g, tok : tok + win, :] = jnp.where(low, thirds_of[g][0], thirds_of[g][1]).astype(BF)
        query_ref[g, tok + win :, :] = marks.astype(BF)


def cross_kernel(heads, count, where_ref, pos_ref, query_ref, *refs):
    kv_refs, refs = refs[:GRID], refs[GRID:]
    last = 2 in heads
    if last:
        before_ref, earlier_ref, out_ref, score_ref, keys, values, expds, total = refs
    else:
        out_ref, mass_ref, keys, values, expds, total = refs
    held = kv_refs[0].shape[0]
    tok = expds.shape[1]
    groups = query_ref.shape[0]
    half = tok // 2
    small = iota((tok, LANES), 1) < HALF
    low = iota((half, LANES), 1) < HALF
    if last:
        total[...] = before_ref[...]
    else:
        total[...] = jnp.zeros_like(total)
    lower = iota((held, LANES), 1) < HALF
    for k, inner in enumerate(heads):
        for c in range(GRID):
            rows = pl.ds(c * held, held)
            block = kv_refs[c][:, k * LANES : (k + 1) * LANES]
            keys[k, rows, :] = block
            scaled = block.astype(F32) * 2.0**-4
            values[k, rows, :] = jnp.where(lower == (inner == 1), scaled, 1.0).astype(BF)

    def one(g, k, slot):
        inner = heads[k]
        value_low = inner == 1
        if inner == 2:
            packed = query_ref[g, tok : tok + half, :]
            turned = pltpu.roll(packed.astype(F32), HALF, 1).astype(BF)
            query = jnp.concatenate([packed, turned], axis=0)
        else:
            query = query_ref[g, :tok, :]
        query = jnp.where(small != value_low, query, jnp.zeros_like(query))
        acc = jnp.zeros((tok, LANES), F32)
        for c in range(0, GRID * held, 512):
            expd = jnp.exp2(dot_t(query, keys[k, c : c + 512, :])).astype(BF)
            expds[slot, :, c : c + 512] = expd
            acc = acc + dot(expd, values[k, c : c + 512, :])
        at = LANES - 1 if value_low else 0
        inverse = 1.0 / acc[:, at : at + 1]
        out = (acc * inverse) * 16.0
        share = jnp.where(iota((tok, 1), 0).astype(F32) < tokens_of(g), inverse, 0.0)
        for c in range(0, GRID * held, 512):
            mass = jnp.sum(expds[slot, :, c : c + 512].astype(F32) * share, axis=0, keepdims=True)
            total[:1, c : c + 512] = total[:1, c : c + 512] + mass
        return out

    def tokens_of(g):
        marks = query_ref[g, tok + half :, :].astype(F32)
        return jnp.sum(jnp.sum(marks, axis=0, keepdims=True), axis=1, keepdims=True)

    if not last:

        def body(i, carry):
            for u in range(2):
                out_ref[2 * i + u] = one(2 * i + u, 0, u).astype(BF)
            return carry

        lax.fori_loop(0, groups // 2, body, 0)
        mass_ref[...] = total[...]
        return

    def body(g, carry):
        out_ref[g, :tok, :] = jnp.where(small, one(g, 0, 0), earlier_ref[g].astype(F32)).astype(BF)
        out = one(g, 1, 1)
        out_ref[g, tok : tok + half, :] = jnp.where(low, pltpu.roll(out[:half], HALF, 1), out[half:]).astype(BF)
        return carry

    lax.fori_loop(0, groups, body, 0)
    padded = pos_ref.shape[1]
    score = jnp.zeros((8, padded), F32)
    line = iota((8, held), 0)
    for c in range(GRID):
        mass = jnp.broadcast_to(total[:1, c * held : (c + 1) * held], (8, held))
        first, second, third = thirds(mass)
        parts = jnp.where(line == 0, first, jnp.where(line == 1, second, jnp.where(line == 2, third, 0.0)))
        origin = (where_ref[1] + GRID - c) & (GRID - 1)
        at = iota((held, padded), 0) // DESC + origin * (count // GRID)
        score = score + dot(parts.astype(BF), (at == pos_ref[...]).astype(F32).astype(BF))
    score = jnp.sum(score, axis=0, keepdims=True)
    tokens = tokens_of(0)
    for g in range(1, groups):
        tokens = tokens + tokens_of(g)
    score = jnp.where(iota((1, padded), 1) == count, tokens, score)
    score_ref[...] = score


def thirds(value):
    first = value.astype(BF).astype(F32)
    second = (value - first).astype(BF).astype(F32)
    return first, second, value - first - second


def final_kernel(middle_ref, got_ref, weight_ref, out_ref):
    tok = middle_ref.shape[0]
    groups = got_ref.shape[0]
    half = tok // 2
    size = 3 * HALF
    low = iota((half, LANES), 1) < HALF
    acc = middle_ref[...].astype(F32)
    for g in range(groups):
        at = g * size
        heads = [weight_ref[at + k * HALF : at + (k + 1) * HALF, :] for k in (1, 0, 2, 2)]
        packed = got_ref[g, tok : tok + half, :]
        nothing = jnp.zeros_like(packed)
        third = jnp.concatenate([jnp.where(low, packed, nothing), jnp.where(low, nothing, packed)], axis=0)
        lhs = jnp.concatenate([got_ref[g, :tok, :], third], axis=1)
        acc = acc + dot(lhs, jnp.concatenate(heads, axis=0))
    out_ref[...] = acc.astype(BF)


def local(hidden, token_ids, w_query, w_keyval, w_out, x_query, x_out, shortlist, code_row, code_cache):
    doc_hidden = hidden[0]
    tok, width = doc_hidden.shape
    seq_count = lax.axis_size("seq")
    docs = lax.axis_size("doc")
    devices = docs * seq_count
    seq_index = lax.axis_index("seq")
    own = lax.axis_index("doc") * seq_count + seq_index
    where = jnp.stack([own, seq_index // GRID, lax.axis_index("doc")]).astype(I32)
    count = shortlist.shape[1]
    padded = -(-count // LANES) * LANES
    code_dev = code_cache.shape[0]
    held = count // GRID * DESC
    message = tok + tok // 2 + 16
    table = code_row.reshape(-1, LANES)

    forward = [(i, i + 1) for i in range(seq_count - 1)]
    backward = [(t, s) for s, t in forward]
    tail, head, asked = pl.pallas_call(
        halo_kernel,
        name="halo",
        out_shape=(jax.ShapeDtypeStruct((HALF_WIN + 8, width), BF),) * 2
        + (jax.ShapeDtypeStruct((docs, 1, count), I32),),
        in_specs=[hbm()] * 3,
        out_specs=(vmem(),) * 3,
        scratch_shapes=[pltpu.VMEM((1, tok), I32), pltpu.VMEM((1, count), I32), pltpu.SemaphoreType.DMA((4,))],
        compiler_params=params(16),
        cost_estimate=cost(10**5, 0, 16 * 10**5),
    )(*map(pinned, (doc_hidden, token_ids, shortlist)))
    all_codes = lax.all_to_all(asked, "doc", split_axis=0, concat_axis=0, tiled=True)
    table, head = lax.optimization_barrier((table, head))
    planes = pl.pallas_call(
        planes_kernel,
        name="planes",
        out_shape=jax.ShapeDtypeStruct((2 * LANES, -(-table.shape[0] // LANES) * LANES), BF),
        in_specs=[vmem()],
        out_specs=vmem(),
        compiler_params=params(16),
        cost_estimate=cost(10**5, 0, 2 * 10**5),
    )(table)
    low = lax.ppermute(tail, "seq", forward)
    high = lax.ppermute(head, "seq", backward)

    send, slots, pos = pl.pallas_call(
        functools.partial(route_kernel, count, code_dev, devices),
        name="route",
        out_shape=(
            jax.ShapeDtypeStruct((docs * GRID, GRID, DESC, 3 * LANES), BF),
            jax.ShapeDtypeStruct((1, devices * DESC), I32),
            jax.ShapeDtypeStruct((1, padded), I32),
        ),
        in_specs=[smem(), vmem(), vmem(), hbm()],
        out_specs=(hbm(), vmem(), vmem()),
        scratch_shapes=[
            pltpu.VMEM((docs * GRID, GRID, DESC, 3 * LANES), BF),
            pltpu.VMEM((docs * GRID, 2, DESC, width), BF),
            pltpu.VMEM((docs, padded), I32),
            pltpu.VMEM((docs, LANES), I32),
            pltpu.SMEM((docs, LANES), I32),
            pltpu.SemaphoreType.DMA((docs * GRID,)),
            pltpu.SemaphoreType.DMA((docs + 1,)),
        ],
        compiler_params=params(24),
        cost_estimate=cost(10**9, 0, 2 * 10**6),
    )(where, all_codes, planes, pinned(code_cache))
    got = lax.all_to_all(
        send.reshape(devices, DESC, 3 * LANES), ("doc", "seq"), split_axis=0, concat_axis=0, tiled=True
    )

    middle, queries = pl.pallas_call(
        window_kernel,
        name="window",
        out_shape=(
            jax.ShapeDtypeStruct((tok, width), BF),
            jax.ShapeDtypeStruct((GRID, message, LANES), BF),
        ),
        in_specs=[vmem()] * 4 + [hbm()] * 4,
        out_specs=(vmem(), vmem()),
        scratch_shapes=[
            pltpu.VMEM((width, 2 * width), BF),
            pltpu.VMEM((width, width), BF),
            pltpu.VMEM((width, width), BF),
            pltpu.VMEM((width, width), BF),
            pltpu.VMEM((tok + 2 * HALF_WIN, width), BF),
            pltpu.VMEM((tok + 2 * HALF_WIN, width), BF),
            pltpu.VMEM((tok + 2 * HALF_WIN, 2 * width), BF),
            pltpu.VMEM((tok, width), BF),
            pltpu.VMEM((tok, width), BF),
            pltpu.VMEM((tok // HALF_WIN, HALF_WIN, 3 * HALF_WIN), F32),
            pltpu.SemaphoreType.DMA((4,)),
        ],
        compiler_params=params(26),
        cost_estimate=cost(12 * 10**9, 5 * 10**6, 10**7),
    )(low, doc_hidden, high, token_ids, *map(pinned, (w_keyval, w_query, w_out, x_query)))

    lines = [[GRID * z + x for x in range(GRID)] for z in range(GRID)]

    def across(block):
        return lax.all_to_all(
            block, "seq", split_axis=0, concat_axis=0, axis_index_groups=lines, tiled=True
        )

    queries = across(queries)

    blocks = pl.pallas_call(
        compact_kernel,
        name="compact",
        out_shape=(jax.ShapeDtypeStruct((held, LANES), BF), jax.ShapeDtypeStruct((held, 2 * LANES), BF)),
        in_specs=[vmem()] * 2,
        out_specs=(vmem(),) * 2,
        compiler_params=params(24),
        cost_estimate=cost(10**9, 0, 2 * 10**6),
    )(slots, got.reshape(devices * DESC, 3 * LANES))

    def turn(block, shift):
        pairs = [(i, (i + GRID * shift) % seq_count) for i in range(seq_count)]
        return lax.ppermute(block, "seq", pairs)

    block, rest_block = blocks
    up, down = turn(block, 1), turn(block, 3)
    rest_up, rest_down = turn(rest_block, 1), turn(rest_block, 3)
    far = turn(down, 3)
    up, down, far, rest_up = lax.optimization_barrier((up, down, far, rest_up))
    rest_far = turn(rest_up, 1)
    first, rest = [block, up, far, down], [rest_block, rest_up, rest_far, rest_down]

    def cross(heads, parts, extra, outs):
        return pl.pallas_call(
            functools.partial(cross_kernel, heads, count),
            name="cross",
            out_shape=outs,
            in_specs=[smem()] + [vmem()] * (2 + GRID + len(extra)),
            out_specs=jax.tree.map(lambda _: vmem(), outs),
            scratch_shapes=[
                pltpu.VMEM((len(heads), GRID * held, LANES), BF),
                pltpu.VMEM((len(heads), GRID * held, LANES), BF),
                pltpu.VMEM((2, tok, GRID * held), BF),
                pltpu.VMEM((8, GRID * held), F32),
            ],
            compiler_params=params(18),
            cost_estimate=cost(len(heads) * 10**10, 5 * 10**6, 4 * 10**6),
        )(where, pos, queries, *parts, *extra)

    out, mass = cross(
        (0,),
        first,
        (),
        (jax.ShapeDtypeStruct((GRID, tok, LANES), BF), jax.ShapeDtypeStruct((8, GRID * held), F32)),
    )
    out, score = cross(
        (1, 2),
        rest,
        (mass, out),
        (jax.ShapeDtypeStruct((GRID, message, LANES), BF), jax.ShapeDtypeStruct((1, padded), F32)),
    )

    across_x = [[(i, GRID * (i // GRID) + (i + shift) % GRID) for i in range(seq_count)] for shift in range(1, GRID)]
    one, two, three = [lax.ppermute(score, "seq", pairs) for pairs in across_x]
    score = (score + two) + (one + three)
    one, two, three = [turn(score, shift) for shift in (1, 2, 3)]
    sums = (score + two) + (one + three)
    tokens = sums[:, count : count + 1] * (1.0 / GRID)
    cand_score = count * sums[:, :count] / (HEADS * tokens)
    out = across(out)

    refined = pl.pallas_call(
        final_kernel,
        name="final",
        out_shape=jax.ShapeDtypeStruct((tok, width), BF),
        in_specs=[vmem()] * 3,
        out_specs=vmem(),
        compiler_params=params(16),
        cost_estimate=cost(10**9, 0, 4 * 10**6),
    )(middle, out, x_out)
    return (refined[None], cand_score)


def solution(mesh):
    return jax.shard_map(
        local,
        mesh=mesh,
        in_specs=(
            P("doc", "seq", None),
            P("doc", "seq"),
            P(),
            P(),
            P(),
            P(),
            P(),
            P("doc", None),
            P(),
            P(("doc", "seq"), None, None, None),
        ),
        out_specs=(P("doc", "seq", None), P("doc", None)),
        check_vma=False,
    )
```

```python
import functools
import math

import jax
import jax.numpy as jnp
from jax import lax
from jax.experimental import pallas as pl
from jax.experimental.pallas import tpu as pltpu
from jax.sharding import PartitionSpec as P

HEADS = 12
HALF_WIN = 256
DESC = 8
GRID = 4
LANES = 128
HALF = 64
SCALE = math.log2(math.e) / 8.0
BF = jnp.bfloat16
F32 = jnp.float32
I32 = jnp.int32


def iota(shape, dim):
    return lax.broadcasted_iota(I32, shape, dim)


def dot(a, b):
    return jnp.dot(a, b, preferred_element_type=F32)


def dot_t(a, b):
    return lax.dot_general(a, b, (((1,), (1,)), ((), ())), preferred_element_type=F32)


def params(mib):
    return pltpu.CompilerParams(vmem_limit_bytes=mib << 20)


def vmem():
    return pl.BlockSpec(memory_space=pltpu.VMEM)


def smem():
    return pl.BlockSpec(memory_space=pltpu.SMEM)


def pinned(array):
    return pltpu.with_memory_space_constraint(array, pltpu.HBM)


def hbm():
    return pl.BlockSpec(memory_space=pltpu.HBM)


def cost(flops, exps, bytes_):
    return pl.CostEstimate(flops=flops, transcendentals=exps, bytes_accessed=bytes_)


def planes_kernel(table_ref, planes_ref):
    missing = planes_ref.shape[1] - table_ref.shape[0]
    rows = jnp.concatenate([table_ref[...].astype(F32), jnp.zeros((missing, LANES), F32)], axis=0)
    wide = jnp.transpose(rows)
    high = jnp.floor(wide * (1.0 / 256.0))
    planes_ref[:LANES, :] = high.astype(BF)
    planes_ref[LANES:, :] = (wide - high * 256.0).astype(BF)


def look_up(code, table):
    n = code.shape[1]
    picks = (iota((table.shape[1], n), 0) == (code >> 7)).astype(F32).astype(BF)
    found = dot(table, picks)
    here = iota((LANES, n), 0) == (code & 127)
    value = jnp.where(here, found[:LANES] * 256.0 + found[LANES:], 0.0)
    return jnp.sum(value, axis=0, keepdims=True)


def ranks(row, count, code_dev, devices, upper):
    n = row.shape[1]
    owner = jnp.floor((row + 0.5) * (1.0 / code_dev))
    local = (row - owner * code_dev).astype(I32)
    owner = jnp.where(iota((1, n), 1) < count, owner.astype(I32), 2 * devices)
    sub = iota((devices, n), 0)
    mine = owner == sub
    starts = jnp.sum((owner < sub).astype(F32), axis=1, keepdims=True)
    before = dot(mine.astype(F32).astype(BF), upper)
    rank = jnp.sum(jnp.where(mine, starts + before, 0.0), axis=0, keepdims=True)
    return owner, local, rank.astype(I32)


def upper_ones(n):
    return (iota((n, n), 0) < iota((n, n), 1)).astype(F32).astype(BF)


def route_kernel(
    count, code_dev, devices, where_ref, codes_ref, planes_ref, cache_ref, send_hbm, slot_ref, pos_ref, send_ref, rows, line, picks, picked, sems, sem
):
    docs = codes_ref.shape[0]
    n = line.shape[1]
    upper = upper_ones(n)
    lane = iota((1, LANES), 1)
    line[...] = jnp.full(line.shape, -1, I32)
    for d in range(docs):
        line[d : d + 1, :count] = codes_ref[d]
    planes = planes_ref[...]
    doc = where_ref[2]
    owner_here = jnp.zeros((1, n), I32)
    rank_here = jnp.zeros((1, n), I32)
    for d in range(docs):
        row = look_up(line[d : d + 1, :], planes)
        owner, local, rank = ranks(row, count, code_dev, devices, upper)
        wanted = jnp.where(owner == where_ref[0], local + 1, 0).astype(F32)
        part = rank & (GRID - 1)
        found = jnp.zeros((1, LANES), F32)
        for z in range(GRID):
            one = jnp.sum(jnp.where(part == z, wanted, 0.0), axis=1, keepdims=True)
            found = found + jnp.where(lane == z, one, 0.0)
        picks[d : d + 1, :] = jnp.maximum(found.astype(I32) - 1, 0)
        owner_here = jnp.where(doc == d, owner, owner_here)
        rank_here = jnp.where(doc == d, rank, rank_here)
    to_scalars = pltpu.make_async_copy(picks, picked, sem.at[docs])
    to_scalars.start()
    to_scalars.wait()
    copies = []
    for d in range(docs):
        for z in range(GRID):
            k = d * GRID + z
            copies.append(pltpu.make_async_copy(cache_ref.at[picked[d, z]], rows.at[k], sems.at[k]))
            copies[-1].start()

    part = rank_here & (GRID - 1)
    spot = rank_here >> 2
    live = jnp.where(part == where_ref[1], (spot + 1).astype(F32), 0.0)
    mine = owner_here == iota((devices, n), 0)
    place = jnp.sum(jnp.where(mine, live, 0.0), axis=1, keepdims=True)
    width = devices * DESC
    spread = jnp.where(iota((devices, width), 0) == iota((devices, width), 1) // DESC, place, 0.0)
    spread = jnp.sum(spread, axis=0, keepdims=True).astype(I32)
    inside = iota((1, width), 1) & (DESC - 1)
    slot_ref[...] = jnp.where(spread > 0, (spread - 1) * DESC + inside, -1)
    pos_ref[...] = part * (count // GRID) + spot

    low = iota((GRID, DESC, LANES), 2) < HALF
    sent = []
    for d in range(docs):
        for copy in copies[d * GRID : (d + 1) * GRID]:
            copy.wait()
        block = pl.ds(d * GRID, GRID)
        for p in range(HEADS // 2):
            cols = pl.ds(p * LANES, LANES)
            keys = rows[block, 0, :, cols].astype(F32)
            values = rows[block, 1, :, cols].astype(F32)
            keys_turned = pltpu.roll(keys, HALF, 2)
            values_turned = pltpu.roll(values, HALF, 2)
            for s in range(2):
                head = 2 * p + s
                group, inner = head // 3, head % 3
                key_low = keys if s == 0 else keys_turned
                key_high = keys_turned if s == 0 else keys
                value_low = values if s == 0 else values_turned
                value_high = values_turned if s == 0 else values
                if inner == 1:
                    tile = jnp.where(low, value_low, key_high)
                else:
                    tile = jnp.where(low, key_low, value_high)
                send_ref[block, group, :, pl.ds(inner * LANES, LANES)] = tile.astype(BF)
        sent.append(pltpu.make_async_copy(send_ref.at[block], send_hbm.at[block], sem.at[d]))
        sent[-1].start()
    for copy in sent:
        copy.wait()


def compact_kernel(slot_ref, got_ref, first_ref, rest_ref):
    rows = first_ref.shape[0]
    pick = (iota((rows, got_ref.shape[0]), 0) == slot_ref[...]).astype(F32).astype(BF)
    packed = dot(pick, got_ref[...]).astype(BF)
    first_ref[...] = packed[:, :LANES]
    rest_ref[...] = packed[:, LANES:]


def layer_norm(values):
    centered = values - jnp.mean(values, axis=-1, keepdims=True)
    spread = jnp.mean(centered * centered, axis=-1, keepdims=True)
    return centered * lax.rsqrt(spread + 1e-05)


def halo_kernel(hidden_hbm, tokens_hbm, wanted_hbm, tail_ref, head_ref, asked_ref, tokens_ref, wanted_ref, sems):
    tok, width = hidden_hbm.shape
    win = HALF_WIN
    places = ((tail_ref, tok - win), (head_ref, 0))
    copies = []
    for k, (ref, start) in enumerate(places):
        copies.append(pltpu.make_async_copy(hidden_hbm.at[pl.ds(start, win), :], ref.at[pl.ds(0, win), :], sems.at[k]))
        copies[-1].start()
    small = [
        pltpu.make_async_copy(wanted_hbm, wanted_ref, sems.at[2]),
        pltpu.make_async_copy(tokens_hbm, tokens_ref, sems.at[3]),
    ]
    for copy in small:
        copy.start()
    small[0].wait()
    for d in range(asked_ref.shape[0]):
        asked_ref[d] = wanted_ref[...]
    small[1].wait()
    flags = (tokens_ref[...] != 0).astype(F32)
    for ref, start in places:
        row = jnp.concatenate([flags[:, start : start + win], jnp.zeros((1, width - win), F32)], axis=1)
        ref[win:, :] = jnp.broadcast_to(row, (8, width)).astype(BF)
    for copy in copies:
        copy.wait()


def window_kernel(
    low_ref, hidden_ref, high_ref, tokens_ref, wkv_hbm, wq_hbm, wo_hbm, xq_hbm, middle_hbm, query_ref, middle_ref, wkv_ref, wq_ref, wo_ref, xq_ref, normed, keys, values, queries, context, bias, sems
):
    tok, width = hidden_ref.shape
    win = HALF_WIN
    span = 3 * win
    total = tok + 2 * win
    pairs = width // LANES
    pieces = ((wkv_hbm, wkv_ref), (wq_hbm, wq_ref), (wo_hbm, wo_ref), (xq_hbm, xq_ref))
    copies = [pltpu.make_async_copy(src, dst, sems.at[k]) for k, (src, dst) in enumerate(pieces)]
    for copy in copies:
        copy.start()
    normed[:win, :] = layer_norm(low_ref[:win, :].astype(F32)).astype(BF)
    normed[win : win + tok, :] = layer_norm(hidden_ref[...].astype(F32)).astype(BF)
    normed[win + tok :, :] = layer_norm(high_ref[:win, :].astype(F32)).astype(BF)
    own_flags = (tokens_ref[...] != 0).astype(F32)
    flags = jnp.concatenate(
        [low_ref[win : win + 1, :win].astype(F32), own_flags, high_ref[win : win + 1, :win].astype(F32)], axis=1
    )
    gap = iota((win, span), 1) - iota((win, span), 0)
    near = (gap >= 0) & (gap <= 2 * win)
    for b in range(tok // win):
        usable = (flags[:, b * win : b * win + span] > 0.0) | (gap == win)
        bias[b] = jnp.where(near & usable, 0.0, -1e30)
    for p in range(pairs):
        values[:, (2 * p + 1) * LANES : (2 * p + 2) * LANES] = jnp.ones((total, LANES), BF)
    wide = 2 * LANES
    copies[0].wait()
    for c in range(0, width, wide):
        keys[:, c : c + wide] = dot(normed[...], wkv_ref[:, c : c + wide]).astype(BF)
    for c in range(0, width, wide):
        part = dot(normed[...], wkv_ref[:, width + c : width + c + wide]).astype(BF).astype(F32) * 2.0**-8
        part = part.astype(BF)
        values[:, 2 * c : 2 * c + LANES] = part[:, :LANES]
        values[:, 2 * c + wide : 2 * c + wide + LANES] = part[:, LANES:]
    copies[1].wait()
    for c in range(0, width, wide):
        queries[:, c : c + wide] = (dot(normed[win : win + tok, :], wq_ref[:, c : c + wide]) * SCALE).astype(BF)
    low = iota((win, LANES), 1) < HALF
    for b in range(tok // win):
        for p in range(pairs):
            cols = slice(p * LANES, (p + 1) * LANES)
            query = queries[b * win : (b + 1) * win, cols]
            key = keys[b * win : b * win + span, cols]
            value = values[b * win : b * win + span, 2 * p * LANES : (2 * p + 2) * LANES]
            nothing = jnp.zeros_like(query)
            both = jnp.concatenate([jnp.where(low, query, nothing), jnp.where(low, nothing, query)], axis=0)
            scores = dot_t(both, key).reshape(2, win, span) + bias[b][None]
            out = dot(jnp.exp2(scores).astype(BF).reshape(2 * win, span), value)
            out = out[:, :LANES] / out[:, LANES:] * 256.0
            context[b * win : (b + 1) * win, cols] = jnp.where(low, out[:win], out[win:]).astype(BF)
    copies[2].wait()
    copies[3].wait()
    thirds_of = [[] for _ in range(GRID)]
    kept = []
    for b in range(tok // win):
        rows = slice(b * win, (b + 1) * win)
        mixed = hidden_ref[rows, :].astype(F32) + dot(context[rows, :], wo_ref[...])
        mixed = mixed.astype(BF)
        middle_ref[rows, :] = mixed
        kept.append(pltpu.make_async_copy(middle_ref.at[rows, :], middle_hbm.at[rows, :], sems.at[4 + b]))
        kept[-1].start()
        cross = dot(layer_norm(mixed.astype(F32)).astype(BF), xq_ref[...]) * SCALE
        tiles = [cross[:, p * LANES : (p + 1) * LANES] for p in range(pairs)]
        turned = [pltpu.roll(t, HALF, 1) for t in tiles]

        def placed(head, upper):
            return (turned if (head % 2 == 1) != upper else tiles)[head // 2]

        for g in range(GRID):
            first = jnp.where(low, placed(3 * g, False), placed(3 * g + 1, True))
            query_ref[g, rows, :] = first.astype(BF)
            thirds_of[g].append(placed(3 * g + 2, b == 1))
    line = iota((16, LANES), 0)
    marks = jnp.zeros((16, LANES), F32)
    for k in range(tok // LANES):
        marks = jnp.where(line == k, own_flags[:, k * LANES : (k + 1) * LANES], marks)
    for g in range(GRID):
        query_ref[g, tok : tok + win, :] = jnp.where(low, thirds_of[g][0], thirds_of[g][1]).astype(BF)
        query_ref[g, tok + win :, :] = marks.astype(BF)
    for copy in kept:
        copy.wait()


def cross_kernel(heads, count, where_ref, pos_ref, query_ref, *refs):
    kv_refs, refs = refs[:GRID], refs[GRID:]
    last = 2 in heads
    if last:
        before_ref, earlier_ref, out_ref, score_ref, keys, values, expds, total = refs
    else:
        out_ref, mass_ref, keys, values, expds, total = refs
    held = kv_refs[0].shape[0]
    tok = expds.shape[1]
    groups = query_ref.shape[0]
    half = tok // 2
    small = iota((tok, LANES), 1) < HALF
    low = iota((half, LANES), 1) < HALF
    if last:
        total[...] = before_ref[...]
    else:
        total[...] = jnp.zeros_like(total)
    lower = iota((held, LANES), 1) < HALF
    for k, inner in enumerate(heads):
        for c in range(GRID):
            rows = pl.ds(c * held, held)
            block = kv_refs[c][:, k * LANES : (k + 1) * LANES]
            keys[k, rows, :] = block
            scaled = block.astype(F32) * 2.0**-4
            values[k, rows, :] = jnp.where(lower == (inner == 1), scaled, 1.0).astype(BF)

    def one(g, k, slot):
        inner = heads[k]
        value_low = inner == 1
        if inner == 2:
            packed = query_ref[g, tok : tok + half, :]
            turned = pltpu.roll(packed.astype(F32), HALF, 1).astype(BF)
            query = jnp.concatenate([packed, turned], axis=0)
        else:
            query = query_ref[g, :tok, :]
        query = jnp.where(small != value_low, query, jnp.zeros_like(query))
        acc = jnp.zeros((tok, LANES), F32)
        for c in range(0, GRID * held, 512):
            expd = jnp.exp2(dot_t(query, keys[k, c : c + 512, :])).astype(BF)
            expds[slot, :, c : c + 512] = expd
            acc = acc + dot(expd, values[k, c : c + 512, :])
        at = LANES - 1 if value_low else 0
        inverse = 1.0 / acc[:, at : at + 1]
        out = (acc * inverse) * 16.0
        share = jnp.where(iota((tok, 1), 0).astype(F32) < tokens_of(g), inverse, 0.0)
        for c in range(0, GRID * held, 512):
            mass = jnp.sum(expds[slot, :, c : c + 512].astype(F32) * share, axis=0, keepdims=True)
            total[:1, c : c + 512] = total[:1, c : c + 512] + mass
        return out

    def tokens_of(g):
        marks = query_ref[g, tok + half :, :].astype(F32)
        return jnp.sum(jnp.sum(marks, axis=0, keepdims=True), axis=1, keepdims=True)

    if not last:

        def body(i, carry):
            for u in range(2):
                out_ref[2 * i + u] = one(2 * i + u, 0, u).astype(BF)
            return carry

        lax.fori_loop(0, groups // 2, body, 0)
        mass_ref[...] = total[...]
        return

    def body(g, carry):
        out_ref[g, :tok, :] = jnp.where(small, one(g, 0, 0), earlier_ref[g].astype(F32)).astype(BF)
        out = one(g, 1, 1)
        out_ref[g, tok : tok + half, :] = jnp.where(low, pltpu.roll(out[:half], HALF, 1), out[half:]).astype(BF)
        return carry

    lax.fori_loop(0, groups, body, 0)
    padded = pos_ref.shape[1]
    score = jnp.zeros((8, padded), F32)
    line = iota((8, held), 0)
    for c in range(GRID):
        mass = jnp.broadcast_to(total[:1, c * held : (c + 1) * held], (8, held))
        first, second, third = thirds(mass)
        parts = jnp.where(line == 0, first, jnp.where(line == 1, second, jnp.where(line == 2, third, 0.0)))
        origin = (where_ref[1] + GRID - c) & (GRID - 1)
        at = iota((held, padded), 0) // DESC + origin * (count // GRID)
        score = score + dot(parts.astype(BF), (at == pos_ref[...]).astype(F32).astype(BF))
    score = jnp.sum(score, axis=0, keepdims=True)
    tokens = tokens_of(0)
    for g in range(1, groups):
        tokens = tokens + tokens_of(g)
    score = jnp.where(iota((1, padded), 1) == count, tokens, score)
    score_ref[...] = score


def thirds(value):
    first = value.astype(BF).astype(F32)
    second = (value - first).astype(BF).astype(F32)
    return first, second, value - first - second


def final_kernel(middle_ref, got_ref, weight_ref, out_ref):
    tok = middle_ref.shape[0]
    groups = got_ref.shape[0]
    half = tok // 2
    size = 3 * HALF
    low = iota((half, LANES), 1) < HALF
    acc = middle_ref[...].astype(F32)
    for g in range(groups):
        at = g * size
        heads = [weight_ref[at + k * HALF : at + (k + 1) * HALF, :] for k in (1, 0, 2, 2)]
        packed = got_ref[g, tok : tok + half, :]
        nothing = jnp.zeros_like(packed)
        third = jnp.concatenate([jnp.where(low, packed, nothing), jnp.where(low, nothing, packed)], axis=0)
        lhs = jnp.concatenate([got_ref[g, :tok, :], third], axis=1)
        acc = acc + dot(lhs, jnp.concatenate(heads, axis=0))
    out_ref[...] = acc.astype(BF)


def local(hidden, token_ids, w_query, w_keyval, w_out, x_query, x_out, shortlist, code_row, code_cache):
    doc_hidden = hidden[0]
    tok, width = doc_hidden.shape
    seq_count = lax.axis_size("seq")
    docs = lax.axis_size("doc")
    devices = docs * seq_count
    seq_index = lax.axis_index("seq")
    own = lax.axis_index("doc") * seq_count + seq_index
    where = jnp.stack([own, seq_index // GRID, lax.axis_index("doc")]).astype(I32)
    count = shortlist.shape[1]
    padded = -(-count // LANES) * LANES
    code_dev = code_cache.shape[0]
    held = count // GRID * DESC
    message = tok + tok // 2 + 16
    table = code_row.reshape(-1, LANES)

    forward = [(i, i + 1) for i in range(seq_count - 1)]
    backward = [(t, s) for s, t in forward]
    tail, head, asked = pl.pallas_call(
        halo_kernel,
        name="halo",
        out_shape=(jax.ShapeDtypeStruct((HALF_WIN + 8, width), BF),) * 2
        + (jax.ShapeDtypeStruct((docs, 1, count), I32),),
        in_specs=[hbm()] * 3,
        out_specs=(vmem(),) * 3,
        scratch_shapes=[pltpu.VMEM((1, tok), I32), pltpu.VMEM((1, count), I32), pltpu.SemaphoreType.DMA((4,))],
        compiler_params=params(16),
        cost_estimate=cost(10**5, 0, 16 * 10**5),
    )(*map(pinned, (doc_hidden, token_ids, shortlist)))
    all_codes = lax.all_to_all(asked, "doc", split_axis=0, concat_axis=0, tiled=True)
    table, head = lax.optimization_barrier((table, head))
    planes = pl.pallas_call(
        planes_kernel,
        name="planes",
        out_shape=jax.ShapeDtypeStruct((2 * LANES, -(-table.shape[0] // LANES) * LANES), BF),
        in_specs=[vmem()],
        out_specs=vmem(),
        compiler_params=params(16),
        cost_estimate=cost(10**5, 0, 2 * 10**5),
    )(table)
    low = lax.ppermute(tail, "seq", forward)
    high = lax.ppermute(head, "seq", backward)

    send, slots, pos = pl.pallas_call(
        functools.partial(route_kernel, count, code_dev, devices),
        name="route",
        out_shape=(
            jax.ShapeDtypeStruct((docs * GRID, GRID, DESC, 3 * LANES), BF),
            jax.ShapeDtypeStruct((1, devices * DESC), I32),
            jax.ShapeDtypeStruct((1, padded), I32),
        ),
        in_specs=[smem(), vmem(), vmem(), hbm()],
        out_specs=(hbm(), vmem(), vmem()),
        scratch_shapes=[
            pltpu.VMEM((docs * GRID, GRID, DESC, 3 * LANES), BF),
            pltpu.VMEM((docs * GRID, 2, DESC, width), BF),
            pltpu.VMEM((docs, padded), I32),
            pltpu.VMEM((docs, LANES), I32),
            pltpu.SMEM((docs, LANES), I32),
            pltpu.SemaphoreType.DMA((docs * GRID,)),
            pltpu.SemaphoreType.DMA((docs + 1,)),
        ],
        compiler_params=params(24),
        cost_estimate=cost(10**9, 0, 2 * 10**6),
    )(where, all_codes, planes, pinned(code_cache))
    got = lax.all_to_all(
        send.reshape(devices, DESC, 3 * LANES), ("doc", "seq"), split_axis=0, concat_axis=0, tiled=True
    )

    middle, queries = pl.pallas_call(
        window_kernel,
        name="window",
        out_shape=(
            pltpu.HBM((tok, width), BF),
            jax.ShapeDtypeStruct((GRID, message, LANES), BF),
        ),
        in_specs=[vmem()] * 4 + [hbm()] * 4,
        out_specs=(hbm(), vmem()),
        scratch_shapes=[
            pltpu.VMEM((tok, width), BF),
            pltpu.VMEM((width, 2 * width), BF),
            pltpu.VMEM((width, width), BF),
            pltpu.VMEM((width, width), BF),
            pltpu.VMEM((width, width), BF),
            pltpu.VMEM((tok + 2 * HALF_WIN, width), BF),
            pltpu.VMEM((tok + 2 * HALF_WIN, width), BF),
            pltpu.VMEM((tok + 2 * HALF_WIN, 2 * width), BF),
            pltpu.VMEM((tok, width), BF),
            pltpu.VMEM((tok, width), BF),
            pltpu.VMEM((tok // HALF_WIN, HALF_WIN, 3 * HALF_WIN), F32),
            pltpu.SemaphoreType.DMA((4 + tok // HALF_WIN,)),
        ],
        compiler_params=params(26),
        cost_estimate=cost(12 * 10**9, 5 * 10**6, 10**7),
    )(low, doc_hidden, high, token_ids, *map(pinned, (w_keyval, w_query, w_out, x_query)))

    lines = [[GRID * z + x for x in range(GRID)] for z in range(GRID)]

    def across(block):
        return lax.all_to_all(
            block, "seq", split_axis=0, concat_axis=0, axis_index_groups=lines, tiled=True
        )

    queries = across(queries)

    blocks = pl.pallas_call(
        compact_kernel,
        name="compact",
        out_shape=(jax.ShapeDtypeStruct((held, LANES), BF), jax.ShapeDtypeStruct((held, 2 * LANES), BF)),
        in_specs=[vmem()] * 2,
        out_specs=(vmem(),) * 2,
        compiler_params=params(24),
        cost_estimate=cost(10**9, 0, 2 * 10**6),
    )(slots, got.reshape(devices * DESC, 3 * LANES))

    def turn(block, shift):
        pairs = [(i, (i + GRID * shift) % seq_count) for i in range(seq_count)]
        return lax.ppermute(block, "seq", pairs)

    block, rest_block = blocks
    up, down = turn(block, 1), turn(block, 3)
    rest_up, rest_down = turn(rest_block, 1), turn(rest_block, 3)
    far = turn(down, 3)
    up, down, far, rest_up = lax.optimization_barrier((up, down, far, rest_up))
    rest_far = turn(rest_up, 1)
    first, rest = [block, up, far, down], [rest_block, rest_up, rest_far, rest_down]

    def cross(heads, parts, extra, outs):
        return pl.pallas_call(
            functools.partial(cross_kernel, heads, count),
            name="cross",
            out_shape=outs,
            in_specs=[smem()] + [vmem()] * (2 + GRID + len(extra)),
            out_specs=jax.tree.map(lambda _: vmem(), outs),
            scratch_shapes=[
                pltpu.VMEM((len(heads), GRID * held, LANES), BF),
                pltpu.VMEM((len(heads), GRID * held, LANES), BF),
                pltpu.VMEM((2, tok, GRID * held), BF),
                pltpu.VMEM((8, GRID * held), F32),
            ],
            compiler_params=params(18),
            cost_estimate=cost(len(heads) * 10**10, 5 * 10**6, 4 * 10**6),
        )(where, pos, queries, *parts, *extra)

    out, mass = cross(
        (0,),
        first,
        (),
        (jax.ShapeDtypeStruct((GRID, tok, LANES), BF), jax.ShapeDtypeStruct((8, GRID * held), F32)),
    )
    out, score = cross(
        (1, 2),
        rest,
        (mass, out),
        (jax.ShapeDtypeStruct((GRID, message, LANES), BF), jax.ShapeDtypeStruct((1, padded), F32)),
    )

    across_x = [[(i, GRID * (i // GRID) + (i + shift) % GRID) for i in range(seq_count)] for shift in range(1, GRID)]
    one, two, three = [lax.ppermute(score, "seq", pairs) for pairs in across_x]
    score = (score + two) + (one + three)
    one, two, three = [turn(score, shift) for shift in (1, 2, 3)]
    sums = (score + two) + (one + three)
    tokens = sums[:, count : count + 1] * (1.0 / GRID)
    cand_score = count * sums[:, :count] / (HEADS * tokens)
    out = across(out)

    refined = pl.pallas_call(
        final_kernel,
        name="final",
        out_shape=jax.ShapeDtypeStruct((tok, width), BF),
        in_specs=[vmem()] * 3,
        out_specs=vmem(),
        compiler_params=params(16),
        cost_estimate=cost(10**9, 0, 4 * 10**6),
    )(middle, out, x_out)
    return (refined[None], cand_score)


def solution(mesh):
    return jax.shard_map(
        local,
        mesh=mesh,
        in_specs=(
            P("doc", "seq", None),
            P("doc", "seq"),
            P(),
            P(),
            P(),
            P(),
            P(),
            P("doc", None),
            P(),
            P(("doc", "seq"), None, None, None),
        ),
        out_specs=(P("doc", "seq", None), P("doc", None)),
        check_vma=False,
    )
```
